512 devices in a mesh: tok: 64 (over z, y_lo, core), head: 8 (over y_hi, x).
Axes of the slice: x: 4, y: 8 (y_hi: 2, y_lo: 4; y = y_hi * 4 + y_lo), z: 8, core: 2. Of those that a mesh axis runs over, the one named last changes fastest.
Arguments:
- queries: bfloat16 [16384, 2560], P('tok', 'head'), may hold values from -256 to 256
- keys: bfloat16 [16384, 2560], P('tok', 'head'), may hold values from -6 to 6
- values: bfloat16 [16384, 2560], P('tok', 'head'), may hold values from -6 to 6
- rates: float32 [16384, 8], P('tok', 'head'), may hold values from 0.00015625 to 0.003125
- back: int32 [16384], P('tok'), may hold values from 64 to 511
- group_end: int32 [1], replicated, may hold values from 4096 to 12287
- gate_init: float32 [8, 320, 320], P('head', None, 'tok'), may hold values from -0.3125 to 0.3125
- up_init: float32 [8, 320, 320], P('head', None, 'tok'), may hold values from -0.3125 to 0.3125
- down_init: float32 [8, 320, 320], P('head', None, 'tok'), may hold values from -0.3125 to 0.3125
- gain: float32 [2560], P('head'), may hold values from 0.5 to 1.5
Outputs:
- output: bfloat16 [16384, 2560], P('tok', 'head')
- gate_final: float32 [8, 320, 320], P('head', None, 'tok')
- up_final: float32 [8, 320, 320], P('head', None, 'tok')
- down_final: float32 [8, 320, 320], P('head', None, 'tok')
The draws below stay inside these ranges and needn't reach their ends.
All inputs are finite; a program needn't handle non-finite values.
Results may differ from the reference program's by a relative error of at most 0.0088.
Values may be sent and summed in bfloat16 or wider, within the bound.
A program may use at most 64 MiB of HBM per device.

```python
import math
import jax
import jax.numpy as jnp
from jax import lax

HEADS = 8
HD = 320
FH = 320
WINDOW = 512
TOKENS = 16384


def joint_fields(key):
    base_keys = jnp.clip(jax.random.normal(jax.random.fold_in(key, 11), (TOKENS, HEADS * HD), jnp.float32), -6.0, 6.0)
    base_queries = jnp.clip(jax.random.normal(jax.random.fold_in(key, 12), (TOKENS, HEADS * HD), jnp.float32), -6.0, 6.0)
    return (base_queries, base_keys)


def draw_queries(key, part):
    queries, keys = joint_fields(key)
    return queries.astype(jnp.bfloat16)


def draw_keys(key, part):
    queries, keys = joint_fields(key)
    return keys.astype(jnp.bfloat16)


def with_ends(drawn, stream_key, low, high):
    longest = drawn.shape.index(max(drawn.shape))
    spots = []
    for shift in (0, 1):
        where = [jax.random.randint(jax.random.fold_in(stream_key, axis), (), 0, length) for axis, length in enumerate(drawn.shape)]
        where[longest] = (where[longest] + shift) % drawn.shape[longest]
        spots.append(tuple(where))
    return drawn.at[spots[0]].set(low).at[spots[1]].set(high)


def level_of(own_key, shape, shards, low, top_value):
    level = 1.0
    for dim, shards_of in shards:
        heights = jax.random.uniform(jax.random.fold_in(jax.random.fold_in(own_key, 6), dim), (shards_of,), jnp.float32, low / len(shards), top_value / len(shards))
        level = level * jnp.repeat(jnp.exp(heights), shape[dim] // shards_of).reshape((-1,) + (1,) * (len(shape) - 1 - dim))
    return level


def gaussian(key, dims, spread, most, shards=(), kind=jnp.bfloat16):
    loudness = level_of(key, dims, shards, -0.22, 0.18) if shards else 1.0
    values = jax.random.normal(key, dims, jnp.float32) * spread * loudness
    return jnp.minimum(jnp.maximum(values, -most), most).astype(kind)


def setup_inputs(seed: int = 0) -> dict:
    splits = jax.random.split(jax.random.key(seed), 11)
    queries = draw_queries(jax.random.fold_in(splits[10], 71), 0)
    keys = draw_keys(jax.random.fold_in(splits[10], 71), 0)
    values = gaussian(splits[2], (TOKENS, HEADS * HD), 1.0, 6.0, ((0, 64), (1, 8)))
    rates = jnp.clip(jnp.exp(math.log(0.003125) - 2.9957323 * jax.random.uniform(splits[3], (TOKENS, HEADS), jnp.float32) ** level_of(splits[3], (TOKENS, HEADS), ((0, 64), (1, 8)), -0.2, 0.2)), 0.00015625, 0.003125)
    back = with_ends(jax.random.randint(splits[4], (TOKENS,), WINDOW // 8, WINDOW), jax.random.fold_in(splits[4], 1), WINDOW // 8, WINDOW - 1).astype(jnp.int32)
    group_end = jax.random.randint(splits[5], (1,), TOKENS // 4, 3 * TOKENS // 4).astype(jnp.int32)
    gate_init = gaussian(splits[6], (HEADS, HD, FH), HD ** -0.5, 0.3125, ((0, 8), (2, 64)), jnp.float32)
    up_init = gaussian(splits[7], (HEADS, HD, FH), HD ** -0.5, 0.3125, ((0, 8), (2, 64)), jnp.float32)
    down_init = gaussian(splits[8], (HEADS, FH, HD), FH ** -0.5, 0.3125, ((0, 8), (2, 64)), jnp.float32)
    gain = jnp.clip(1.0 + 0.1 * jax.random.normal(splits[9], (HEADS * HD,), jnp.float32), 0.5, 1.5)
    return dict(queries=queries, keys=keys, values=values, rates=rates, back=back, group_end=group_end, gate_init=gate_init, up_init=up_init, down_init=down_init, gain=gain)


def swiglu_apply(w_gate, w_up, w_down, inputs):
    pre_gate = jnp.dot(inputs, w_gate, preferred_element_type=jnp.float32)
    pre_up = jnp.dot(inputs, w_up, preferred_element_type=jnp.float32)
    hidden = (pre_gate * jax.nn.sigmoid(pre_gate) * pre_up).astype(jnp.bfloat16)
    return jnp.dot(hidden, w_down, preferred_element_type=jnp.float32)

def swiglu_grads(w_gate, w_up, w_down, key_rows, value_rows, step_rates):
    pre_gate = jnp.dot(key_rows, w_gate, preferred_element_type=jnp.float32)
    pre_up = jnp.dot(key_rows, w_up, preferred_element_type=jnp.float32)
    sigma = jax.nn.sigmoid(pre_gate)
    active = pre_gate * sigma
    hidden = (active * pre_up).astype(jnp.bfloat16)
    errors = (-step_rates[:, None] * value_rows.astype(jnp.float32)).astype(jnp.bfloat16)
    grad_down = jnp.dot(hidden.T, errors, preferred_element_type=jnp.float32)
    d_hidden = jnp.dot(errors, w_down.T, preferred_element_type=jnp.float32)
    d_gate = (d_hidden * pre_up * sigma * (1.0 + pre_gate * (1.0 - sigma))).astype(jnp.bfloat16)
    d_up = (d_hidden * active).astype(jnp.bfloat16)
    grad_gate = jnp.dot(key_rows.T, d_gate, preferred_element_type=jnp.float32)
    grad_up = jnp.dot(key_rows.T, d_up, preferred_element_type=jnp.float32)
    return (grad_gate, grad_up, grad_down)

def rescale(weight, grad):
    fresh = weight - grad
    old_norm = jnp.sqrt(lax.optimization_barrier(jnp.sum(weight * weight, axis=0, keepdims=True)))
    new_norm = jnp.sqrt(lax.optimization_barrier(jnp.sum(fresh * fresh, axis=0, keepdims=True)) + 1e-06)
    return fresh * (old_norm / new_norm)

def reference(queries, keys, values, rates, back, group_end, gate_init, up_init, down_init, gain):
    positions = jnp.arange(TOKENS, dtype=jnp.int32)
    first = positions < group_end[0]
    query3 = queries.reshape(TOKENS, HEADS, HD)
    key3 = keys.reshape(TOKENS, HEADS, HD)
    value3 = values.reshape(TOKENS, HEADS, HD)

    def one_head(items):
        q_rows, k_rows, v_rows, lr_rows, w_gate, w_up, w_down = items
        state = (w_gate, w_up, w_down)
        outs = []
        for group in range(2):
            live = first if group == 0 else jnp.logical_not(first)
            packed = tuple((w.astype(jnp.bfloat16) for w in state))
            outs.append(swiglu_apply(packed[0], packed[1], packed[2], q_rows))
            grads = swiglu_grads(packed[0], packed[1], packed[2], k_rows, v_rows, jnp.where(live, lr_rows, 0.0))
            state = tuple((rescale(w, g) for w, g in zip(state, grads)))
        mixed = jnp.where(first[:, None], outs[0], outs[1])
        return (mixed, state[0], state[1], state[2])
    mixed, gate_final, up_final, down_final = lax.map(one_head, (query3.transpose(1, 0, 2), key3.transpose(1, 0, 2), value3.transpose(1, 0, 2), rates.T, gate_init, up_init, down_init))
    mixed = mixed.transpose(1, 0, 2)
    mean_square = lax.optimization_barrier(jnp.mean(mixed * mixed, axis=(1, 2), keepdims=True))
    normed = mixed / jnp.sqrt(mean_square + 1e-06) * gain.reshape(1, HEADS, HD)
    block = math.gcd(TOKENS, 512)
    key_pad = jnp.concatenate([jnp.zeros((WINDOW, HEADS, HD), jnp.bfloat16), key3], axis=0)
    value_pad = jnp.concatenate([jnp.zeros((WINDOW, HEADS, HD), jnp.bfloat16), value3], axis=0)

    def attend(index):
        begin = (index * block).astype(jnp.int32)
        q_block = lax.dynamic_slice_in_dim(query3, begin, block, 0).astype(jnp.float32)
        k_block = lax.dynamic_slice_in_dim(key_pad, begin, block + WINDOW, 0).astype(jnp.float32)
        v_block = lax.dynamic_slice_in_dim(value_pad, begin, block + WINDOW, 0).astype(jnp.float32)
        reach = lax.dynamic_slice_in_dim(back, begin, block, 0)
        q_pos = begin + jnp.arange(block, dtype=jnp.int32)
        k_pos = begin - WINDOW + jnp.arange(block + WINDOW, dtype=jnp.int32)
        allowed = (k_pos[None, :] >= 0) & (k_pos[None, :] <= q_pos[:, None]) & (k_pos[None, :] >= q_pos[:, None] - reach[:, None])
        scores = jnp.einsum('qhd,khd->hqk', q_block, k_block) * (1.0 / math.sqrt(HD))
        scores = jnp.where(allowed[None], scores, -jnp.inf)
        top = lax.optimization_barrier(jnp.max(scores, axis=2, keepdims=True))
        weights = jnp.where(allowed[None], jnp.exp(scores - top), 0.0)
        total = lax.optimization_barrier(jnp.sum(weights, axis=2, keepdims=True))
        probs = (weights / total).astype(jnp.bfloat16).astype(jnp.float32)
        return jnp.einsum('hqk,khd->qhd', probs, v_block)
    attn = lax.map(attend, jnp.arange(TOKENS // block, dtype=jnp.int32))
    attn = attn.reshape(TOKENS, HEADS, HD)
    output = (normed + attn).astype(jnp.bfloat16).reshape(TOKENS, HEADS * HD)
    return (output, gate_final, up_final, down_final)
```

```python
import functools
import math

import jax
import jax.numpy as jnp
import numpy as np
from jax import lax
from jax.experimental import pallas as pl
from jax.experimental.pallas import tpu as pltpu
from jax.sharding import PartitionSpec as P

HEADS = 8
HD = 320
FH = 320
WINDOW = 512
NZ, NY, NC = 8, 4, 2
CHIPS = NZ * NY
OWN = 5
SLOT = 16
ZROWS = NY * NC * OWN
FAR_FIRST = (4, 3, 5, 2, 6, 1, 7, 0)
NEAR_FIRST = (0, 1, 7, 2, 6, 3, 5, 4)
F32, BF16 = jnp.float32, jnp.bfloat16


def nn(a, b):
    return lax.dot_general(a, b, (((1,), (0,)), ((), ())), preferred_element_type=F32)


def nt(a, b):
    return lax.dot_general(a, b, (((1,), (1,)), ((), ())), preferred_element_type=F32)


def tn(a, b):
    return lax.dot_general(a, b, (((0,), (0,)), ((), ())), preferred_element_type=F32)


def order_matrix():
    perm = np.zeros((128, 128), np.float32)
    for m in range(3):
        for y in range(NY):
            for c in range(NC):
                for j in range(OWN):
                    perm[m * ZROWS + (y * NC + c) * OWN + j, c * 64 + y * SLOT + m * OWN + j] = 1.0
    return perm


def kernel(
    ge, q, k, v, rates, back, s0, gain, perm, perm_t,
    out, s2,
    own, ag, gs, cr, red, rr, kv_far, kv_near, sq, sqr, nat, gt, ut, dt, es, y_buf, at_buf, state,
    ag_send, ag_recv, fw_send, fw_recv, cs_send, cs_recv, rs_send, rs_recv, kv_send, kv_recv, sq_send, sq_recv,
):
    rows = q.shape[0]
    t = lax.axis_index("tok")
    h = lax.axis_index("head")
    c = lax.rem(t, 2)
    chip = lax.div(t, 2)
    zme = lax.div(chip, NY)
    yme = lax.rem(chip, NY)
    mate = t + 1 - 2 * c

    def at_chip(p):
        return {"tok": 2 * p + c}

    barrier = pltpu.get_barrier_semaphore()

    def greet(i, _):
        pl.semaphore_signal(barrier, inc=1, device_id=at_chip(lax.rem(chip + i, CHIPS)))
        return 0

    lax.fori_loop(1, CHIPS, greet, 0)
    pl.semaphore_signal(barrier, inc=1, device_id={"tok": mate})

    def greet_head(i, _):
        pl.semaphore_signal(barrier, inc=1, device_id={"head": lax.rem(h + i, HEADS)})
        return 0

    lax.fori_loop(1, HEADS, greet_head, 0)

    start = t * rows
    pos = start + lax.broadcasted_iota(jnp.int32, (rows, 1), 0)
    first = pos < ge[0]
    rate = rates[...]
    vf = v[...].astype(F32)
    es[0] = (-jnp.where(first, rate, 0.0) * vf).astype(BF16)
    es[1] = (-jnp.where(first, 0.0, rate) * vf).astype(BF16)
    state[...] = s0[...]
    own[0] = s0[...].astype(BF16)

    pl.semaphore_wait(barrier, (CHIPS - 1) + 1 + (HEADS - 1))

    def peers(dzs, body):
        for dz in dzs:
            zz = lax.rem(zme + dz, NZ)
            for dy in range(NY):
                yy = lax.rem(yme + dy, NY)
                body(zz, yy, dz == 0 and dy == 0)

    def gather_start(g):
        mine = ag.at[g, c, chip]

        def send(zz, yy, is_me):
            if is_me:
                pltpu.make_async_copy(own.at[g], mine, ag_recv.at[g, zme]).start()
            else:
                pltpu.make_async_remote_copy(
                    own.at[g], mine, ag_send.at[g], ag_recv.at[g, zme], at_chip(zz * NY + yy)
                ).start()

        peers(FAR_FIRST, send)

    def gather_forward(g):
        for dz in NEAR_FIRST:
            zz = lax.rem(zme + dz, NZ)
            four = ag.at[g, c, pl.ds(zz * NY, NY)]
            pltpu.make_async_copy(four, four, ag_recv.at[g, zz]).wait()
            pltpu.make_async_remote_copy(four, four, fw_send.at[g], fw_recv.at[g, zz], {"tok": mate}).start()

    def gather_finish(g):
        for z in range(NZ):
            four = ag.at[g, 1 - c, pl.ds(z * NY, NY)]
            pltpu.make_async_copy(four, four, fw_recv.at[g, z]).wait()
            block = ag[g, :, z * NY : (z + 1) * NY].reshape(NC * NY * SLOT, HD)
            ordered = nn(perm[...], block)
            for m in range(3):
                nat[m, z * ZROWS : (z + 1) * ZROWS] = ordered[m * ZROWS : (m + 1) * ZROWS]
        gt[...] = nat[0].astype(BF16)
        ut[...] = nat[1].astype(BF16)
        dt[...] = nat[2].astype(BF16)

    def gather_drain(g):
        thirty_one = ag.at[g, 0, pl.ds(0, CHIPS - 1)]
        pltpu.make_async_copy(thirty_one, thirty_one, ag_send.at[g]).wait()
        every = ag.at[g, 0]
        pltpu.make_async_copy(every, every, fw_send.at[g]).wait()

    def grads(g):
        kk, e = k[...], es[g]
        a = nt(kk, gt[...])
        b = nt(kk, ut[...])
        s = jax.nn.sigmoid(a)
        active = a * s
        r = (active * b).astype(BF16)
        du = nn(e, dt[...])
        da = (du * b * s * (1.0 + a * (1.0 - s))).astype(BF16)
        db = (du * active).astype(BF16)
        nat[0] = tn(da, kk)
        nat[1] = tn(db, kk)
        nat[2] = tn(e, r)

    def reduce_start(g):
        for z in range(NZ):
            part = [nat[m, z * ZROWS : (z + 1) * ZROWS] for m in range(3)]
            part.append(jnp.zeros((128 - 3 * ZROWS, HD), F32))
            block = nn(perm_t[...], jnp.concatenate(part, axis=0).astype(BF16)).astype(BF16)
            gs[g, :, z * NY : (z + 1) * NY] = block.reshape(NC, NY, SLOT, HD)
            pltpu.make_async_remote_copy(
                gs.at[g, 1 - c, pl.ds(z * NY, NY)], cr.at[g, pl.ds(z * NY, NY)],
                cs_send.at[g], cs_recv.at[g, z], {"tok": mate},
            ).start()
        for dz in FAR_FIRST:
            zz = lax.rem(zme + dz, NZ)
            here = pl.ds(zz * NY, NY)
            four = cr.at[g, here]
            pltpu.make_async_copy(four, four, cs_recv.at[g, zz]).wait()
            red[g, here] = (gs[g, c, here].astype(F32) + cr[g, here].astype(F32)).astype(BF16)

            def send(z_to, yy, is_me):
                p = z_to * NY + yy
                if is_me:
                    pltpu.make_async_copy(red.at[g, p], rr.at[g, chip], rs_recv.at[g]).start()
                else:
                    pltpu.make_async_remote_copy(
                        red.at[g, p], rr.at[g, chip], rs_send.at[g], rs_recv.at[g], at_chip(p)
                    ).start()

            peers((dz,), send)

    def reduce_finish(g):
        every = rr.at[g]
        pltpu.make_async_copy(every, every, rs_recv.at[g]).wait()
        total = jnp.sum(rr[g].astype(F32), axis=0)
        old = state[...]
        fresh = old - total
        old_norm = jnp.sqrt(jnp.sum(old * old, axis=1, keepdims=True))
        new_norm = jnp.sqrt(jnp.sum(fresh * fresh, axis=1, keepdims=True) + 1e-06)
        return fresh * (old_norm / new_norm)

    def reduce_drain(g):
        every = cr.at[g]
        pltpu.make_async_copy(every, every, cs_send.at[g]).wait()
        thirty_one = rr.at[g, pl.ds(0, CHIPS - 1)]
        pltpu.make_async_copy(thirty_one, thirty_one, rs_send.at[g]).wait()

    def apply_queries():
        a = nt(q[...], gt[...])
        b = nt(q[...], ut[...])
        hidden = (a * jax.nn.sigmoid(a) * b).astype(BF16)
        return nt(hidden, dt[...])

    gather_start(0)

    nxt = at_chip(lax.rem(chip + 1, CHIPS))
    far_copies = [
        pltpu.make_async_remote_copy(src, kv_far.at[i], kv_send.at[i], kv_recv.at[i], nxt) for i, src in enumerate((k, v))
    ]
    for copy in far_copies:
        copy.start()

    def near_copies(srcs):
        return [
            pltpu.make_async_remote_copy(src, kv_near.at[i], kv_send.at[2 + i], kv_recv.at[2 + i], {"tok": mate})
            for i, src in enumerate(srcs)
        ]

    @pl.when(c == 0)
    def _():
        for copy in near_copies((k, v)):
            copy.start()

    gather_forward(0)
    gather_finish(0)
    grads(0)
    reduce_start(0)
    y_buf[...] = apply_queries()
    for copy in far_copies:
        copy.wait()

    @pl.when(c == 1)
    def _():
        for copy in near_copies((kv_far.at[0], kv_far.at[1])):
            copy.start()

    middle = reduce_finish(0)
    state[...] = middle
    own[1] = middle.astype(BF16)
    gather_start(1)

    for copy in near_copies((kv_far.at[0], kv_far.at[1])):
        copy.wait()
    qq = q[...]
    scale = 1.0 / math.sqrt(HD)
    i = lax.broadcasted_iota(jnp.int32, (rows, rows), 0)
    j = lax.broadcasted_iota(jnp.int32, (rows, rows), 1)
    reach = back[...]
    scores = []
    for ahead, keys in ((2 * rows, kv_far.at[0]), (rows, kv_near.at[0]), (0, k)):
        away = i - j + ahead
        seen = (away >= 0) & (away <= reach) & (start + j - ahead >= 0)
        scores.append((jnp.where(seen, nt(qq, keys[...]) * scale, -jnp.inf)))
    top = functools.reduce(jnp.maximum, [jnp.max(s, axis=1, keepdims=True) for s in scores])
    weights = [jnp.exp(s - top) for s in scores]
    total = functools.reduce(jnp.add, [jnp.sum(w, axis=1, keepdims=True) for w in weights])
    pieces = [
        nn((w / total).astype(BF16), vals[...]) for w, vals in zip(weights, (kv_far.at[1], kv_near.at[1], v))
    ]
    at_buf[...] = pieces[0] + pieces[1] + pieces[2]

    gather_forward(1)
    gather_finish(1)
    grads(1)
    reduce_start(1)
    mixed = jnp.where(first, y_buf[...], apply_queries())
    y_buf[...] = mixed
    sums = lax.dot_general(
        jnp.ones((8, HD), F32), mixed * mixed, (((1,), (1,)), ((), ())),
        precision=lax.Precision.HIGHEST, preferred_element_type=F32,
    )
    sq[...] = sums
    sqr[h] = sums

    def send_squares(n, _):
        pltpu.make_async_remote_copy(sq, sqr.at[h], sq_send, sq_recv, {"head": lax.rem(h + n, HEADS)}).start()
        return 0

    lax.fori_loop(1, HEADS, send_squares, 0)
    seven = sqr.at[pl.ds(0, HEADS - 1)]
    pltpu.make_async_copy(seven, seven, sq_recv).wait()
    squares = jnp.sum(sqr[...], axis=0).T[:, 0:1]
    mean_square = squares / (HEADS * HD)
    normed = y_buf[...] / jnp.sqrt(mean_square + 1e-06) * gain[...]
    out[...] = (normed + at_buf[...]).astype(BF16)
    s2[...] = reduce_finish(1)
    pltpu.make_async_copy(seven, seven, sq_send).wait()
    for g in range(2):
        gather_drain(g)
        reduce_drain(g)


def on_device(queries, keys, values, rates, back, group_end, gate_init, up_init, down_init, gain):
    rows = rates.shape[0]
    perm = order_matrix()
    shares = (gate_init[0].T, up_init[0].T, down_init[0].T)
    s0 = jnp.concatenate((*shares, jnp.zeros((SLOT - 3 * OWN, HD), F32)), axis=0)
    vmem = pl.BlockSpec(memory_space=pltpu.VMEM)
    slots = (CHIPS, SLOT, HD)
    dma = pltpu.SemaphoreType.DMA
    out, s2 = pl.pallas_call(
        kernel,
        out_shape=(
            jax.ShapeDtypeStruct((rows, HD), BF16),
            jax.ShapeDtypeStruct((SLOT, HD), F32),
        ),
        in_specs=[pl.BlockSpec(memory_space=pltpu.SMEM)] + [vmem] * 9,
        out_specs=(vmem, vmem),
        scratch_shapes=[
            pltpu.VMEM((2, SLOT, HD), BF16),
            pltpu.VMEM((2, NC, *slots), BF16),
            pltpu.VMEM((2, NC, *slots), BF16),
            pltpu.VMEM((2, *slots), BF16),
            pltpu.VMEM((2, *slots), BF16),
            pltpu.VMEM((2, *slots), BF16),
            pltpu.VMEM((2, rows, HD), BF16),
            pltpu.VMEM((2, rows, HD), BF16),
            pltpu.VMEM((8, rows), F32),
            pltpu.VMEM((HEADS, 8, rows), F32),
            pltpu.VMEM((3, HD, HD), F32),
            pltpu.VMEM((FH, HD), BF16),
            pltpu.VMEM((FH, HD), BF16),
            pltpu.VMEM((HD, FH), BF16),
            pltpu.VMEM((2, rows, HD), BF16),
            pltpu.VMEM((rows, HD), F32),
            pltpu.VMEM((rows, HD), F32),
            pltpu.VMEM((SLOT, HD), F32),
            dma((2,)), dma((2, NZ)),
            dma((2,)), dma((2, NZ)),
            dma((2,)), dma((2, NZ)),
            dma((2,)), dma((2,)),
            dma((4,)), dma((4,)),
            dma, dma,
        ],
        compiler_params=pltpu.CompilerParams(
            collective_id=0, has_side_effects=True, vmem_limit_bytes=48 * 1024 * 1024
        ),
        name="layer",
    )(
        group_end, queries, keys, values, rates, back.reshape(rows, 1), s0, gain.reshape(1, HD),
        jnp.asarray(perm, BF16), jnp.asarray(perm.T, BF16),
    )
    finals = [s2[m * OWN : (m + 1) * OWN].T[None] for m in range(3)]
    return (out, *finals)


def solution(mesh):
    placed = (
        P("tok", "head"),
        P("tok", "head"),
        P("tok", "head"),
        P("tok", "head"),
        P("tok"),
        P(),
        P("head", None, "tok"),
        P("head", None, "tok"),
        P("head", None, "tok"),
        P("head"),
    )
    return jax.shard_map(
        on_device,
        mesh=mesh,
        in_specs=placed,
        out_specs=(
            P("tok", "head"),
            P("head", None, "tok"),
            P("head", None, "tok"),
            P("head", None, "tok"),
        ),
        check_vma=False,
    )
```

```python
import functools
import math

import jax
import jax.numpy as jnp
import numpy as np
from jax import lax
from jax.experimental import pallas as pl
from jax.experimental.pallas import tpu as pltpu
from jax.sharding import PartitionSpec as P

HEADS = 8
HD = 320
FH = 320
WINDOW = 512
NZ, NY, NC = 8, 4, 2
CHIPS = NZ * NY
OWN = 5
SLOT = 16
ZROWS = NY * NC * OWN
LAST_FIRST = 12288 * NZ // 16384
FIRST_SECOND = 4096 * NZ // 16384
FAR_FIRST = (4, 3, 5, 2, 6, 1, 7, 0)
NEAR_FIRST = (0, 1, 7, 2, 6, 3, 5, 4)
F32, BF16 = jnp.float32, jnp.bfloat16


def nn(a, b):
    return lax.dot_general(a, b, (((1,), (0,)), ((), ())), preferred_element_type=F32)


def nt(a, b):
    return lax.dot_general(a, b, (((1,), (1,)), ((), ())), preferred_element_type=F32)


def tn(a, b):
    return lax.dot_general(a, b, (((0,), (0,)), ((), ())), preferred_element_type=F32)


def order_matrix():
    perm = np.zeros((128, 128), np.float32)
    for m in range(3):
        for y in range(NY):
            for c in range(NC):
                for j in range(OWN):
                    perm[m * ZROWS + (y * NC + c) * OWN + j, c * 64 + y * SLOT + m * OWN + j] = 1.0
    return perm


def kernel(
    ge, q_hbm, k_hbm, v_hbm, rates_hbm, back_hbm, g_hbm, u_hbm, d_hbm, gain_hbm, perm, perm_t,
    out, g_out, u_out, d_out,
    q, k, v, rates, back, rows0, gain,
    own, ag, gs, cr, red, rr, kv_far, kv_near, sq, sqr, nat, gt, ut, dt, es, y_buf, probs, state,
    in_sem, ag_send, ag_recv, fw_send, fw_recv, cs_send, cs_recv, rs_send, rs_recv, kv_send, kv_recv, sq_send, sq_recv,
):
    toks = q.shape[1]
    t = lax.axis_index("tok")
    h = lax.axis_index("head")
    c = lax.rem(t, 2)
    chip = lax.div(t, 2)
    zme = lax.div(chip, NY)
    yme = lax.rem(chip, NY)
    mate = t + 1 - 2 * c

    loads = [
        pltpu.make_async_copy(src, dst, in_sem.at[n])
        for n, (src, dst) in enumerate(
            (
                (g_hbm, rows0.at[pl.ds(0, OWN)]),
                (u_hbm, rows0.at[pl.ds(OWN, OWN)]),
                (d_hbm, rows0.at[pl.ds(2 * OWN, OWN)]),
                (k_hbm, k),
                (v_hbm, v),
                (q_hbm, q),
                (rates_hbm, rates),
                (back_hbm, back),
                (gain_hbm, gain),
            )
        )
    ]
    for load in loads:
        load.start()

    def at_chip(p):
        return {"tok": 2 * p + c}

    barrier = pltpu.get_barrier_semaphore()

    def greet(i, _):
        pl.semaphore_signal(barrier, inc=1, device_id=at_chip(lax.rem(chip + i, CHIPS)))
        return 0

    lax.fori_loop(1, CHIPS, greet, 0)
    pl.semaphore_signal(barrier, inc=1, device_id={"tok": mate})

    def greet_head(i, _):
        pl.semaphore_signal(barrier, inc=1, device_id={"head": lax.rem(h + i, HEADS)})
        return 0

    lax.fori_loop(1, HEADS, greet_head, 0)

    rows0[pl.ds(3 * OWN, 1)] = jnp.zeros((1, 1, HD), F32)
    for load in loads:
        load.wait()
    state[...] = rows0[...].reshape(SLOT, HD)
    own[0] = state[...].astype(BF16)
    start = t * toks
    first = start + lax.broadcasted_iota(jnp.int32, (1, toks), 1) < ge[0]
    rate = rates[...]
    vf = v[...].astype(F32)
    es[0] = (-jnp.where(first, rate, 0.0) * vf).astype(BF16)
    es[1] = (-jnp.where(first, 0.0, rate) * vf).astype(BF16)
    y_buf[...] = jnp.zeros_like(y_buf)

    pl.semaphore_wait(barrier, (CHIPS - 1) + 1 + (HEADS - 1))

    def active(g, z):
        return z < LAST_FIRST if g == 0 else z >= FIRST_SECOND

    live = [active(g, zme) for g in range(2)]
    z_from = (0, FIRST_SECOND)

    def peers(dzs, body):
        for dz in dzs:
            zz = lax.rem(zme + dz, NZ)
            for dy in range(NY):
                yy = lax.rem(yme + dy, NY)
                body(zz, yy, dz == 0 and dy == 0)

    def gather_start(g):
        mine = ag.at[g, c, chip]

        def send(zz, yy, is_me):
            @pl.when(active(g, zz))
            def _():
                if is_me:
                    pltpu.make_async_copy(own.at[g], mine, ag_recv.at[g, zme]).start()
                else:
                    pltpu.make_async_remote_copy(
                        own.at[g], mine, ag_send.at[g], ag_recv.at[g, zme], at_chip(zz * NY + yy)
                    ).start()

        peers(FAR_FIRST, send)

    def gather_forward(g):
        for dz in NEAR_FIRST:
            zz = lax.rem(zme + dz, NZ)
            four = ag.at[g, c, pl.ds(zz * NY, NY)]
            pltpu.make_async_copy(four, four, ag_recv.at[g, zz]).wait()
            pltpu.make_async_remote_copy(four, four, fw_send.at[g], fw_recv.at[g, zz], {"tok": mate}).start()

    def gather_finish(g):
        for z in range(NZ):
            four = ag.at[g, 1 - c, pl.ds(z * NY, NY)]
            pltpu.make_async_copy(four, four, fw_recv.at[g, z]).wait()
            block = ag[g, :, z * NY : (z + 1) * NY].reshape(NC * NY * SLOT, HD)
            ordered = nn(perm[...], block)
            for m in range(3):
                nat[m, z * ZROWS : (z + 1) * ZROWS] = ordered[m * ZROWS : (m + 1) * ZROWS]
        gt[...] = nat[0].astype(BF16)
        ut[...] = nat[1].astype(BF16)
        dt[...] = nat[2].astype(BF16)

    def gather_drain(g):
        sends = NY * (LAST_FIRST if g == 0 else NZ - FIRST_SECOND)

        def drain(n):
            some = ag.at[g, 0, pl.ds(0, n)]
            pltpu.make_async_copy(some, some, ag_send.at[g]).wait()

        @pl.when(live[g])
        def _():
            drain(sends - 1)
            every = ag.at[g, 0]
            pltpu.make_async_copy(every, every, fw_send.at[g]).wait()

        @pl.when(jnp.logical_not(live[g]))
        def _():
            drain(sends)

    def grads(g):
        kk, e = k[...], es[g]
        a = nn(gt[...], kk)
        b = nn(ut[...], kk)
        s = jax.nn.sigmoid(a)
        act = a * s
        r = (act * b).astype(BF16)
        du = tn(dt[...], e)
        da = (du * b * s * (1.0 + a * (1.0 - s))).astype(BF16)
        db = (du * act).astype(BF16)
        nat[0] = nt(da, kk)
        nat[1] = nt(db, kk)
        nat[2] = nt(e, r)

    def reduce_start(g):
        for z in range(NZ):
            part = [nat[m, z * ZROWS : (z + 1) * ZROWS] for m in range(3)]
            part.append(jnp.zeros((128 - 3 * ZROWS, HD), F32))
            block = nn(perm_t[...], jnp.concatenate(part, axis=0).astype(BF16)).astype(BF16)
            gs[g, :, z * NY : (z + 1) * NY] = block.reshape(NC, NY, SLOT, HD)
            pltpu.make_async_remote_copy(
                gs.at[g, 1 - c, pl.ds(z * NY, NY)], cr.at[g, pl.ds(z * NY, NY)],
                cs_send.at[g], cs_recv.at[g, z], {"tok": mate},
            ).start()
        for dz in FAR_FIRST:
            zz = lax.rem(zme + dz, NZ)
            here = pl.ds(zz * NY, NY)
            four = cr.at[g, here]
            pltpu.make_async_copy(four, four, cs_recv.at[g, zz]).wait()
            red[g, here] = (gs[g, c, here].astype(F32) + cr[g, here].astype(F32)).astype(BF16)
            landing = rr.at[g, chip - z_from[g] * NY]

            def send(z_to, yy, is_me):
                p = z_to * NY + yy
                if is_me:
                    pltpu.make_async_copy(red.at[g, p], landing, rs_recv.at[g]).start()
                else:
                    pltpu.make_async_remote_copy(
                        red.at[g, p], landing, rs_send.at[g], rs_recv.at[g], at_chip(p)
                    ).start()

            peers((dz,), send)

    def reduce_finish(g):
        every = rr.at[g]
        pltpu.make_async_copy(every, every, rs_recv.at[g]).wait()
        total = jnp.sum(rr[g].astype(F32), axis=0)
        old = state[...]
        fresh = old - total
        old_norm = jnp.sqrt(jnp.sum(old * old, axis=1, keepdims=True))
        new_norm = jnp.sqrt(jnp.sum(fresh * fresh, axis=1, keepdims=True) + 1e-06)
        return fresh * (old_norm / new_norm)

    def reduce_drain(g):
        @pl.when(live[g])
        def _():
            every = cr.at[g]
            pltpu.make_async_copy(every, every, cs_send.at[g]).wait()
            thirty_one = red.at[g, pl.ds(0, CHIPS - 1)]
            pltpu.make_async_copy(thirty_one, thirty_one, rs_send.at[g]).wait()

    def apply_queries():
        a = nn(gt[...], q[...])
        b = nn(ut[...], q[...])
        hidden = (a * jax.nn.sigmoid(a) * b).astype(BF16)
        return nn(dt[...], hidden)

    def far_copy(n):
        return pltpu.make_async_remote_copy(
            (k, v)[n], kv_far.at[n], kv_send.at[n], kv_recv.at[n], at_chip(lax.rem(chip + 1, CHIPS))
        )

    def near_copy(n, src):
        return pltpu.make_async_remote_copy(src, kv_near.at[n], kv_send.at[2 + n], kv_recv.at[2 + n], {"tok": mate})

    def pass_on(n):
        far_copy(n).wait()

        @pl.when(c == 1)
        def _():
            near_copy(n, kv_far.at[n]).start()

    gather_start(0)

    @pl.when(c == 0)
    def _():
        for n in range(2):
            near_copy(n, (k, v)[n]).start()

    @pl.when(live[0])
    def _():
        gather_forward(0)

    far_copy(0).start()

    @pl.when(live[0])
    def _():
        gather_finish(0)
        grads(0)
        reduce_start(0)
        y_buf[...] = apply_queries()

    pass_on(0)
    middle = reduce_finish(0)
    state[...] = middle
    own[1] = middle.astype(BF16)
    gather_start(1)

    near_copy(0, k).wait()
    scale = 1.0 / math.sqrt(HD)
    j = lax.broadcasted_iota(jnp.int32, (toks, toks), 0)
    i = lax.broadcasted_iota(jnp.int32, (toks, toks), 1)
    reach = back[...]
    scores = []
    for ahead, keys in ((2 * toks, kv_far.at[0]), (toks, kv_near.at[0]), (0, k)):
        away = i - j + ahead
        seen = (away >= 0) & (away <= reach) & (start + j - ahead >= 0)
        scores.append(jnp.where(seen, tn(keys[...], q[...]) * scale, -jnp.inf))
    top = functools.reduce(jnp.maximum, [jnp.max(s, axis=0, keepdims=True) for s in scores])
    weights = [jnp.exp(s - top) for s in scores]
    total = functools.reduce(jnp.add, [jnp.sum(w, axis=0, keepdims=True) for w in weights])
    for n, w in enumerate(weights):
        probs[n] = (w / total).astype(BF16)

    @pl.when(live[1])
    def _():
        gather_forward(1)

    far_copy(1).start()

    @pl.when(live[1])
    def _():
        gather_finish(1)
        grads(1)
        reduce_start(1)
        y_buf[...] = jnp.where(first, y_buf[...], apply_queries())

    mixed = y_buf[...]
    sums = jnp.sum(mixed * mixed, axis=0, keepdims=True)
    sq[...] = sums
    sqr[h] = sums

    def send_squares(n, _):
        pltpu.make_async_remote_copy(sq, sqr.at[h], sq_send, sq_recv, {"head": lax.rem(h + n, HEADS)}).start()
        return 0

    lax.fori_loop(1, HEADS, send_squares, 0)
    pass_on(1)
    near_copy(1, v).wait()
    attn = nn(kv_far[1], probs[0]) + nn(kv_near[1], probs[1]) + nn(v[...], probs[2])
    seven = sqr.at[pl.ds(0, HEADS - 1)]
    pltpu.make_async_copy(seven, seven, sq_recv).wait()
    mean_square = jnp.sum(sqr[...], axis=0) / (HEADS * HD)
    gains = jnp.broadcast_to(gain[...].reshape(1, HD), (8, HD)).T[:, 0:1]
    normed = y_buf[...] / jnp.sqrt(mean_square + 1e-06) * gains
    out[...] = (normed + attn).astype(BF16)
    last = reduce_finish(1)
    for m, ref in enumerate((g_out, u_out, d_out)):
        ref[...] = last[m * OWN : (m + 1) * OWN].reshape(OWN, 1, HD)
    pltpu.make_async_copy(seven, seven, sq_send).wait()
    for g in range(2):
        gather_drain(g)
        reduce_drain(g)


def on_device(queries, keys, values, rates, back, group_end, gate_init, up_init, down_init, gain):
    toks = rates.shape[0]
    perm = order_matrix()
    vmem = pl.BlockSpec(memory_space=pltpu.VMEM)
    anywhere = pl.BlockSpec(memory_space=pl.ANY)
    slots = (CHIPS, SLOT, HD)
    dma = pltpu.SemaphoreType.DMA
    shares = [w.transpose(2, 0, 1) for w in (gate_init, up_init, down_init)]
    share = jax.ShapeDtypeStruct((OWN, 1, HD), F32)
    out, *finals = pl.pallas_call(
        kernel,
        out_shape=(jax.ShapeDtypeStruct((HD, toks), BF16), share, share, share),
        in_specs=[pl.BlockSpec(memory_space=pltpu.SMEM)] + [anywhere] * 9 + [vmem] * 2,
        out_specs=(vmem,) * 4,
        scratch_shapes=[
            pltpu.VMEM((HD, toks), BF16),
            pltpu.VMEM((HD, toks), BF16),
            pltpu.VMEM((HD, toks), BF16),
            pltpu.VMEM((1, toks), F32),
            pltpu.VMEM((1, toks), jnp.int32),
            pltpu.VMEM((SLOT, 1, HD), F32),
            pltpu.VMEM((HD,), F32),
            pltpu.VMEM((2, SLOT, HD), BF16),
            pltpu.VMEM((2, NC, *slots), BF16),
            pltpu.VMEM((2, NC, *slots), BF16),
            pltpu.VMEM((2, *slots), BF16),
            pltpu.VMEM((2, *slots), BF16),
            pltpu.VMEM((2, LAST_FIRST * NY, SLOT, HD), BF16),
            pltpu.VMEM((2, HD, toks), BF16),
            pltpu.VMEM((2, HD, toks), BF16),
            pltpu.VMEM((1, toks), F32),
            pltpu.VMEM((HEADS, 1, toks), F32),
            pltpu.VMEM((3, HD, HD), F32),
            pltpu.VMEM((FH, HD), BF16),
            pltpu.VMEM((FH, HD), BF16),
            pltpu.VMEM((HD, FH), BF16),
            pltpu.VMEM((2, HD, toks), BF16),
            pltpu.VMEM((HD, toks), F32),
            pltpu.VMEM((3, toks, toks), BF16),
            pltpu.VMEM((SLOT, HD), F32),
            dma((9,)),
            dma((2,)), dma((2, NZ)),
            dma((2,)), dma((2, NZ)),
            dma((2,)), dma((2, NZ)),
            dma((2,)), dma((2,)),
            dma((4,)), dma((4,)),
            dma, dma,
        ],
        compiler_params=pltpu.CompilerParams(
            collective_id=0, has_side_effects=True, vmem_limit_bytes=48 * 1024 * 1024
        ),
        name="layer",
    )(
        group_end, queries.T, keys.T, values.T, rates.T, back.reshape(1, toks), *shares, gain,
        jnp.asarray(perm, BF16), jnp.asarray(perm.T, BF16),
    )
    return (out.T, *(w.transpose(1, 2, 0) for w in finals))


def solution(mesh):
    placed = (
        P("tok", "head"),
        P("tok", "head"),
        P("tok", "head"),
        P("tok", "head"),
        P("tok"),
        P(),
        P("head", None, "tok"),
        P("head", None, "tok"),
        P("head", None, "tok"),
        P("head"),
    )
    return jax.shard_map(
        on_device,
        mesh=mesh,
        in_specs=placed,
        out_specs=(
            P("tok", "head"),
            P("head", None, "tok"),
            P("head", None, "tok"),
            P("head", None, "tok"),
        ),
        check_vma=False,
    )
```

```python
import functools
import math

import jax
import jax.numpy as jnp
import numpy as np
from jax import lax
from jax.experimental import pallas as pl
from jax.experimental.pallas import tpu as pltpu
from jax.sharding import PartitionSpec as P

HEADS = 8
HD = 320
FH = 320
WINDOW = 512
NZ, NY, NC = 8, 4, 2
CHIPS = NZ * NY
OWN = 5
SLOT = 16
ZROWS = NY * NC * OWN
LAST_FIRST = 12288 * NZ // 16384
FIRST_SECOND = 4096 * NZ // 16384
FAR_FIRST = (4, 3, 5, 2, 6, 1, 7, 0)
NEAR_FIRST = (0, 1, 7, 2, 6, 3, 5, 4)
F32, BF16 = jnp.float32, jnp.bfloat16


def nn(a, b):
    return lax.dot_general(a, b, (((1,), (0,)), ((), ())), preferred_element_type=F32)


def nt(a, b):
    return lax.dot_general(a, b, (((1,), (1,)), ((), ())), preferred_element_type=F32)


def tn(a, b):
    return lax.dot_general(a, b, (((0,), (0,)), ((), ())), preferred_element_type=F32)


def order_matrix():
    perm = np.zeros((128, 128), np.float32)
    for m in range(3):
        for y in range(NY):
            for c in range(NC):
                for j in range(OWN):
                    perm[m * ZROWS + (y * NC + c) * OWN + j, c * 64 + y * SLOT + m * OWN + j] = 1.0
    return perm


def kernel(
    ge, q_hbm, k_hbm, v_hbm, rates_hbm, back_hbm, g_hbm, u_hbm, d_hbm, gain_hbm, perm_hbm, perm_t_hbm,
    out, g_out, u_out, d_out,
    q, k, v, rates, back, rows0, gain, perm, perm_t,
    own, ag, gs, cr, red, rr, kv_far, kv_near, sq, sqr, nat, gt, ut, dt, es, y_buf, probs, state,
    in_sem, ag_send, ag_recv, fw_send, fw_recv, cs_send, cs_recv, rs_send, rs_recv, kv_send, kv_recv, sq_send, sq_recv,
):
    toks = q.shape[1]
    t = lax.axis_index("tok")
    h = lax.axis_index("head")
    c = lax.rem(t, 2)
    chip = lax.div(t, 2)
    zme = lax.div(chip, NY)
    yme = lax.rem(chip, NY)
    mate = t + 1 - 2 * c

    loads = [
        pltpu.make_async_copy(src, dst, in_sem.at[n])
        for n, (src, dst) in enumerate(
            (
                (g_hbm, rows0.at[pl.ds(0, OWN)]),
                (u_hbm, rows0.at[pl.ds(OWN, OWN)]),
                (d_hbm, rows0.at[pl.ds(2 * OWN, OWN)]),
                (k_hbm, k),
                (v_hbm, v),
                (q_hbm, q),
                (rates_hbm, rates),
                (back_hbm, back),
                (gain_hbm, gain),
                (perm_hbm, perm),
                (perm_t_hbm, perm_t),
            )
        )
    ]
    for load in loads:
        load.start()

    def at_chip(p):
        return {"tok": 2 * p + c}

    barrier = pltpu.get_barrier_semaphore()

    def greet(i, _):
        pl.semaphore_signal(barrier, inc=1, device_id=at_chip(lax.rem(chip + i, CHIPS)))
        return 0

    lax.fori_loop(1, CHIPS, greet, 0)
    pl.semaphore_signal(barrier, inc=1, device_id={"tok": mate})

    def greet_head(i, _):
        pl.semaphore_signal(barrier, inc=1, device_id={"head": lax.rem(h + i, HEADS)})
        return 0

    lax.fori_loop(1, HEADS, greet_head, 0)

    rows0[pl.ds(3 * OWN, 1)] = jnp.zeros((1, 1, HD), F32)
    for load in loads:
        load.wait()
    state[...] = rows0[...].reshape(SLOT, HD)
    own[0] = state[...].astype(BF16)
    start = t * toks
    first = start + lax.broadcasted_iota(jnp.int32, (1, toks), 1) < ge[0]
    rate = rates[...]
    vf = v[...].astype(F32)
    es[0] = (-jnp.where(first, rate, 0.0) * vf).astype(BF16)
    es[1] = (-jnp.where(first, 0.0, rate) * vf).astype(BF16)
    y_buf[...] = jnp.zeros_like(y_buf)

    pl.semaphore_wait(barrier, (CHIPS - 1) + 1 + (HEADS - 1))

    def active(g, z):
        return z < LAST_FIRST if g == 0 else z >= FIRST_SECOND

    live = [active(g, zme) for g in range(2)]
    z_from = (0, FIRST_SECOND)

    def peers(dzs, body):
        for dz in dzs:
            zz = lax.rem(zme + dz, NZ)
            for dy in range(NY):
                yy = lax.rem(yme + dy, NY)
                body(zz, yy, dz == 0 and dy == 0)

    def gather_start(g):
        mine = ag.at[g, c, chip]

        def send(zz, yy, is_me):
            @pl.when(active(g, zz))
            def _():
                if is_me:
                    pltpu.make_async_copy(own.at[g], mine, ag_recv.at[g, zme]).start()
                else:
                    pltpu.make_async_remote_copy(
                        own.at[g], mine, ag_send.at[g], ag_recv.at[g, zme], at_chip(zz * NY + yy)
                    ).start()

        peers(FAR_FIRST, send)

    def gather_forward(g):
        for dz in NEAR_FIRST:
            zz = lax.rem(zme + dz, NZ)
            four = ag.at[g, c, pl.ds(zz * NY, NY)]
            pltpu.make_async_copy(four, four, ag_recv.at[g, zz]).wait()
            pltpu.make_async_remote_copy(four, four, fw_send.at[g], fw_recv.at[g, zz], {"tok": mate}).start()

    def gather_finish(g):
        for z in range(NZ):
            four = ag.at[g, 1 - c, pl.ds(z * NY, NY)]
            pltpu.make_async_copy(four, four, fw_recv.at[g, z]).wait()
            block = ag[g, :, z * NY : (z + 1) * NY].reshape(NC * NY * SLOT, HD)
            ordered = nn(perm[...], block)
            for m in range(3):
                nat[m, z * ZROWS : (z + 1) * ZROWS] = ordered[m * ZROWS : (m + 1) * ZROWS]
        gt[...] = nat[0].astype(BF16)
        ut[...] = nat[1].astype(BF16)
        dt[...] = nat[2].astype(BF16)

    def gather_drain(g):
        sends = NY * (LAST_FIRST if g == 0 else NZ - FIRST_SECOND)

        def drain(n):
            some = ag.at[g, 0, pl.ds(0, n)]
            pltpu.make_async_copy(some, some, ag_send.at[g]).wait()

        @pl.when(live[g])
        def _():
            drain(sends - 1)
            every = ag.at[g, 0]
            pltpu.make_async_copy(every, every, fw_send.at[g]).wait()

        @pl.when(jnp.logical_not(live[g]))
        def _():
            drain(sends)

    def grads(g):
        kk, e = k[...], es[g]
        a = nn(gt[...], kk)
        b = nn(ut[...], kk)
        s = jax.nn.sigmoid(a)
        act = a * s
        r = (act * b).astype(BF16)
        du = tn(dt[...], e)
        da = (du * b * s * (1.0 + a * (1.0 - s))).astype(BF16)
        db = (du * act).astype(BF16)
        nat[0] = nt(da, kk)
        nat[1] = nt(db, kk)
        nat[2] = nt(e, r)

    def reduce_start(g):
        for z in range(NZ):
            part = [nat[m, z * ZROWS : (z + 1) * ZROWS] for m in range(3)]
            part.append(jnp.zeros((128 - 3 * ZROWS, HD), F32))
            block = nn(perm_t[...], jnp.concatenate(part, axis=0).astype(BF16)).astype(BF16)
            gs[g, :, z * NY : (z + 1) * NY] = block.reshape(NC, NY, SLOT, HD)
            pltpu.make_async_remote_copy(
                gs.at[g, 1 - c, pl.ds(z * NY, NY)], cr.at[g, pl.ds(z * NY, NY)],
                cs_send.at[g], cs_recv.at[g, z], {"tok": mate},
            ).start()
        for dz in FAR_FIRST:
            zz = lax.rem(zme + dz, NZ)
            here = pl.ds(zz * NY, NY)
            four = cr.at[g, here]
            pltpu.make_async_copy(four, four, cs_recv.at[g, zz]).wait()
            red[g, here] = (gs[g, c, here].astype(F32) + cr[g, here].astype(F32)).astype(BF16)
            landing = rr.at[g, chip - z_from[g] * NY]

            def send(z_to, yy, is_me):
                p = z_to * NY + yy
                if is_me:
                    pltpu.make_async_copy(red.at[g, p], landing, rs_recv.at[g]).start()
                else:
                    pltpu.make_async_remote_copy(
                        red.at[g, p], landing, rs_send.at[g], rs_recv.at[g], at_chip(p)
                    ).start()

            peers((dz,), send)

    def reduce_finish(g):
        every = rr.at[g]
        pltpu.make_async_copy(every, every, rs_recv.at[g]).wait()
        total = jnp.sum(rr[g].astype(F32), axis=0)
        old = state[...]
        fresh = old - total
        old_norm = jnp.sqrt(jnp.sum(old * old, axis=1, keepdims=True))
        new_norm = jnp.sqrt(jnp.sum(fresh * fresh, axis=1, keepdims=True) + 1e-06)
        return fresh * (old_norm / new_norm)

    def reduce_drain(g):
        @pl.when(live[g])
        def _():
            every = cr.at[g]
            pltpu.make_async_copy(every, every, cs_send.at[g]).wait()
            thirty_one = red.at[g, pl.ds(0, CHIPS - 1)]
            pltpu.make_async_copy(thirty_one, thirty_one, rs_send.at[g]).wait()

    def apply_queries():
        a = nn(gt[...], q[...])
        b = nn(ut[...], q[...])
        hidden = (a * jax.nn.sigmoid(a) * b).astype(BF16)
        return nn(dt[...], hidden)

    def far_copy(n):
        return pltpu.make_async_remote_copy(
            (k, v)[n], kv_far.at[n], kv_send.at[n], kv_recv.at[n], at_chip(lax.rem(chip + 1, CHIPS))
        )

    def near_copy(n, src):
        return pltpu.make_async_remote_copy(src, kv_near.at[n], kv_send.at[2 + n], kv_recv.at[2 + n], {"tok": mate})

    def pass_on(n):
        far_copy(n).wait()

        @pl.when(c == 1)
        def _():
            near_copy(n, kv_far.at[n]).start()

    gather_start(0)

    @pl.when(c == 0)
    def _():
        for n in range(2):
            near_copy(n, (k, v)[n]).start()

    @pl.when(live[0])
    def _():
        gather_forward(0)

    far_copy(0).start()

    @pl.when(live[0])
    def _():
        gather_finish(0)
        grads(0)
        reduce_start(0)
        y_buf[...] = apply_queries()

    pass_on(0)
    middle = reduce_finish(0)
    state[...] = middle
    own[1] = middle.astype(BF16)
    gather_start(1)

    near_copy(0, k).wait()
    scale = 1.0 / math.sqrt(HD)
    j = lax.broadcasted_iota(jnp.int32, (toks, toks), 0)
    i = lax.broadcasted_iota(jnp.int32, (toks, toks), 1)
    reach = back[...]
    scores = []
    for ahead, keys in ((2 * toks, kv_far.at[0]), (toks, kv_near.at[0]), (0, k)):
        away = i - j + ahead
        seen = (away >= 0) & (away <= reach) & (start + j - ahead >= 0)
        scores.append(jnp.where(seen, tn(keys[...], q[...]) * scale, -jnp.inf))
    top = functools.reduce(jnp.maximum, [jnp.max(s, axis=0, keepdims=True) for s in scores])
    weights = [jnp.exp(s - top) for s in scores]
    total = functools.reduce(jnp.add, [jnp.sum(w, axis=0, keepdims=True) for w in weights])
    for n, w in enumerate(weights):
        probs[n] = (w / total).astype(BF16)

    @pl.when(live[1])
    def _():
        gather_forward(1)

    far_copy(1).start()

    @pl.when(live[1])
    def _():
        gather_finish(1)
        grads(1)
        reduce_start(1)
        y_buf[...] = jnp.where(first, y_buf[...], apply_queries())

    mixed = y_buf[...]
    sums = jnp.sum(mixed * mixed, axis=0, keepdims=True)
    sq[...] = sums
    sqr[h] = sums

    def send_squares(n, _):
        pltpu.make_async_remote_copy(sq, sqr.at[h], sq_send, sq_recv, {"head": lax.rem(h + n, HEADS)}).start()
        return 0

    lax.fori_loop(1, HEADS, send_squares, 0)
    pass_on(1)
    near_copy(1, v).wait()
    attn = nn(kv_far[1], probs[0]) + nn(kv_near[1], probs[1]) + nn(v[...], probs[2])
    seven = sqr.at[pl.ds(0, HEADS - 1)]
    pltpu.make_async_copy(seven, seven, sq_recv).wait()
    mean_square = jnp.sum(sqr[...], axis=0) / (HEADS * HD)
    gains = jnp.broadcast_to(gain[...].reshape(1, HD), (8, HD)).T[:, 0:1]
    normed = y_buf[...] / jnp.sqrt(mean_square + 1e-06) * gains
    out[...] = (normed + attn).astype(BF16)
    last = reduce_finish(1)
    for m, ref in enumerate((g_out, u_out, d_out)):
        ref[...] = last[m * OWN : (m + 1) * OWN].reshape(OWN, 1, HD)
    pltpu.make_async_copy(seven, seven, sq_send).wait()
    for g in range(2):
        gather_drain(g)
        reduce_drain(g)


def write_out(*refs):
    half = len(refs) // 2
    srcs, dsts, sem = refs[:half], refs[half:-1], refs[-1]
    copies = [pltpu.make_async_copy(src, dst, sem.at[n]) for n, (src, dst) in enumerate(zip(srcs, dsts))]
    for copy in copies:
        copy.start()
    for copy in copies:
        copy.wait()


def on_device(queries, keys, values, rates, back, group_end, gate_init, up_init, down_init, gain):
    toks = rates.shape[0]
    perm = order_matrix()
    vmem = pl.BlockSpec(memory_space=pltpu.VMEM)
    hbm = pl.BlockSpec(memory_space=pltpu.HBM)
    slots = (CHIPS, SLOT, HD)
    dma = pltpu.SemaphoreType.DMA
    shares = [w.transpose(2, 0, 1) for w in (gate_init, up_init, down_init)]
    share = jax.ShapeDtypeStruct((OWN, 1, HD), F32)
    shapes = (jax.ShapeDtypeStruct((HD, toks), BF16), share, share, share)
    results = pl.pallas_call(
        kernel,
        out_shape=shapes,
        in_specs=[pl.BlockSpec(memory_space=pltpu.SMEM)] + [hbm] * 11,
        out_specs=(vmem,) * 4,
        scratch_shapes=[
            pltpu.VMEM((HD, toks), BF16),
            pltpu.VMEM((HD, toks), BF16),
            pltpu.VMEM((HD, toks), BF16),
            pltpu.VMEM((1, toks), F32),
            pltpu.VMEM((1, toks), jnp.int32),
            pltpu.VMEM((SLOT, 1, HD), F32),
            pltpu.VMEM((HD,), F32),
            pltpu.VMEM((128, 128), BF16),
            pltpu.VMEM((128, 128), BF16),
            pltpu.VMEM((2, SLOT, HD), BF16),
            pltpu.VMEM((2, NC, *slots), BF16),
            pltpu.VMEM((2, NC, *slots), BF16),
            pltpu.VMEM((2, *slots), BF16),
            pltpu.VMEM((2, *slots), BF16),
            pltpu.VMEM((2, LAST_FIRST * NY, SLOT, HD), BF16),
            pltpu.VMEM((2, HD, toks), BF16),
            pltpu.VMEM((2, HD, toks), BF16),
            pltpu.VMEM((1, toks), F32),
            pltpu.VMEM((HEADS, 1, toks), F32),
            pltpu.VMEM((3, HD, HD), F32),
            pltpu.VMEM((FH, HD), BF16),
            pltpu.VMEM((FH, HD), BF16),
            pltpu.VMEM((HD, FH), BF16),
            pltpu.VMEM((2, HD, toks), BF16),
            pltpu.VMEM((HD, toks), F32),
            pltpu.VMEM((3, toks, toks), BF16),
            pltpu.VMEM((SLOT, HD), F32),
            dma((11,)),
            dma((2,)), dma((2, NZ)),
            dma((2,)), dma((2, NZ)),
            dma((2,)), dma((2, NZ)),
            dma((2,)), dma((2,)),
            dma((4,)), dma((4,)),
            dma, dma,
        ],
        compiler_params=pltpu.CompilerParams(
            collective_id=0, has_side_effects=True, vmem_limit_bytes=48 * 1024 * 1024
        ),
        name="layer",
    )(
        group_end,
        *(
            pltpu.with_memory_space_constraint(array, pltpu.HBM)
            for array in (
                queries.T, keys.T, values.T, rates.T, back.reshape(1, toks), *shares, gain,
                jnp.asarray(perm, BF16), jnp.asarray(perm.T, BF16),
            )
        ),
    )
    out, *finals = pl.pallas_call(
        write_out,
        out_shape=shapes,
        in_specs=[vmem] * 4,
        out_specs=(hbm,) * 4,
        scratch_shapes=[dma((4,))],
        compiler_params=pltpu.CompilerParams(vmem_limit_bytes=1024 * 1024),
        name="write_out",
    )(*results)
    return (out.T, *(w.transpose(1, 2, 0) for w in finals))


def solution(mesh):
    placed = (
        P("tok", "head"),
        P("tok", "head"),
        P("tok", "head"),
        P("tok", "head"),
        P("tok"),
        P(),
        P("head", None, "tok"),
        P("head", None, "tok"),
        P("head", None, "tok"),
        P("head"),
    )
    return jax.shard_map(
        on_device,
        mesh=mesh,
        in_specs=placed,
        out_specs=(
            P("tok", "head"),
            P("head", None, "tok"),
            P("head", None, "tok"),
            P("head", None, "tok"),
        ),
        check_vma=False,
    )
```

```python
import functools
import math

import jax
import jax.numpy as jnp
import numpy as np
from jax import lax
from jax.experimental import pallas as pl
from jax.experimental.pallas import tpu as pltpu
from jax.sharding import PartitionSpec as P

HEADS = 8
HD = 320
FH = 320
WINDOW = 512
NZ, NY, NC = 8, 4, 2
CHIPS = NZ * NY
OWN = 5
SLOT = 16
LINES = 40
PAD = 384
ZROWS = NY * NC * OWN
LAST_FIRST = 12288 * NZ // 16384
FIRST_SECOND = 4096 * NZ // 16384
FAR_FIRST = (4, 3, 5, 2, 6, 1, 7, 0)
NEAR_FIRST = (0, 1, 7, 2, 6, 3, 5, 4)
F32, BF16 = jnp.float32, jnp.bfloat16


def nn(a, b):
    return lax.dot_general(a, b, (((1,), (0,)), ((), ())), preferred_element_type=F32)


def nt(a, b):
    return lax.dot_general(a, b, (((1,), (1,)), ((), ())), preferred_element_type=F32)


def tn(a, b):
    return lax.dot_general(a, b, (((0,), (0,)), ((), ())), preferred_element_type=F32)


def order_matrices():
    perm = np.zeros((2, 128, 128), np.float32)
    for m in range(3):
        for y in range(NY):
            for c in range(NC):
                for j in range(OWN):
                    row = m * OWN + j
                    natural = m * ZROWS + (y * NC + c) * OWN + j
                    perm[0, natural, c * 64 + y * SLOT + row] = 1.0
                    perm[1, natural, row // 8 * 64 + c * 32 + y * 8 + row % 8] = 1.0
    return np.concatenate([perm, perm.transpose(0, 2, 1)])


def pack(rows):
    last = rows[:, 256:384]
    return jnp.concatenate([rows[:, 0:128], rows[:, 128:256], last[0:8] + pltpu.roll(last[8:16], 64, 1)], axis=0)


def unpack(packed):
    last = jnp.concatenate([packed[32:40], pltpu.roll(packed[32:40], 64, 1)], axis=0)
    return jnp.concatenate([packed[0:16], packed[16:32], last[:, 0:64]], axis=1)


def row_sums(packed):
    left = lax.broadcasted_iota(jnp.int32, (8, 128), 1) < 64
    last = packed[32:40]
    ends = [jnp.where(left, last, 0.0), jnp.where(left, 0.0, last)]
    whole = packed[0:16] + packed[16:32] + jnp.concatenate(ends, axis=0)
    return jnp.sum(whole, axis=1, keepdims=True)


def spread(factor):
    wide = jnp.broadcast_to(factor, (SLOT, 128))
    left = lax.broadcasted_iota(jnp.int32, (8, 128), 1) < 64
    return jnp.concatenate([wide, wide, jnp.where(left, wide[0:8], wide[8:16])], axis=0)


def kernel(
    ge, q_hbm, k_hbm, v_hbm, rates_hbm, back_hbm, g_hbm, u_hbm, d_hbm, gain_hbm, perm_hbm,
    out, g_out, u_out, d_out,
    q, k, v, rates, back, rows0, gain, perm,
    own, ag, gs, cr, red, rr, kv_far, kv_near, sq, sqr, nat, gt, ut, dt, es, y_buf, probs, state,
    in_sem, ag_send, ag_recv, fw_send, fw_recv, cs_send, cs_recv, rs_send, rs_recv, kv_send, kv_recv, sq_send, sq_recv,
):
    toks = q.shape[1]
    t = lax.axis_index("tok")
    h = lax.axis_index("head")
    c = lax.rem(t, 2)
    chip = lax.div(t, 2)
    zme = lax.div(chip, NY)
    yme = lax.rem(chip, NY)
    mate = t + 1 - 2 * c

    loads = [
        pltpu.make_async_copy(src, dst, in_sem.at[n])
        for n, (src, dst) in enumerate(
            (
                (g_hbm, rows0.at[pl.ds(0, OWN)]),
                (u_hbm, rows0.at[pl.ds(OWN, OWN)]),
                (d_hbm, rows0.at[pl.ds(2 * OWN, OWN)]),
                (k_hbm, k.at[pl.ds(0, HD)]),
                (v_hbm, v),
                (q_hbm, q),
                (rates_hbm, rates),
                (back_hbm, back),
                (gain_hbm, gain),
                (perm_hbm, perm),
            )
        )
    ]
    for load in loads:
        load.start()

    def at_chip(p):
        return {"tok": 2 * p + c}

    barrier = pltpu.get_barrier_semaphore()

    def greet(i, _):
        pl.semaphore_signal(barrier, inc=1, device_id=at_chip(lax.rem(chip + i, CHIPS)))
        return 0

    lax.fori_loop(1, CHIPS, greet, 0)
    pl.semaphore_signal(barrier, inc=1, device_id={"tok": mate})

    def greet_head(i, _):
        pl.semaphore_signal(barrier, inc=1, device_id={"head": lax.rem(h + i, HEADS)})
        return 0

    lax.fori_loop(1, HEADS, greet_head, 0)

    rows0[pl.ds(3 * OWN, 1)] = jnp.zeros((1, 1, HD), F32)
    for load in loads:
        load.wait()
    share = rows0[...].reshape(SLOT, HD)
    state[...] = pack(jnp.concatenate([share, jnp.zeros((SLOT, PAD - HD), F32)], axis=1))
    own[0] = state[...].astype(BF16)
    k[pl.ds(HD, PAD - HD)] = jnp.zeros((PAD - HD, toks), BF16)
    start = t * toks
    first = start + lax.broadcasted_iota(jnp.int32, (1, toks), 1) < ge[0]
    rate = rates[...]
    vf = v[...].astype(F32)
    es[0] = (-jnp.where(first, rate, 0.0) * vf).astype(BF16)
    es[1] = (-jnp.where(first, 0.0, rate) * vf).astype(BF16)
    y_buf[...] = jnp.zeros_like(y_buf)

    pl.semaphore_wait(barrier, (CHIPS - 1) + 1 + (HEADS - 1))

    def active(g, z):
        return z < LAST_FIRST if g == 0 else z >= FIRST_SECOND

    live = [active(g, zme) for g in range(2)]
    z_from = (0, FIRST_SECOND)

    def peers(dzs, body):
        for dz in dzs:
            zz = lax.rem(zme + dz, NZ)
            for dy in range(NY):
                yy = lax.rem(yme + dy, NY)
                body(zz, yy, dz == 0 and dy == 0)

    def gather_start(g):
        mine = ag.at[g, c, chip]

        def send(zz, yy, is_me):
            @pl.when(active(g, zz))
            def _():
                if is_me:
                    pltpu.make_async_copy(own.at[g], mine, ag_recv.at[g, zme]).start()
                else:
                    pltpu.make_async_remote_copy(
                        own.at[g], mine, ag_send.at[g], ag_recv.at[g, zme], at_chip(zz * NY + yy)
                    ).start()

        peers(FAR_FIRST, send)

    def block_at(zz):
        return pl.ds(pl.multiple_of(zz * ZROWS, 8), ZROWS)

    def gather_finish(g):
        def arrange(zz):
            four = ag.at[g, 1 - c, pl.ds(zz * NY, NY)]
            pltpu.make_async_copy(four, four, fw_recv.at[g, zz]).wait()
            both = [ag[g, core, pl.ds(zz * NY, NY)] for core in range(NC)]
            wide = [
                jnp.concatenate([x[:, r : r + SLOT].reshape(NY * SLOT, 128) for x in both], axis=0) for r in (0, SLOT)
            ]
            ordered = nn(perm[0], jnp.concatenate(wide, axis=1))
            ends = jnp.concatenate([x[:, 2 * SLOT :].reshape(NY * 8, 128) for x in both], axis=0).astype(F32)
            left = lax.broadcasted_iota(jnp.int32, ends.shape, 1) < 64
            halves = [jnp.where(left, x, 0.0) for x in (ends, pltpu.roll(ends, 64, 1))]
            ordered_ends = nn(perm[1], jnp.concatenate(halves, axis=0).astype(BF16))
            for m in range(3):
                rows = slice(m * ZROWS, (m + 1) * ZROWS)
                nat[m, block_at(zz), 0:256] = ordered[rows]
                nat[m, block_at(zz), 256:PAD] = ordered_ends[rows]

        order = [lax.rem(zme + dz, NZ) for dz in NEAR_FIRST]
        for n, zz in enumerate(order):
            four = ag.at[g, c, pl.ds(zz * NY, NY)]
            pltpu.make_async_copy(four, four, ag_recv.at[g, zz]).wait()
            pltpu.make_async_remote_copy(four, four, fw_send.at[g], fw_recv.at[g, zz], {"tok": mate}).start()
            if n:
                arrange(order[n - 1])
        far_copy(g).start()
        arrange(order[-1])
        for m, ref in enumerate((gt, ut, dt)):
            ref[...] = nat[m, :, 0:HD].astype(BF16)

    def gather_drain(g):
        sends = NY * (LAST_FIRST if g == 0 else NZ - FIRST_SECOND)

        def drain(n):
            some = ag.at[g, 0, pl.ds(0, n)]
            pltpu.make_async_copy(some, some, ag_send.at[g]).wait()

        @pl.when(live[g])
        def _():
            drain(sends - 1)
            every = ag.at[g, 0]
            pltpu.make_async_copy(every, every, fw_send.at[g]).wait()

        @pl.when(jnp.logical_not(live[g]))
        def _():
            drain(sends)

    def grads(g):
        kk, e = k[pl.ds(0, HD)], es[g]
        a = nn(gt[...], kk)
        b = nn(ut[...], kk)
        s = jax.nn.sigmoid(a)
        act = a * s
        r = (act * b).astype(BF16)
        du = tn(dt[...], e)
        da = (du * b * s * (1.0 + a * (1.0 - s))).astype(BF16)
        db = (du * act).astype(BF16)
        nat[0] = nt(da, k[...])
        nat[1] = nt(db, k[...])
        nat[2] = nt(e, jnp.concatenate([r, jnp.zeros((PAD - FH, toks), BF16)], axis=0))

    def reduce_start(g):
        def split(zz):
            part = [nat[m, block_at(zz)] for m in range(3)]
            part.append(jnp.zeros((128 - 3 * ZROWS, PAD), F32))
            block = jnp.concatenate(part, axis=0).astype(BF16)
            slots = nn(perm[2], block[:, 0:256]).astype(BF16)
            ends = nn(perm[3], block[:, 256:PAD])
            ends = (ends[0:64] + pltpu.roll(ends[64:128], 64, 1)).astype(BF16)
            here = pl.ds(zz * NY, NY)
            gs[g, :, here, 0:SLOT] = slots[:, 0:128].reshape(NC, NY, SLOT, 128)
            gs[g, :, here, SLOT : 2 * SLOT] = slots[:, 128:256].reshape(NC, NY, SLOT, 128)
            gs[g, :, here, 2 * SLOT : LINES] = ends.reshape(NC, NY, 8, 128)
            pltpu.make_async_remote_copy(
                gs.at[g, 1 - c, here], cr.at[g, here], cs_send.at[g], cs_recv.at[g, zz], {"tok": mate}
            ).start()

        landing = rr.at[g, chip - z_from[g] * NY]

        def send(zz, yy, is_me):
            p = zz * NY + yy
            if is_me:
                pltpu.make_async_copy(red.at[g, p], landing, rs_recv.at[g]).start()
            else:
                pltpu.make_async_remote_copy(
                    red.at[g, p], landing, rs_send.at[g], rs_recv.at[g], at_chip(p)
                ).start()

        def pass_sum(dz):
            zz = lax.rem(zme + dz, NZ)
            here = pl.ds(zz * NY, NY)
            four = cr.at[g, here]
            pltpu.make_async_copy(four, four, cs_recv.at[g, zz]).wait()
            red[g, here] = (gs[g, c, here].astype(F32) + cr[g, here].astype(F32)).astype(BF16)
            peers((dz,), send)

        lag = 4
        for n, dz in enumerate(FAR_FIRST):
            split(lax.rem(zme + dz, NZ))
            if n >= lag:
                pass_sum(FAR_FIRST[n - lag])
        for dz in FAR_FIRST[NZ - lag :]:
            pass_sum(dz)

    def reduce_finish(g):
        every = rr.at[g]
        pltpu.make_async_copy(every, every, rs_recv.at[g]).wait()
        total = jnp.sum(rr[g].astype(F32), axis=0)
        old = state[...]
        fresh = old - total
        old_norm = jnp.sqrt(row_sums(old * old))
        new_norm = jnp.sqrt(row_sums(fresh * fresh) + 1e-06)
        return fresh * spread(old_norm / new_norm)

    def reduce_drain(g):
        @pl.when(live[g])
        def _():
            every = cr.at[g]
            pltpu.make_async_copy(every, every, cs_send.at[g]).wait()
            thirty_one = red.at[g, pl.ds(0, CHIPS - 1)]
            pltpu.make_async_copy(thirty_one, thirty_one, rs_send.at[g]).wait()

    def apply_queries():
        a = nn(gt[...], q[...])
        b = nn(ut[...], q[...])
        hidden = (a * jax.nn.sigmoid(a) * b).astype(BF16)
        return nn(dt[...], hidden)

    def far_copy(n):
        return pltpu.make_async_remote_copy(
            (k.at[pl.ds(0, HD)], v)[n], kv_far.at[n], kv_send.at[n], kv_recv.at[n], at_chip(lax.rem(chip + 1, CHIPS))
        )

    def near_copy(n, src):
        return pltpu.make_async_remote_copy(src, kv_near.at[n], kv_send.at[2 + n], kv_recv.at[2 + n], {"tok": mate})

    def pass_on(n):
        far_copy(n).wait()

        @pl.when(c == 1)
        def _():
            near_copy(n, kv_far.at[n]).start()

    gather_start(0)

    @pl.when(c == 0)
    def _():
        for n in range(2):
            near_copy(n, (k.at[pl.ds(0, HD)], v)[n]).start()

    @pl.when(jnp.logical_not(live[0]))
    def _():
        far_copy(0).start()

    @pl.when(live[0])
    def _():
        gather_finish(0)
        grads(0)
        reduce_start(0)
        y_buf[...] = apply_queries()

    pass_on(0)
    middle = reduce_finish(0)
    state[...] = middle
    own[1] = middle.astype(BF16)
    gather_start(1)

    near_copy(0, kv_far.at[0]).wait()
    scale = 1.0 / math.sqrt(HD)
    j = lax.broadcasted_iota(jnp.int32, (toks, toks), 0)
    i = lax.broadcasted_iota(jnp.int32, (toks, toks), 1)
    reach = back[...]
    scores = []
    for ahead, keys in ((2 * toks, kv_far.at[0]), (toks, kv_near.at[0]), (0, k.at[pl.ds(0, HD)])):
        away = i - j + ahead
        seen = (away >= 0) & (away <= reach) & (start + j - ahead >= 0)
        scores.append(jnp.where(seen, tn(keys[...], q[...]) * scale, -jnp.inf))
    top = functools.reduce(jnp.maximum, [jnp.max(s, axis=0, keepdims=True) for s in scores])
    weights = [jnp.exp(s - top) for s in scores]
    total = functools.reduce(jnp.add, [jnp.sum(w, axis=0, keepdims=True) for w in weights])
    for n, w in enumerate(weights):
        probs[n] = (w / total).astype(BF16)

    @pl.when(jnp.logical_not(live[1]))
    def _():
        far_copy(1).start()

    @pl.when(live[1])
    def _():
        gather_finish(1)
        grads(1)
        reduce_start(1)
        y_buf[...] = jnp.where(first, y_buf[...], apply_queries())

    mixed = y_buf[...]
    sums = jnp.sum(mixed * mixed, axis=0, keepdims=True)
    sq[...] = sums
    sqr[h] = sums

    def send_squares(n, _):
        pltpu.make_async_remote_copy(sq, sqr.at[h], sq_send, sq_recv, {"head": lax.rem(h + n, HEADS)}).start()
        return 0

    lax.fori_loop(1, HEADS, send_squares, 0)
    pass_on(1)
    near_copy(1, v).wait()
    attn = nn(kv_far[1], probs[0]) + nn(kv_near[1], probs[1]) + nn(v[...], probs[2])
    seven = sqr.at[pl.ds(0, HEADS - 1)]
    pltpu.make_async_copy(seven, seven, sq_recv).wait()
    mean_square = jnp.sum(sqr[...], axis=0) / (HEADS * HD)
    gains = jnp.broadcast_to(gain[...].reshape(1, HD), (8, HD)).T[:, 0:1]
    normed = y_buf[...] / jnp.sqrt(mean_square + 1e-06) * gains
    out[...] = (normed + attn).astype(BF16)
    last = unpack(reduce_finish(1))
    for m, ref in enumerate((g_out, u_out, d_out)):
        ref[...] = last[m * OWN : (m + 1) * OWN].reshape(OWN, 1, HD)
    pltpu.make_async_copy(seven, seven, sq_send).wait()
    for g in range(2):
        gather_drain(g)
        reduce_drain(g)


def write_out(*refs):
    half = len(refs) // 2
    srcs, dsts, sem = refs[:half], refs[half:-1], refs[-1]
    copies = [pltpu.make_async_copy(src, dst, sem.at[n]) for n, (src, dst) in enumerate(zip(srcs, dsts))]
    for copy in copies:
        copy.start()
    for copy in copies:
        copy.wait()


def on_device(queries, keys, values, rates, back, group_end, gate_init, up_init, down_init, gain):
    toks = rates.shape[0]
    perm = order_matrices()
    vmem = pl.BlockSpec(memory_space=pltpu.VMEM)
    hbm = pl.BlockSpec(memory_space=pltpu.HBM)
    slots = (CHIPS, LINES, 128)
    dma = pltpu.SemaphoreType.DMA
    shares = [w.transpose(2, 0, 1) for w in (gate_init, up_init, down_init)]
    share = jax.ShapeDtypeStruct((OWN, 1, HD), F32)
    shapes = (jax.ShapeDtypeStruct((HD, toks), BF16), share, share, share)
    results = pl.pallas_call(
        kernel,
        out_shape=shapes,
        in_specs=[pl.BlockSpec(memory_space=pltpu.SMEM)] + [hbm] * 10,
        out_specs=(vmem,) * 4,
        scratch_shapes=[
            pltpu.VMEM((HD, toks), BF16),
            pltpu.VMEM((PAD, toks), BF16),
            pltpu.VMEM((HD, toks), BF16),
            pltpu.VMEM((1, toks), F32),
            pltpu.VMEM((1, toks), jnp.int32),
            pltpu.VMEM((SLOT, 1, HD), F32),
            pltpu.VMEM((HD,), F32),
            pltpu.VMEM((4, 128, 128), BF16),
            pltpu.VMEM((2, LINES, 128), BF16),
            pltpu.VMEM((2, NC, *slots), BF16),
            pltpu.VMEM((2, NC, *slots), BF16),
            pltpu.VMEM((2, *slots), BF16),
            pltpu.VMEM((2, *slots), BF16),
            pltpu.VMEM((2, LAST_FIRST * NY, LINES, 128), BF16),
            pltpu.VMEM((2, HD, toks), BF16),
            pltpu.VMEM((2, HD, toks), BF16),
            pltpu.VMEM((1, toks), F32),
            pltpu.VMEM((HEADS, 1, toks), F32),
            pltpu.VMEM((3, HD, PAD), F32),
            pltpu.VMEM((FH, HD), BF16),
            pltpu.VMEM((FH, HD), BF16),
            pltpu.VMEM((HD, FH), BF16),
            pltpu.VMEM((2, HD, toks), BF16),
            pltpu.VMEM((HD, toks), F32),
            pltpu.VMEM((3, toks, toks), BF16),
            pltpu.VMEM((LINES, 128), F32),
            dma((10,)),
            dma((2,)), dma((2, NZ)),
            dma((2,)), dma((2, NZ)),
            dma((2,)), dma((2, NZ)),
            dma((2,)), dma((2,)),
            dma((4,)), dma((4,)),
            dma, dma,
        ],
        compiler_params=pltpu.CompilerParams(
            collective_id=0, has_side_effects=True, vmem_limit_bytes=48 * 1024 * 1024
        ),
        name="layer",
    )(
        group_end,
        *(
            pltpu.with_memory_space_constraint(array, pltpu.HBM)
            for array in (
                queries.T, keys.T, values.T, rates.T, back.reshape(1, toks), *shares, gain,
                jnp.asarray(perm, BF16),
            )
        ),
    )
    out, *finals = pl.pallas_call(
        write_out,
        out_shape=shapes,
        in_specs=[vmem] * 4,
        out_specs=(hbm,) * 4,
        scratch_shapes=[dma((4,))],
        compiler_params=pltpu.CompilerParams(vmem_limit_bytes=1024 * 1024),
        name="write_out",
    )(*results)
    return (out.T, *(w.transpose(1, 2, 0) for w in finals))


def solution(mesh):
    placed = (
        P("tok", "head"),
        P("tok", "head"),
        P("tok", "head"),
        P("tok", "head"),
        P("tok"),
        P(),
        P("head", None, "tok"),
        P("head", None, "tok"),
        P("head", None, "tok"),
        P("head"),
    )
    return jax.shard_map(
        on_device,
        mesh=mesh,
        in_specs=placed,
        out_specs=(
            P("tok", "head"),
            P("head", None, "tok"),
            P("head", None, "tok"),
            P("head", None, "tok"),
        ),
        check_vma=False,
    )
```

```python
import functools
import math

import jax
import jax.numpy as jnp
import numpy as np
from jax import lax
from jax.experimental import pallas as pl
from jax.experimental.pallas import tpu as pltpu
from jax.sharding import PartitionSpec as P

HEADS = 8
HD = 320
FH = 320
WINDOW = 512
NZ, NY, NC = 8, 4, 2
CHIPS = NZ * NY
OWN = 5
SLOT = 16
LINES = 40
PAD = 384
ZROWS = NY * NC * OWN
LAST_FIRST = 12288 * NZ // 16384
FIRST_SECOND = 4096 * NZ // 16384
FAR_FIRST = (4, 3, 5, 2, 6, 1, 7, 0)
NEAR_FIRST = (0, 1, 7, 2, 6, 3, 5, 4)
F32, BF16 = jnp.float32, jnp.bfloat16


def nn(a, b):
    return lax.dot_general(a, b, (((1,), (0,)), ((), ())), preferred_element_type=F32)


def nt(a, b):
    return lax.dot_general(a, b, (((1,), (1,)), ((), ())), preferred_element_type=F32)


def tn(a, b):
    return lax.dot_general(a, b, (((0,), (0,)), ((), ())), preferred_element_type=F32)


def order_matrices():
    perm = np.zeros((2, 128, 128), np.float32)
    for m in range(3):
        for y in range(NY):
            for c in range(NC):
                for j in range(OWN):
                    row = m * OWN + j
                    natural = m * ZROWS + (y * NC + c) * OWN + j
                    perm[0, natural, c * 64 + y * SLOT + row] = 1.0
                    perm[1, natural, row // 8 * 64 + c * 32 + y * 8 + row % 8] = 1.0
    return np.concatenate([perm, perm.transpose(0, 2, 1)])


def pack(rows):
    last = rows[:, 256:384]
    return jnp.concatenate([rows[:, 0:128], rows[:, 128:256], last[0:8] + pltpu.roll(last[8:16], 64, 1)], axis=0)


def unpack(packed):
    last = jnp.concatenate([packed[32:40], pltpu.roll(packed[32:40], 64, 1)], axis=0)
    return jnp.concatenate([packed[0:16], packed[16:32], last[:, 0:64]], axis=1)


def row_sums(packed):
    left = lax.broadcasted_iota(jnp.int32, (8, 128), 1) < 64
    last = packed[32:40]
    ends = [jnp.where(left, last, 0.0), jnp.where(left, 0.0, last)]
    whole = packed[0:16] + packed[16:32] + jnp.concatenate(ends, axis=0)
    return jnp.sum(whole, axis=1, keepdims=True)


def spread(factor):
    wide = jnp.broadcast_to(factor, (SLOT, 128))
    left = lax.broadcasted_iota(jnp.int32, (8, 128), 1) < 64
    return jnp.concatenate([wide, wide, jnp.where(left, wide[0:8], wide[8:16])], axis=0)


def kernel(
    ge, q_hbm, k_hbm, v_hbm, rates_hbm, back_hbm, g_hbm, u_hbm, d_hbm, gain_hbm, perm_hbm,
    out, g_out, u_out, d_out,
    q, k, v, rates, back, rows0, gain, perm,
    own, ag, gs, cr, red, rr, kv_far, kv_near, sq, sqr, nat, gt, ut, dt, es, y_buf, probs, state,
    in_sem, ag_send, ag_recv, fw_send, fw_recv, cs_send, cs_recv, rs_send, rs_recv, kv_send, kv_recv, sq_send, sq_recv,
):
    toks = q.shape[1]
    t = lax.axis_index("tok")
    h = lax.axis_index("head")
    c = lax.rem(t, 2)
    chip = lax.div(t, 2)
    zme = lax.div(chip, NY)
    yme = lax.rem(chip, NY)
    mate = t + 1 - 2 * c

    loads = [
        pltpu.make_async_copy(src, dst, in_sem.at[n])
        for n, (src, dst) in enumerate(
            (
                (g_hbm, rows0.at[pl.ds(0, OWN)]),
                (u_hbm, rows0.at[pl.ds(OWN, OWN)]),
                (d_hbm, rows0.at[pl.ds(2 * OWN, OWN)]),
                (k_hbm, k.at[pl.ds(0, HD)]),
                (v_hbm, v),
                (q_hbm, q),
                (rates_hbm, rates),
                (back_hbm, back),
                (gain_hbm, gain),
                (perm_hbm, perm),
            )
        )
    ]
    for load in loads:
        load.start()

    def at_chip(p):
        return {"tok": 2 * p + c}

    barrier = pltpu.get_barrier_semaphore()

    def greet(i, _):
        pl.semaphore_signal(barrier, inc=1, device_id=at_chip(lax.rem(chip + i, CHIPS)))
        return 0

    lax.fori_loop(1, CHIPS, greet, 0)
    pl.semaphore_signal(barrier, inc=1, device_id={"tok": mate})

    def greet_head(i, _):
        pl.semaphore_signal(barrier, inc=1, device_id={"head": lax.rem(h + i, HEADS)})
        return 0

    lax.fori_loop(1, HEADS, greet_head, 0)

    rows0[pl.ds(3 * OWN, 1)] = jnp.zeros((1, 1, HD), F32)
    for load in loads:
        load.wait()
    share = rows0[...].reshape(SLOT, HD)
    state[...] = pack(jnp.concatenate([share, jnp.zeros((SLOT, PAD - HD), F32)], axis=1))
    own[0] = state[...].astype(BF16)
    k[pl.ds(HD, PAD - HD)] = jnp.zeros((PAD - HD, toks), BF16)
    start = t * toks
    first = start + lax.broadcasted_iota(jnp.int32, (1, toks), 1) < ge[0]
    rate = rates[...]
    vf = v[...].astype(F32)
    es[0] = (-jnp.where(first, rate, 0.0) * vf).astype(BF16)
    es[1] = (-jnp.where(first, 0.0, rate) * vf).astype(BF16)
    y_buf[...] = jnp.zeros_like(y_buf)

    pl.semaphore_wait(barrier, (CHIPS - 1) + 1 + (HEADS - 1))

    def active(g, z):
        return z < LAST_FIRST if g == 0 else z >= FIRST_SECOND

    live = [active(g, zme) for g in range(2)]
    z_from = (0, FIRST_SECOND)

    def peers(dzs, body):
        for dz in dzs:
            zz = lax.rem(zme + dz, NZ)
            for dy in range(NY):
                yy = lax.rem(yme + dy, NY)
                body(zz, yy, dz == 0 and dy == 0)

    def gather_start(g):
        mine = ag.at[g, c, chip]

        def send(zz, yy, is_me):
            @pl.when(active(g, zz))
            def _():
                if is_me:
                    pltpu.make_async_copy(own.at[g], mine, ag_recv.at[g, zme]).start()
                else:
                    pltpu.make_async_remote_copy(
                        own.at[g], mine, ag_send.at[g], ag_recv.at[g, zme], at_chip(zz * NY + yy)
                    ).start()

        peers(FAR_FIRST, send)

    def block_at(zz):
        return pl.ds(pl.multiple_of(zz * ZROWS, 8), ZROWS)

    def gather_finish(g):
        def forwarded(zz):
            four = ag.at[g, 1 - c, pl.ds(zz * NY, NY)]
            pltpu.make_async_copy(four, four, fw_recv.at[g, zz]).wait()

        def arrange(zz):
            both = [ag[g, core, pl.ds(zz * NY, NY)] for core in range(NC)]
            wide = [
                jnp.concatenate([x[:, r : r + SLOT].reshape(NY * SLOT, 128) for x in both], axis=0) for r in (0, SLOT)
            ]
            ordered = nn(perm[0], jnp.concatenate(wide, axis=1))
            ends = jnp.concatenate([x[:, 2 * SLOT :].reshape(NY * 8, 128) for x in both], axis=0).astype(F32)
            left = lax.broadcasted_iota(jnp.int32, ends.shape, 1) < 64
            halves = [jnp.where(left, x, 0.0) for x in (ends, pltpu.roll(ends, 64, 1))]
            ordered_ends = nn(perm[1], jnp.concatenate(halves, axis=0).astype(BF16))
            for m in range(3):
                rows = slice(m * ZROWS, (m + 1) * ZROWS)
                nat[m, block_at(zz), 0:256] = ordered[rows]
                nat[m, block_at(zz), 256:PAD] = ordered_ends[rows]

        order = [lax.rem(zme + dz, NZ) for dz in NEAR_FIRST]
        for n, zz in enumerate(order):
            four = ag.at[g, c, pl.ds(zz * NY, NY)]
            pltpu.make_async_copy(four, four, ag_recv.at[g, zz]).wait()
            pltpu.make_async_remote_copy(four, four, fw_send.at[g], fw_recv.at[g, zz], {"tok": mate}).start()
            if n % 2 and n >= 5:
                for zz in order[n - 5 : n - 3]:
                    forwarded(zz)
                for zz in order[n - 5 : n - 3]:
                    arrange(zz)
        far_copy(g).start()
        for zz in order[4:]:
            forwarded(zz)
        for zz in order[4:]:
            arrange(zz)
        for m, ref in enumerate((gt, ut, dt)):
            ref[...] = nat[m, :, 0:HD].astype(BF16)

    def gather_drain(g):
        sends = NY * (LAST_FIRST if g == 0 else NZ - FIRST_SECOND)

        def drain(n):
            some = ag.at[g, 0, pl.ds(0, n)]
            pltpu.make_async_copy(some, some, ag_send.at[g]).wait()

        @pl.when(live[g])
        def _():
            drain(sends - 1)
            every = ag.at[g, 0]
            pltpu.make_async_copy(every, every, fw_send.at[g]).wait()

        @pl.when(jnp.logical_not(live[g]))
        def _():
            drain(sends)

    def grads(g):
        kk, e = k[pl.ds(0, HD)], es[g]
        a = nn(gt[...], kk)
        b = nn(ut[...], kk)
        s = jax.nn.sigmoid(a)
        act = a * s
        r = (act * b).astype(BF16)
        du = tn(dt[...], e)
        da = (du * b * s * (1.0 + a * (1.0 - s))).astype(BF16)
        db = (du * act).astype(BF16)
        nat[0] = nt(da, k[...])
        nat[1] = nt(db, k[...])
        nat[2] = nt(e, jnp.concatenate([r, jnp.zeros((PAD - FH, toks), BF16)], axis=0))

    def reduce_start(g, meanwhile):
        def split(zz):
            part = [nat[m, block_at(zz)] for m in range(3)]
            part.append(jnp.zeros((128 - 3 * ZROWS, PAD), F32))
            block = jnp.concatenate(part, axis=0).astype(BF16)
            slots = nn(perm[2], block[:, 0:256]).astype(BF16)
            ends = nn(perm[3], block[:, 256:PAD])
            ends = (ends[0:64] + pltpu.roll(ends[64:128], 64, 1)).astype(BF16)
            here = pl.ds(zz * NY, NY)
            gs[g, :, here, 0:SLOT] = slots[:, 0:128].reshape(NC, NY, SLOT, 128)
            gs[g, :, here, SLOT : 2 * SLOT] = slots[:, 128:256].reshape(NC, NY, SLOT, 128)
            gs[g, :, here, 2 * SLOT : LINES] = ends.reshape(NC, NY, 8, 128)

        def to_mate(zz):
            here = pl.ds(zz * NY, NY)
            pltpu.make_async_remote_copy(
                gs.at[g, 1 - c, here], cr.at[g, here], cs_send.at[g], cs_recv.at[g, zz], {"tok": mate}
            ).start()

        landing = rr.at[g, chip - z_from[g] * NY]

        def send(zz, yy, is_me):
            p = zz * NY + yy
            if is_me:
                pltpu.make_async_copy(red.at[g, p], landing, rs_recv.at[g]).start()
            else:
                pltpu.make_async_remote_copy(
                    red.at[g, p], landing, rs_send.at[g], rs_recv.at[g], at_chip(p)
                ).start()

        def pass_sum(dz):
            zz = lax.rem(zme + dz, NZ)
            here = pl.ds(zz * NY, NY)
            four = cr.at[g, here]
            pltpu.make_async_copy(four, four, cs_recv.at[g, zz]).wait()
            red[g, here] = (gs[g, c, here].astype(F32) + cr[g, here].astype(F32)).astype(BF16)
            peers((dz,), send)

        for half in (FAR_FIRST[: NZ // 2], FAR_FIRST[NZ // 2 :]):
            for dz in half:
                split(lax.rem(zme + dz, NZ))
            for dz in half:
                to_mate(lax.rem(zme + dz, NZ))
        meanwhile()
        for dz in FAR_FIRST:
            pass_sum(dz)

    def reduce_finish(g):
        every = rr.at[g]
        pltpu.make_async_copy(every, every, rs_recv.at[g]).wait()
        total = jnp.sum(rr[g].astype(F32), axis=0)
        old = state[...]
        fresh = old - total
        old_norm = jnp.sqrt(row_sums(old * old))
        new_norm = jnp.sqrt(row_sums(fresh * fresh) + 1e-06)
        return fresh * spread(old_norm / new_norm)

    def reduce_drain(g):
        @pl.when(live[g])
        def _():
            every = cr.at[g]
            pltpu.make_async_copy(every, every, cs_send.at[g]).wait()
            thirty_one = red.at[g, pl.ds(0, CHIPS - 1)]
            pltpu.make_async_copy(thirty_one, thirty_one, rs_send.at[g]).wait()

    def apply_queries():
        a = nn(gt[...], q[...])
        b = nn(ut[...], q[...])
        hidden = (a * jax.nn.sigmoid(a) * b).astype(BF16)
        return nn(dt[...], hidden)

    def far_copy(n):
        return pltpu.make_async_remote_copy(
            (k.at[pl.ds(0, HD)], v)[n], kv_far.at[n], kv_send.at[n], kv_recv.at[n], at_chip(lax.rem(chip + 1, CHIPS))
        )

    def near_copy(n, src):
        return pltpu.make_async_remote_copy(src, kv_near.at[n], kv_send.at[2 + n], kv_recv.at[2 + n], {"tok": mate})

    def pass_on(n):
        far_copy(n).wait()

        @pl.when(c == 1)
        def _():
            near_copy(n, kv_far.at[n]).start()

    def exchange_squares():
        mixed = y_buf[...]
        sums = jnp.sum(mixed * mixed, axis=0, keepdims=True)
        sq[...] = sums
        sqr[h] = sums
        for n in range(1, HEADS):
            pltpu.make_async_remote_copy(sq, sqr.at[h], sq_send, sq_recv, {"head": lax.rem(h + n, HEADS)}).start()

    gather_start(0)

    @pl.when(c == 0)
    def _():
        for n in range(2):
            near_copy(n, (k.at[pl.ds(0, HD)], v)[n]).start()

    @pl.when(jnp.logical_not(live[0]))
    def _():
        far_copy(0).start()

    @pl.when(live[0])
    def _():
        gather_finish(0)
        grads(0)
        reduce_start(0, lambda: None)
        y_buf[...] = apply_queries()

    pass_on(0)
    middle = reduce_finish(0)
    state[...] = middle
    own[1] = middle.astype(BF16)
    gather_start(1)

    near_copy(0, kv_far.at[0]).wait()
    scale = 1.0 / math.sqrt(HD)
    j = lax.broadcasted_iota(jnp.int32, (toks, toks), 0)
    i = lax.broadcasted_iota(jnp.int32, (toks, toks), 1)
    reach = back[...]
    scores = []
    for ahead, keys in ((2 * toks, kv_far.at[0]), (toks, kv_near.at[0]), (0, k.at[pl.ds(0, HD)])):
        away = i - j + ahead
        seen = (away >= 0) & (away <= reach) & (start + j - ahead >= 0)
        scores.append(jnp.where(seen, tn(keys[...], q[...]) * scale, -jnp.inf))
    top = functools.reduce(jnp.maximum, [jnp.max(s, axis=0, keepdims=True) for s in scores])
    weights = [jnp.exp(s - top) for s in scores]
    total = functools.reduce(jnp.add, [jnp.sum(w, axis=0, keepdims=True) for w in weights])
    for n, w in enumerate(weights):
        probs[n] = (w / total).astype(BF16)

    @pl.when(jnp.logical_not(live[1]))
    def _():
        far_copy(1).start()

    @pl.when(live[1])
    def _():
        gather_finish(1)
        grads(1)

        def outputs():
            y_buf[...] = jnp.where(first, y_buf[...], apply_queries())
            exchange_squares()

        reduce_start(1, outputs)

    @pl.when(jnp.logical_not(live[1]))
    def _():
        exchange_squares()

    pass_on(1)
    near_copy(1, v).wait()
    attn = nn(kv_far[1], probs[0]) + nn(kv_near[1], probs[1]) + nn(v[...], probs[2])
    seven = sqr.at[pl.ds(0, HEADS - 1)]
    pltpu.make_async_copy(seven, seven, sq_recv).wait()
    mean_square = jnp.sum(sqr[...], axis=0) / (HEADS * HD)
    gains = jnp.broadcast_to(gain[...].reshape(1, HD), (8, HD)).T[:, 0:1]
    normed = y_buf[...] / jnp.sqrt(mean_square + 1e-06) * gains
    out[...] = (normed + attn).astype(BF16)
    last = unpack(reduce_finish(1))
    for m, ref in enumerate((g_out, u_out, d_out)):
        ref[...] = last[m * OWN : (m + 1) * OWN].reshape(OWN, 1, HD)
    pltpu.make_async_copy(seven, seven, sq_send).wait()
    for g in range(2):
        gather_drain(g)
        reduce_drain(g)


def write_out(*refs):
    half = len(refs) // 2
    srcs, dsts, sem = refs[:half], refs[half:-1], refs[-1]
    copies = [pltpu.make_async_copy(src, dst, sem.at[n]) for n, (src, dst) in enumerate(zip(srcs, dsts))]
    for copy in copies:
        copy.start()
    for copy in copies:
        copy.wait()


def on_device(queries, keys, values, rates, back, group_end, gate_init, up_init, down_init, gain):
    toks = rates.shape[0]
    perm = order_matrices()
    vmem = pl.BlockSpec(memory_space=pltpu.VMEM)
    hbm = pl.BlockSpec(memory_space=pltpu.HBM)
    slots = (CHIPS, LINES, 128)
    dma = pltpu.SemaphoreType.DMA
    shares = [w.transpose(2, 0, 1) for w in (gate_init, up_init, down_init)]
    share = jax.ShapeDtypeStruct((OWN, 1, HD), F32)
    shapes = (jax.ShapeDtypeStruct((HD, toks), BF16), share, share, share)
    results = pl.pallas_call(
        kernel,
        out_shape=shapes,
        in_specs=[pl.BlockSpec(memory_space=pltpu.SMEM)] + [hbm] * 10,
        out_specs=(vmem,) * 4,
        scratch_shapes=[
            pltpu.VMEM((HD, toks), BF16),
            pltpu.VMEM((PAD, toks), BF16),
            pltpu.VMEM((HD, toks), BF16),
            pltpu.VMEM((1, toks), F32),
            pltpu.VMEM((1, toks), jnp.int32),
            pltpu.VMEM((SLOT, 1, HD), F32),
            pltpu.VMEM((HD,), F32),
            pltpu.VMEM((4, 128, 128), BF16),
            pltpu.VMEM((2, LINES, 128), BF16),
            pltpu.VMEM((2, NC, *slots), BF16),
            pltpu.VMEM((2, NC, *slots), BF16),
            pltpu.VMEM((2, *slots), BF16),
            pltpu.VMEM((2, *slots), BF16),
            pltpu.VMEM((2, LAST_FIRST * NY, LINES, 128), BF16),
            pltpu.VMEM((2, HD, toks), BF16),
            pltpu.VMEM((2, HD, toks), BF16),
            pltpu.VMEM((1, toks), F32),
            pltpu.VMEM((HEADS, 1, toks), F32),
            pltpu.VMEM((3, HD, PAD), F32),
            pltpu.VMEM((FH, HD), BF16),
            pltpu.VMEM((FH, HD), BF16),
            pltpu.VMEM((HD, FH), BF16),
            pltpu.VMEM((2, HD, toks), BF16),
            pltpu.VMEM((HD, toks), F32),
            pltpu.VMEM((3, toks, toks), BF16),
            pltpu.VMEM((LINES, 128), F32),
            dma((10,)),
            dma((2,)), dma((2, NZ)),
            dma((2,)), dma((2, NZ)),
            dma((2,)), dma((2, NZ)),
            dma((2,)), dma((2,)),
            dma((4,)), dma((4,)),
            dma, dma,
        ],
        compiler_params=pltpu.CompilerParams(
            collective_id=0, has_side_effects=True, vmem_limit_bytes=48 * 1024 * 1024
        ),
        name="layer",
    )(
        group_end,
        *(
            pltpu.with_memory_space_constraint(array, pltpu.HBM)
            for array in (
                queries.T, keys.T, values.T, rates.T, back.reshape(1, toks), *shares, gain,
                jnp.asarray(perm, BF16),
            )
        ),
    )
    out, *finals = pl.pallas_call(
        write_out,
        out_shape=shapes,
        in_specs=[vmem] * 4,
        out_specs=(hbm,) * 4,
        scratch_shapes=[dma((4,))],
        compiler_params=pltpu.CompilerParams(vmem_limit_bytes=1024 * 1024),
        name="write_out",
    )(*results)
    return (out.T, *(w.transpose(1, 2, 0) for w in finals))


def solution(mesh):
    placed = (
        P("tok", "head"),
        P("tok", "head"),
        P("tok", "head"),
        P("tok", "head"),
        P("tok"),
        P(),
        P("head", None, "tok"),
        P("head", None, "tok"),
        P("head", None, "tok"),
        P("head"),
    )
    return jax.shard_map(
        on_device,
        mesh=mesh,
        in_specs=placed,
        out_specs=(
            P("tok", "head"),
            P("head", None, "tok"),
            P("head", None, "tok"),
            P("head", None, "tok"),
        ),
        check_vma=False,
    )
```

```python
import functools
import math

import jax
import jax.numpy as jnp
import numpy as np
from jax import lax
from jax.experimental import pallas as pl
from jax.experimental.pallas import tpu as pltpu
from jax.sharding import PartitionSpec as P

HEADS = 8
HD = 320
FH = 320
WINDOW = 512
NZ, NY, NC = 8, 4, 2
CHIPS = NZ * NY
OWN = 5
SLOT = 16
LINES = 40
PAD = 384
ZROWS = NY * NC * OWN
LAST_FIRST = 12288 * NZ // 16384
FIRST_SECOND = 4096 * NZ // 16384
FAR_FIRST = (4, 3, 5, 2, 6, 1, 7, 0)
NEAR_FIRST = (0, 1, 7, 2, 6, 3, 5, 4)
F32, BF16 = jnp.float32, jnp.bfloat16


def nn(a, b):
    return lax.dot_general(a, b, (((1,), (0,)), ((), ())), preferred_element_type=F32)


def nt(a, b):
    return lax.dot_general(a, b, (((1,), (1,)), ((), ())), preferred_element_type=F32)


def tn(a, b):
    return lax.dot_general(a, b, (((0,), (0,)), ((), ())), preferred_element_type=F32)


def order_matrices():
    perm = np.zeros((2, 128, 128), np.float32)
    for m in range(3):
        for y in range(NY):
            for c in range(NC):
                for j in range(OWN):
                    row = m * OWN + j
                    natural = m * ZROWS + (y * NC + c) * OWN + j
                    perm[0, natural, c * 64 + y * SLOT + row] = 1.0
                    perm[1, natural, row // 8 * 64 + c * 32 + y * 8 + row % 8] = 1.0
    return np.concatenate([perm, perm.transpose(0, 2, 1)])


def pack(rows):
    last = rows[:, 256:384]
    return jnp.concatenate([rows[:, 0:128], rows[:, 128:256], last[0:8] + pltpu.roll(last[8:16], 64, 1)], axis=0)


def unpack(packed):
    last = jnp.concatenate([packed[32:40], pltpu.roll(packed[32:40], 64, 1)], axis=0)
    return jnp.concatenate([packed[0:16], packed[16:32], last[:, 0:64]], axis=1)


def row_sums(packed):
    left = lax.broadcasted_iota(jnp.int32, (8, 128), 1) < 64
    last = packed[32:40]
    ends = [jnp.where(left, last, 0.0), jnp.where(left, 0.0, last)]
    whole = packed[0:16] + packed[16:32] + jnp.concatenate(ends, axis=0)
    return jnp.sum(whole, axis=1, keepdims=True)


def spread(factor):
    wide = jnp.broadcast_to(factor, (SLOT, 128))
    left = lax.broadcasted_iota(jnp.int32, (8, 128), 1) < 64
    return jnp.concatenate([wide, wide, jnp.where(left, wide[0:8], wide[8:16])], axis=0)


def kernel(
    ge, q_hbm, k_hbm, v_hbm, rates_hbm, back_hbm, g_hbm, u_hbm, d_hbm, gain_hbm, perm_hbm,
    out, g_out, u_out, d_out,
    q, k, v, rates, back, rows0, gain, perm,
    own, ag, gs, cr, red, rr, kv_far, kv_near, sq, sqr, nat, gt, ut, dt, es, y_buf, probs, state,
    in_sem, ag_send, ag_recv, fw_send, fw_recv, cs_send, cs_recv, rs_send, rs_recv, kv_send, kv_recv, sq_send, sq_recv, go,
):
    toks = q.shape[1]
    t = lax.axis_index("tok")
    h = lax.axis_index("head")
    c = lax.rem(t, 2)
    chip = lax.div(t, 2)
    zme = lax.div(chip, NY)
    yme = lax.rem(chip, NY)
    mate = t + 1 - 2 * c

    loads = [
        pltpu.make_async_copy(src, dst, in_sem.at[n])
        for n, (src, dst) in enumerate(
            (
                (g_hbm, rows0.at[pl.ds(0, OWN)]),
                (u_hbm, rows0.at[pl.ds(OWN, OWN)]),
                (d_hbm, rows0.at[pl.ds(2 * OWN, OWN)]),
                (k_hbm, k.at[pl.ds(0, HD)]),
                (v_hbm, v),
                (q_hbm, q),
                (rates_hbm, rates),
                (back_hbm, back),
                (gain_hbm, gain),
                (perm_hbm, perm),
            )
        )
    ]
    def at_chip(p):
        return {"tok": 2 * p + c}

    barrier = pltpu.get_barrier_semaphore()

    def greet(i, _):
        pl.semaphore_signal(barrier, inc=1, device_id=at_chip(lax.rem(chip + i, CHIPS)))
        return 0

    lax.fori_loop(1, CHIPS, greet, 0)
    pl.semaphore_signal(barrier, inc=1, device_id={"tok": mate})

    def greet_head(i, _):
        pl.semaphore_signal(barrier, inc=1, device_id={"head": lax.rem(h + i, HEADS)})
        return 0

    lax.fori_loop(1, HEADS, greet_head, 0)
    for load in loads:
        load.start()

    rows0[pl.ds(3 * OWN, 1)] = jnp.zeros((1, 1, HD), F32)
    for load in loads:
        load.wait()
    share = rows0[...].reshape(SLOT, HD)
    state[...] = pack(jnp.concatenate([share, jnp.zeros((SLOT, PAD - HD), F32)], axis=1))
    own[0] = state[...].astype(BF16)
    k[pl.ds(HD, PAD - HD)] = jnp.zeros((PAD - HD, toks), BF16)
    start = t * toks
    first = start + lax.broadcasted_iota(jnp.int32, (1, toks), 1) < ge[0]
    rate = rates[...]
    vf = v[...].astype(F32)
    es[0] = (-jnp.where(first, rate, 0.0) * vf).astype(BF16)
    es[1] = (-jnp.where(first, 0.0, rate) * vf).astype(BF16)
    y_buf[...] = jnp.zeros_like(y_buf)

    pl.semaphore_wait(barrier, (CHIPS - 1) + 1 + (HEADS - 1))

    def active(g, z):
        return z < LAST_FIRST if g == 0 else z >= FIRST_SECOND

    live = [active(g, zme) for g in range(2)]
    z_from = (0, FIRST_SECOND)

    def peers(dzs, body):
        for dz in dzs:
            zz = lax.rem(zme + dz, NZ)
            for dy in range(NY):
                yy = lax.rem(yme + dy, NY)
                body(zz, yy, dz == 0 and dy == 0)

    def gather_start(g):
        mine = ag.at[g, c, chip]

        def send(zz, yy, is_me):
            @pl.when(active(g, zz))
            def _():
                if is_me:
                    pltpu.make_async_copy(own.at[g], mine, ag_recv.at[g, zme]).start()
                else:
                    pltpu.make_async_remote_copy(
                        own.at[g], mine, ag_send.at[g], ag_recv.at[g, zme], at_chip(zz * NY + yy)
                    ).start()

        peers(FAR_FIRST, send)

    def block_at(zz):
        return pl.ds(pl.multiple_of(zz * ZROWS, 8), ZROWS)

    def gather_finish(g):
        def forwarded(zz):
            four = ag.at[g, 1 - c, pl.ds(zz * NY, NY)]
            pltpu.make_async_copy(four, four, fw_recv.at[g, zz]).wait()

        def arrange(zz):
            both = [ag[g, core, pl.ds(zz * NY, NY)] for core in range(NC)]
            wide = [
                jnp.concatenate([x[:, r : r + SLOT].reshape(NY * SLOT, 128) for x in both], axis=0) for r in (0, SLOT)
            ]
            ordered = nn(perm[0], jnp.concatenate(wide, axis=1))
            ends = jnp.concatenate([x[:, 2 * SLOT :].reshape(NY * 8, 128) for x in both], axis=0).astype(F32)
            left = lax.broadcasted_iota(jnp.int32, ends.shape, 1) < 64
            halves = [jnp.where(left, x, 0.0) for x in (ends, pltpu.roll(ends, 64, 1))]
            ordered_ends = nn(perm[1], jnp.concatenate(halves, axis=0).astype(BF16))
            for m in range(3):
                rows = slice(m * ZROWS, (m + 1) * ZROWS)
                nat[m, block_at(zz), 0:256] = ordered[rows]
                nat[m, block_at(zz), 256:PAD] = ordered_ends[rows]

        order = [lax.rem(zme + dz, NZ) for dz in NEAR_FIRST]
        for n, zz in enumerate(order):
            four = ag.at[g, c, pl.ds(zz * NY, NY)]
            pltpu.make_async_copy(four, four, ag_recv.at[g, zz]).wait()
            pltpu.make_async_remote_copy(four, four, fw_send.at[g], fw_recv.at[g, zz], {"tok": mate}).start()
            if n % 2 and n >= 5:
                for zz in order[n - 5 : n - 3]:
                    forwarded(zz)
                for zz in order[n - 5 : n - 3]:
                    arrange(zz)
        far_copy(g).start()
        tell, away = ((2, 3), 4) if g == 0 else ((4, 5), -4)

        @pl.when((zme == tell[0]) | (zme == tell[1]))
        def _():
            pl.semaphore_signal(go, inc=1, device_id={"tok": t + away * NY * NC})

        for zz in order[4:]:
            forwarded(zz)
        for zz in order[4:]:
            arrange(zz)
        for m, ref in enumerate((gt, ut, dt)):
            ref[...] = nat[m, :, 0:HD].astype(BF16)

    def gather_drain(g):
        sends = NY * (LAST_FIRST if g == 0 else NZ - FIRST_SECOND)

        def drain(n):
            some = ag.at[g, 0, pl.ds(0, n)]
            pltpu.make_async_copy(some, some, ag_send.at[g]).wait()

        @pl.when(live[g])
        def _():
            drain(sends - 1)
            every = ag.at[g, 0]
            pltpu.make_async_copy(every, every, fw_send.at[g]).wait()

        @pl.when(jnp.logical_not(live[g]))
        def _():
            drain(sends)

    def grads(g):
        kk, e = k[pl.ds(0, HD)], es[g]
        a = nn(gt[...], kk)
        b = nn(ut[...], kk)
        s = jax.nn.sigmoid(a)
        act = a * s
        r = (act * b).astype(BF16)
        du = tn(dt[...], e)
        da = (du * b * s * (1.0 + a * (1.0 - s))).astype(BF16)
        db = (du * act).astype(BF16)
        nat[0] = nt(da, k[...])
        nat[1] = nt(db, k[...])
        nat[2] = nt(e, jnp.concatenate([r, jnp.zeros((PAD - FH, toks), BF16)], axis=0))

    def reduce_start(g, meanwhile):
        def split(zz):
            part = [nat[m, block_at(zz)] for m in range(3)]
            part.append(jnp.zeros((128 - 3 * ZROWS, PAD), F32))
            block = jnp.concatenate(part, axis=0).astype(BF16)
            slots = nn(perm[2], block[:, 0:256]).astype(BF16)
            ends = nn(perm[3], block[:, 256:PAD])
            ends = (ends[0:64] + pltpu.roll(ends[64:128], 64, 1)).astype(BF16)
            here = pl.ds(zz * NY, NY)
            gs[g, :, here, 0:SLOT] = slots[:, 0:128].reshape(NC, NY, SLOT, 128)
            gs[g, :, here, SLOT : 2 * SLOT] = slots[:, 128:256].reshape(NC, NY, SLOT, 128)
            gs[g, :, here, 2 * SLOT : LINES] = ends.reshape(NC, NY, 8, 128)

        def to_mate(zz):
            here = pl.ds(zz * NY, NY)
            pltpu.make_async_remote_copy(
                gs.at[g, 1 - c, here], cr.at[g, here], cs_send.at[g], cs_recv.at[g, zz], {"tok": mate}
            ).start()

        landing = rr.at[g, chip - z_from[g] * NY]

        def send(zz, yy, is_me):
            p = zz * NY + yy
            if is_me:
                pltpu.make_async_copy(red.at[g, p], landing, rs_recv.at[g]).start()
            else:
                pltpu.make_async_remote_copy(
                    red.at[g, p], landing, rs_send.at[g], rs_recv.at[g], at_chip(p)
                ).start()

        def pass_sum(dz):
            zz = lax.rem(zme + dz, NZ)
            here = pl.ds(zz * NY, NY)
            four = cr.at[g, here]
            pltpu.make_async_copy(four, four, cs_recv.at[g, zz]).wait()
            red[g, here] = (gs[g, c, here].astype(F32) + cr[g, here].astype(F32)).astype(BF16)
            peers((dz,), send)

        for half in (FAR_FIRST[: NZ // 2], FAR_FIRST[NZ // 2 :]):
            for dz in half:
                split(lax.rem(zme + dz, NZ))
            for dz in half:
                to_mate(lax.rem(zme + dz, NZ))
        meanwhile()
        for dz in FAR_FIRST:
            pass_sum(dz)

    def reduce_finish(g):
        every = rr.at[g]
        pltpu.make_async_copy(every, every, rs_recv.at[g]).wait()
        total = jnp.sum(rr[g].astype(F32), axis=0)
        old = state[...]
        fresh = old - total
        old_norm = jnp.sqrt(row_sums(old * old))
        new_norm = jnp.sqrt(row_sums(fresh * fresh) + 1e-06)
        return fresh * spread(old_norm / new_norm)

    def reduce_drain(g):
        @pl.when(live[g])
        def _():
            every = cr.at[g]
            pltpu.make_async_copy(every, every, cs_send.at[g]).wait()
            thirty_one = red.at[g, pl.ds(0, CHIPS - 1)]
            pltpu.make_async_copy(thirty_one, thirty_one, rs_send.at[g]).wait()

    def apply_queries():
        a = nn(gt[...], q[...])
        b = nn(ut[...], q[...])
        hidden = (a * jax.nn.sigmoid(a) * b).astype(BF16)
        return nn(dt[...], hidden)

    def far_copy(n):
        return pltpu.make_async_remote_copy(
            (k.at[pl.ds(0, HD)], v)[n], kv_far.at[n], kv_send.at[n], kv_recv.at[n], at_chip(lax.rem(chip + 1, CHIPS))
        )

    def near_copy(n, src):
        return pltpu.make_async_remote_copy(src, kv_near.at[n], kv_send.at[2 + n], kv_recv.at[2 + n], {"tok": mate})

    def pass_on(n):
        far_copy(n).wait()

        @pl.when(c == 1)
        def _():
            near_copy(n, kv_far.at[n]).start()

    def exchange_squares():
        mixed = y_buf[...]
        sums = jnp.sum(mixed * mixed, axis=0, keepdims=True)
        sq[...] = sums
        sqr[h] = sums
        for n in range(1, HEADS):
            pltpu.make_async_remote_copy(sq, sqr.at[h], sq_send, sq_recv, {"head": lax.rem(h + n, HEADS)}).start()

    gather_start(0)

    @pl.when(c == 0)
    def _():
        for n in range(2):
            near_copy(n, (k.at[pl.ds(0, HD)], v)[n]).start()

    @pl.when(live[0])
    def _():
        gather_finish(0)
        grads(0)
        reduce_start(0, lambda: None)
        y_buf[...] = apply_queries()

    @pl.when(jnp.logical_not(live[0]))
    def _():
        pl.semaphore_wait(go, 1)
        far_copy(0).start()

    pass_on(0)
    middle = reduce_finish(0)
    state[...] = middle
    own[1] = middle.astype(BF16)
    gather_start(1)

    near_copy(0, kv_far.at[0]).wait()
    scale = 1.0 / math.sqrt(HD)
    j = lax.broadcasted_iota(jnp.int32, (toks, toks), 0)
    i = lax.broadcasted_iota(jnp.int32, (toks, toks), 1)
    reach = back[...]
    scores = []
    for ahead, keys in ((2 * toks, kv_far.at[0]), (toks, kv_near.at[0]), (0, k.at[pl.ds(0, HD)])):
        away = i - j + ahead
        seen = (away >= 0) & (away <= reach) & (start + j - ahead >= 0)
        scores.append(jnp.where(seen, tn(keys[...], q[...]) * scale, -jnp.inf))
    top = functools.reduce(jnp.maximum, [jnp.max(s, axis=0, keepdims=True) for s in scores])
    weights = [jnp.exp(s - top) for s in scores]
    total = functools.reduce(jnp.add, [jnp.sum(w, axis=0, keepdims=True) for w in weights])
    for n, w in enumerate(weights):
        probs[n] = (w / total).astype(BF16)

    @pl.when(jnp.logical_not(live[1]))
    def _():
        pl.semaphore_wait(go, 1)
        far_copy(1).start()

    @pl.when(live[1])
    def _():
        gather_finish(1)
        grads(1)

        def outputs():
            y_buf[...] = jnp.where(first, y_buf[...], apply_queries())
            exchange_squares()

        reduce_start(1, outputs)

    @pl.when(jnp.logical_not(live[1]))
    def _():
        exchange_squares()

    pass_on(1)
    near_copy(1, v).wait()
    attn = nn(kv_far[1], probs[0]) + nn(kv_near[1], probs[1]) + nn(v[...], probs[2])
    seven = sqr.at[pl.ds(0, HEADS - 1)]
    pltpu.make_async_copy(seven, seven, sq_recv).wait()
    mean_square = jnp.sum(sqr[...], axis=0) / (HEADS * HD)
    gains = jnp.broadcast_to(gain[...].reshape(1, HD), (8, HD)).T[:, 0:1]
    normed = y_buf[...] / jnp.sqrt(mean_square + 1e-06) * gains
    out[...] = (normed + attn).astype(BF16)
    last = unpack(reduce_finish(1))
    for m, ref in enumerate((g_out, u_out, d_out)):
        ref[...] = last[m * OWN : (m + 1) * OWN].reshape(OWN, 1, HD)
    pltpu.make_async_copy(seven, seven, sq_send).wait()
    for g in range(2):
        gather_drain(g)
        reduce_drain(g)


def write_out(*refs):
    half = len(refs) // 2
    srcs, dsts, sem = refs[:half], refs[half:-1], refs[-1]
    copies = [pltpu.make_async_copy(src, dst, sem.at[n]) for n, (src, dst) in enumerate(zip(srcs, dsts))]
    for copy in copies:
        copy.start()
    for copy in copies:
        copy.wait()


def on_device(queries, keys, values, rates, back, group_end, gate_init, up_init, down_init, gain):
    toks = rates.shape[0]
    perm = order_matrices()
    vmem = pl.BlockSpec(memory_space=pltpu.VMEM)
    hbm = pl.BlockSpec(memory_space=pltpu.HBM)
    slots = (CHIPS, LINES, 128)
    dma = pltpu.SemaphoreType.DMA
    shares = [w.transpose(2, 0, 1) for w in (gate_init, up_init, down_init)]
    share = jax.ShapeDtypeStruct((OWN, 1, HD), F32)
    shapes = (jax.ShapeDtypeStruct((HD, toks), BF16), share, share, share)
    results = pl.pallas_call(
        kernel,
        out_shape=shapes,
        in_specs=[pl.BlockSpec(memory_space=pltpu.SMEM)] + [hbm] * 10,
        out_specs=(vmem,) * 4,
        scratch_shapes=[
            pltpu.VMEM((HD, toks), BF16),
            pltpu.VMEM((PAD, toks), BF16),
            pltpu.VMEM((HD, toks), BF16),
            pltpu.VMEM((1, toks), F32),
            pltpu.VMEM((1, toks), jnp.int32),
            pltpu.VMEM((SLOT, 1, HD), F32),
            pltpu.VMEM((HD,), F32),
            pltpu.VMEM((4, 128, 128), BF16),
            pltpu.VMEM((2, LINES, 128), BF16),
            pltpu.VMEM((2, NC, *slots), BF16),
            pltpu.VMEM((2, NC, *slots), BF16),
            pltpu.VMEM((2, *slots), BF16),
            pltpu.VMEM((2, *slots), BF16),
            pltpu.VMEM((2, LAST_FIRST * NY, LINES, 128), BF16),
            pltpu.VMEM((2, HD, toks), BF16),
            pltpu.VMEM((2, HD, toks), BF16),
            pltpu.VMEM((1, toks), F32),
            pltpu.VMEM((HEADS, 1, toks), F32),
            pltpu.VMEM((3, HD, PAD), F32),
            pltpu.VMEM((FH, HD), BF16),
            pltpu.VMEM((FH, HD), BF16),
            pltpu.VMEM((HD, FH), BF16),
            pltpu.VMEM((2, HD, toks), BF16),
            pltpu.VMEM((HD, toks), F32),
            pltpu.VMEM((3, toks, toks), BF16),
            pltpu.VMEM((LINES, 128), F32),
            dma((10,)),
            dma((2,)), dma((2, NZ)),
            dma((2,)), dma((2, NZ)),
            dma((2,)), dma((2, NZ)),
            dma((2,)), dma((2,)),
            dma((4,)), dma((4,)),
            dma, dma,
            pltpu.SemaphoreType.REGULAR,
        ],
        compiler_params=pltpu.CompilerParams(
            collective_id=0, has_side_effects=True, vmem_limit_bytes=48 * 1024 * 1024
        ),
        name="layer",
    )(
        group_end,
        *(
            pltpu.with_memory_space_constraint(array, pltpu.HBM)
            for array in (
                queries.T, keys.T, values.T, rates.T, back.reshape(1, toks), *shares, gain,
                jnp.asarray(perm, BF16),
            )
        ),
    )
    out, *finals = pl.pallas_call(
        write_out,
        out_shape=shapes,
        in_specs=[vmem] * 4,
        out_specs=(hbm,) * 4,
        scratch_shapes=[dma((4,))],
        compiler_params=pltpu.CompilerParams(vmem_limit_bytes=1024 * 1024),
        name="write_out",
    )(*results)
    return (out.T, *(w.transpose(1, 2, 0) for w in finals))


def solution(mesh):
    placed = (
        P("tok", "head"),
        P("tok", "head"),
        P("tok", "head"),
        P("tok", "head"),
        P("tok"),
        P(),
        P("head", None, "tok"),
        P("head", None, "tok"),
        P("head", None, "tok"),
        P("head"),
    )
    return jax.shard_map(
        on_device,
        mesh=mesh,
        in_specs=placed,
        out_specs=(
            P("tok", "head"),
            P("head", None, "tok"),
            P("head", None, "tok"),
            P("head", None, "tok"),
        ),
        check_vma=False,
    )
```

```python
import functools
import math

import jax
import jax.numpy as jnp
import numpy as np
from jax import lax
from jax.experimental import pallas as pl
from jax.experimental.pallas import tpu as pltpu
from jax.sharding import PartitionSpec as P

HEADS = 8
HD = 320
FH = 320
WINDOW = 512
NZ, NY, NC = 8, 4, 2
CHIPS = NZ * NY
OWN = 5
SLOT = 16
LINES = 40
PAD = 384
ZROWS = NY * NC * OWN
LAST_FIRST = 12288 * NZ // 16384
FIRST_SECOND = 4096 * NZ // 16384
FAR_FIRST = (4, 3, 5, 2, 6, 1, 7, 0)
NEAR_FIRST = (6, 2, 0, 1, 7, 5, 3, 4)
F32, BF16 = jnp.float32, jnp.bfloat16


def nn(a, b):
    return lax.dot_general(a, b, (((1,), (0,)), ((), ())), preferred_element_type=F32)


def nt(a, b):
    return lax.dot_general(a, b, (((1,), (1,)), ((), ())), preferred_element_type=F32)


def tn(a, b):
    return lax.dot_general(a, b, (((0,), (0,)), ((), ())), preferred_element_type=F32)


def order_matrices():
    perm = np.zeros((2, 128, 128), np.float32)
    for m in range(3):
        for y in range(NY):
            for c in range(NC):
                for j in range(OWN):
                    row = m * OWN + j
                    natural = m * ZROWS + (y * NC + c) * OWN + j
                    perm[0, natural, c * 64 + y * SLOT + row] = 1.0
                    perm[1, natural, row // 8 * 64 + c * 32 + y * 8 + row % 8] = 1.0
    return np.concatenate([perm, perm.transpose(0, 2, 1)])


def pack(rows):
    last = rows[:, 256:384]
    return jnp.concatenate([rows[:, 0:128], rows[:, 128:256], last[0:8] + pltpu.roll(last[8:16], 64, 1)], axis=0)


def unpack(packed):
    last = jnp.concatenate([packed[32:40], pltpu.roll(packed[32:40], 64, 1)], axis=0)
    return jnp.concatenate([packed[0:16], packed[16:32], last[:, 0:64]], axis=1)


def row_sums(packed):
    left = lax.broadcasted_iota(jnp.int32, (8, 128), 1) < 64
    last = packed[32:40]
    ends = [jnp.where(left, last, 0.0), jnp.where(left, 0.0, last)]
    whole = packed[0:16] + packed[16:32] + jnp.concatenate(ends, axis=0)
    return jnp.sum(whole, axis=1, keepdims=True)


def spread(factor):
    wide = jnp.broadcast_to(factor, (SLOT, 128))
    left = lax.broadcasted_iota(jnp.int32, (8, 128), 1) < 64
    return jnp.concatenate([wide, wide, jnp.where(left, wide[0:8], wide[8:16])], axis=0)


def kernel(
    ge, q_hbm, k_hbm, v_hbm, rates_hbm, back_hbm, g_hbm, u_hbm, d_hbm, gain_hbm, perm_hbm,
    out, g_out, u_out, d_out,
    q, k, v, rates, back, rows0, gain, perm,
    own, ag, gs, cr, red, rr, kv_far, kv_near, sq, sqr, nat, gt, ut, dt, es, y_buf, probs, state,
    in_sem, ag_send, ag_recv, fw_send, fw_recv, cs_send, cs_recv, rs_send, rs_recv, kv_send, kv_recv, sq_send, sq_recv, go,
):
    toks = q.shape[1]
    t = lax.axis_index("tok")
    h = lax.axis_index("head")
    c = lax.rem(t, 2)
    chip = lax.div(t, 2)
    zme = lax.div(chip, NY)
    yme = lax.rem(chip, NY)
    mate = t + 1 - 2 * c

    loads = [
        pltpu.make_async_copy(src, dst, in_sem.at[n])
        for n, (src, dst) in enumerate(
            (
                (g_hbm, rows0.at[pl.ds(0, OWN)]),
                (u_hbm, rows0.at[pl.ds(OWN, OWN)]),
                (d_hbm, rows0.at[pl.ds(2 * OWN, OWN)]),
                (k_hbm, k.at[pl.ds(0, HD)]),
                (v_hbm, v),
                (q_hbm, q),
                (rates_hbm, rates),
                (back_hbm, back),
                (gain_hbm, gain),
                (perm_hbm, perm),
            )
        )
    ]
    def at_chip(p):
        return {"tok": 2 * p + c}

    barrier = pltpu.get_barrier_semaphore()

    for dz in FAR_FIRST:
        zz = lax.rem(zme + dz, NZ)
        for dy in range(NY):
            if dz or dy:
                pl.semaphore_signal(barrier, inc=1, device_id=at_chip(zz * NY + lax.rem(yme + dy, NY)))
    for n in range(1, HEADS):
        pl.semaphore_signal(barrier, inc=1, device_id={"head": lax.rem(h + n, HEADS)})
    pl.semaphore_signal(barrier, inc=1, device_id={"tok": mate})
    for load in loads:
        load.start()

    rows0[pl.ds(3 * OWN, 1)] = jnp.zeros((1, 1, HD), F32)
    for load in loads:
        load.wait()
    share = rows0[...].reshape(SLOT, HD)
    state[...] = pack(jnp.concatenate([share, jnp.zeros((SLOT, PAD - HD), F32)], axis=1))
    own[0] = state[...].astype(BF16)
    k[pl.ds(HD, PAD - HD)] = jnp.zeros((PAD - HD, toks), BF16)
    start = t * toks
    first = start + lax.broadcasted_iota(jnp.int32, (1, toks), 1) < ge[0]
    rate = rates[...]
    vf = v[...].astype(F32)
    es[0] = (-jnp.where(first, rate, 0.0) * vf).astype(BF16)
    es[1] = (-jnp.where(first, 0.0, rate) * vf).astype(BF16)
    y_buf[...] = jnp.zeros_like(y_buf)

    pl.semaphore_wait(barrier, (CHIPS - 1) + 1 + (HEADS - 1))

    def active(g, z):
        return z < LAST_FIRST if g == 0 else z >= FIRST_SECOND

    live = [active(g, zme) for g in range(2)]
    z_from = (0, FIRST_SECOND)

    def peers(dzs, body):
        for dz in dzs:
            zz = lax.rem(zme + dz, NZ)
            for dy in range(NY):
                yy = lax.rem(yme + dy, NY)
                body(zz, yy, dz == 0 and dy == 0)

    def gather_start(g):
        mine = ag.at[g, c, chip]

        def send(zz, yy, is_me):
            if is_me:
                pltpu.make_async_copy(own.at[g], mine, ag_recv.at[g, zme]).start()
            else:
                pltpu.make_async_remote_copy(
                    own.at[g], mine, ag_send.at[g], ag_recv.at[g, zme], at_chip(zz * NY + yy)
                ).start()

        peers((2, 6), send)
        for dz in (1, 7, 0):

            @pl.when(active(g, lax.rem(zme + dz, NZ)))
            def _():
                peers((dz,), send)

    def arrived(g, zz):
        four = ag.at[g, c, pl.ds(zz * NY, NY)]
        pltpu.make_async_copy(four, four, ag_recv.at[g, zz]).wait()

    def relay(g, dz):
        zz = lax.rem(zme + dz, NZ)
        half = 0 if dz == 6 else NY // 2
        for more, begin, size in ((1, 0, NY), (2, half, NY // 2)):
            to = lax.rem(zme + (more if dz == 6 else NZ - more), NZ)

            @pl.when(active(g, to))
            def _():
                some = ag.at[g, c, pl.ds(zz * NY + begin, size)]
                pltpu.make_async_remote_copy(
                    some, some, ag_send.at[g], ag_recv.at[g, zz], at_chip(to * NY + yme)
                ).start()

    def relay_only(g):
        for dz in (2, 6):
            arrived(g, lax.rem(zme + dz, NZ))
            relay(g, dz)

    def block_at(zz):
        return pl.ds(pl.multiple_of(zz * ZROWS, 8), ZROWS)

    def gather_finish(g):
        def forwarded(zz):
            four = ag.at[g, 1 - c, pl.ds(zz * NY, NY)]
            pltpu.make_async_copy(four, four, fw_recv.at[g, zz]).wait()

        def arrange(zz):
            both = [ag[g, core, pl.ds(zz * NY, NY)] for core in range(NC)]
            wide = [
                jnp.concatenate([x[:, r : r + SLOT].reshape(NY * SLOT, 128) for x in both], axis=0) for r in (0, SLOT)
            ]
            ordered = nn(perm[0], jnp.concatenate(wide, axis=1))
            ends = jnp.concatenate([x[:, 2 * SLOT :].reshape(NY * 8, 128) for x in both], axis=0).astype(F32)
            left = lax.broadcasted_iota(jnp.int32, ends.shape, 1) < 64
            halves = [jnp.where(left, x, 0.0) for x in (ends, pltpu.roll(ends, 64, 1))]
            ordered_ends = nn(perm[1], jnp.concatenate(halves, axis=0).astype(BF16))
            for m in range(3):
                rows = slice(m * ZROWS, (m + 1) * ZROWS)
                nat[m, block_at(zz), 0:256] = ordered[rows]
                nat[m, block_at(zz), 256:PAD] = ordered_ends[rows]

        order = [lax.rem(zme + dz, NZ) for dz in NEAR_FIRST]
        for n, zz in enumerate(order):
            four = ag.at[g, c, pl.ds(zz * NY, NY)]
            arrived(g, zz)
            if NEAR_FIRST[n] in (2, 6):
                relay(g, NEAR_FIRST[n])
            pltpu.make_async_remote_copy(four, four, fw_send.at[g], fw_recv.at[g, zz], {"tok": mate}).start()
            if n % 2 and n >= 5:
                for zz in order[n - 5 : n - 3]:
                    forwarded(zz)
                for zz in order[n - 5 : n - 3]:
                    arrange(zz)
        far_copy(g).start()
        tell, away = ((2, 3), 4) if g == 0 else ((4, 5), -4)

        @pl.when((zme == tell[0]) | (zme == tell[1]))
        def _():
            pl.semaphore_signal(go, inc=1, device_id={"tok": t + away * NY * NC})

        for pair in (order[4:6], order[6:8]):
            for zz in pair:
                forwarded(zz)
            for zz in pair:
                arrange(zz)
        for m, ref in enumerate((gt, ut, dt)):
            ref[...] = nat[m, :, 0:HD].astype(BF16)

    def gather_drain(g):
        taking = [z < LAST_FIRST if g == 0 else z >= FIRST_SECOND for z in range(NZ)]
        weights = ((1, 2 * NY), (7, 2 * NY), (0, NY - 1), (2, NY // 2), (6, NY // 2))
        sent = [2 * NY + sum(n for dz, n in weights if taking[(z + dz) % NZ]) for z in range(NZ)]
        for n in sorted(set(sent)):
            same = functools.reduce(jnp.logical_or, [zme == z for z in range(NZ) if sent[z] == n])

            @pl.when(same)
            def _():
                some = ag.at[g, 0, pl.ds(0, n)]
                pltpu.make_async_copy(some, some, ag_send.at[g]).wait()

        @pl.when(live[g])
        def _():
            every = ag.at[g, 0]
            pltpu.make_async_copy(every, every, fw_send.at[g]).wait()

    def grads(g):
        kk, e = k[pl.ds(0, HD)], es[g]
        a = nn(gt[...], kk)
        b = nn(ut[...], kk)
        s = jax.nn.sigmoid(a)
        act = a * s
        r = (act * b).astype(BF16)
        du = tn(dt[...], e)
        da = (du * b * s * (1.0 + a * (1.0 - s))).astype(BF16)
        db = (du * act).astype(BF16)
        nat[0] = nt(da, k[...])
        nat[1] = nt(db, k[...])
        nat[2] = nt(e, jnp.concatenate([r, jnp.zeros((PAD - FH, toks), BF16)], axis=0))

    def reduce_start(g, meanwhile):
        def split(zz):
            part = [nat[m, block_at(zz)] for m in range(3)]
            part.append(jnp.zeros((128 - 3 * ZROWS, PAD), F32))
            block = jnp.concatenate(part, axis=0).astype(BF16)
            slots = nn(perm[2], block[:, 0:256]).astype(BF16)
            ends = nn(perm[3], block[:, 256:PAD])
            ends = (ends[0:64] + pltpu.roll(ends[64:128], 64, 1)).astype(BF16)
            here = pl.ds(zz * NY, NY)
            gs[g, :, here, 0:SLOT] = slots[:, 0:128].reshape(NC, NY, SLOT, 128)
            gs[g, :, here, SLOT : 2 * SLOT] = slots[:, 128:256].reshape(NC, NY, SLOT, 128)
            gs[g, :, here, 2 * SLOT : LINES] = ends.reshape(NC, NY, 8, 128)

        def to_mate(zz):
            here = pl.ds(zz * NY, NY)
            pltpu.make_async_remote_copy(
                gs.at[g, 1 - c, here], cr.at[g, here], cs_send.at[g], cs_recv.at[g, zz], {"tok": mate}
            ).start()

        landing = rr.at[g, chip - z_from[g] * NY]

        def send(zz, yy, is_me):
            p = zz * NY + yy
            if is_me:
                pltpu.make_async_copy(red.at[g, p], landing, rs_recv.at[g]).start()
            else:
                pltpu.make_async_remote_copy(
                    red.at[g, p], landing, rs_send.at[g], rs_recv.at[g], at_chip(p)
                ).start()

        def pass_sum(dz):
            zz = lax.rem(zme + dz, NZ)
            here = pl.ds(zz * NY, NY)
            four = cr.at[g, here]
            pltpu.make_async_copy(four, four, cs_recv.at[g, zz]).wait()
            red[g, here] = (gs[g, c, here].astype(F32) + cr[g, here].astype(F32)).astype(BF16)
            peers((dz,), send)

        for half in (FAR_FIRST[: NZ // 2], FAR_FIRST[NZ // 2 :]):
            for dz in half:
                split(lax.rem(zme + dz, NZ))
            for dz in half:
                to_mate(lax.rem(zme + dz, NZ))
        meanwhile()
        for dz in FAR_FIRST:
            pass_sum(dz)

    def reduce_finish(g):
        every = rr.at[g]
        pltpu.make_async_copy(every, every, rs_recv.at[g]).wait()
        total = jnp.sum(rr[g].astype(F32), axis=0)
        old = state[...]
        fresh = old - total
        old_norm = jnp.sqrt(row_sums(old * old))
        new_norm = jnp.sqrt(row_sums(fresh * fresh) + 1e-06)
        return fresh * spread(old_norm / new_norm)

    def reduce_drain(g):
        @pl.when(live[g])
        def _():
            every = cr.at[g]
            pltpu.make_async_copy(every, every, cs_send.at[g]).wait()
            thirty_one = red.at[g, pl.ds(0, CHIPS - 1)]
            pltpu.make_async_copy(thirty_one, thirty_one, rs_send.at[g]).wait()

    def apply_queries():
        a = nn(gt[...], q[...])
        b = nn(ut[...], q[...])
        hidden = (a * jax.nn.sigmoid(a) * b).astype(BF16)
        return nn(dt[...], hidden)

    def far_copy(n):
        return pltpu.make_async_remote_copy(
            (k.at[pl.ds(0, HD)], v)[n], kv_far.at[n], kv_send.at[n], kv_recv.at[n], at_chip(lax.rem(chip + 1, CHIPS))
        )

    def near_copy(n, src):
        return pltpu.make_async_remote_copy(src, kv_near.at[n], kv_send.at[2 + n], kv_recv.at[2 + n], {"tok": mate})

    def pass_on(n):
        far_copy(n).wait()

        @pl.when(c == 1)
        def _():
            near_copy(n, kv_far.at[n]).start()

    def exchange_squares():
        mixed = y_buf[...]
        sums = jnp.sum(mixed * mixed, axis=0, keepdims=True)
        sq[...] = sums
        sqr[h] = sums
        for n in range(1, HEADS):
            pltpu.make_async_remote_copy(sq, sqr.at[h], sq_send, sq_recv, {"head": lax.rem(h + n, HEADS)}).start()

    gather_start(0)

    @pl.when(c == 0)
    def _():
        for n in range(2):
            near_copy(n, (k.at[pl.ds(0, HD)], v)[n]).start()

    @pl.when(live[0])
    def _():
        gather_finish(0)
        grads(0)
        reduce_start(0, lambda: None)
        y_buf[...] = apply_queries()

    @pl.when(jnp.logical_not(live[0]))
    def _():
        relay_only(0)
        pl.semaphore_wait(go, 1)
        far_copy(0).start()

    pass_on(0)
    middle = reduce_finish(0)
    state[...] = middle
    own[1] = middle.astype(BF16)
    gather_start(1)

    near_copy(0, kv_far.at[0]).wait()
    scale = 1.0 / math.sqrt(HD)
    j = lax.broadcasted_iota(jnp.int32, (toks, toks), 0)
    i = lax.broadcasted_iota(jnp.int32, (toks, toks), 1)
    reach = back[...]
    scores = []
    for ahead, keys in ((2 * toks, kv_far.at[0]), (toks, kv_near.at[0]), (0, k.at[pl.ds(0, HD)])):
        away = i - j + ahead
        seen = (away >= 0) & (away <= reach) & (start + j - ahead >= 0)
        scores.append(jnp.where(seen, tn(keys[...], q[...]) * scale, -jnp.inf))
    top = functools.reduce(jnp.maximum, [jnp.max(s, axis=0, keepdims=True) for s in scores])
    weights = [jnp.exp(s - top) for s in scores]
    total = functools.reduce(jnp.add, [jnp.sum(w, axis=0, keepdims=True) for w in weights])
    for n, w in enumerate(weights):
        probs[n] = (w / total).astype(BF16)

    @pl.when(jnp.logical_not(live[1]))
    def _():
        relay_only(1)
        pl.semaphore_wait(go, 1)
        far_copy(1).start()

    @pl.when(live[1])
    def _():
        gather_finish(1)
        grads(1)

        def outputs():
            y_buf[...] = jnp.where(first, y_buf[...], apply_queries())
            exchange_squares()

        reduce_start(1, outputs)

    @pl.when(jnp.logical_not(live[1]))
    def _():
        exchange_squares()

    pass_on(1)
    near_copy(1, v).wait()
    attn = nn(kv_far[1], probs[0]) + nn(kv_near[1], probs[1]) + nn(v[...], probs[2])
    seven = sqr.at[pl.ds(0, HEADS - 1)]
    pltpu.make_async_copy(seven, seven, sq_recv).wait()
    mean_square = jnp.sum(sqr[...], axis=0) / (HEADS * HD)
    gains = jnp.broadcast_to(gain[...].reshape(1, HD), (8, HD)).T[:, 0:1]
    normed = y_buf[...] / jnp.sqrt(mean_square + 1e-06) * gains
    out[...] = (normed + attn).astype(BF16)
    last = unpack(reduce_finish(1))
    for m, ref in enumerate((g_out, u_out, d_out)):
        ref[...] = last[m * OWN : (m + 1) * OWN].reshape(OWN, 1, HD)
    pltpu.make_async_copy(seven, seven, sq_send).wait()
    for g in range(2):
        gather_drain(g)
        reduce_drain(g)


def write_out(*refs):
    half = len(refs) // 2
    srcs, dsts, sem = refs[:half], refs[half:-1], refs[-1]
    copies = [pltpu.make_async_copy(src, dst, sem.at[n]) for n, (src, dst) in enumerate(zip(srcs, dsts))]
    for copy in copies:
        copy.start()
    for copy in copies:
        copy.wait()


def on_device(queries, keys, values, rates, back, group_end, gate_init, up_init, down_init, gain):
    toks = rates.shape[0]
    perm = order_matrices()
    vmem = pl.BlockSpec(memory_space=pltpu.VMEM)
    hbm = pl.BlockSpec(memory_space=pltpu.HBM)
    slots = (CHIPS, LINES, 128)
    dma = pltpu.SemaphoreType.DMA
    shares = [w.transpose(2, 0, 1) for w in (gate_init, up_init, down_init)]
    share = jax.ShapeDtypeStruct((OWN, 1, HD), F32)
    shapes = (jax.ShapeDtypeStruct((HD, toks), BF16), share, share, share)
    results = pl.pallas_call(
        kernel,
        out_shape=shapes,
        in_specs=[pl.BlockSpec(memory_space=pltpu.SMEM)] + [hbm] * 10,
        out_specs=(vmem,) * 4,
        scratch_shapes=[
            pltpu.VMEM((HD, toks), BF16),
            pltpu.VMEM((PAD, toks), BF16),
            pltpu.VMEM((HD, toks), BF16),
            pltpu.VMEM((1, toks), F32),
            pltpu.VMEM((1, toks), jnp.int32),
            pltpu.VMEM((SLOT, 1, HD), F32),
            pltpu.VMEM((HD,), F32),
            pltpu.VMEM((4, 128, 128), BF16),
            pltpu.VMEM((2, LINES, 128), BF16),
            pltpu.VMEM((2, NC, *slots), BF16),
            pltpu.VMEM((2, NC, *slots), BF16),
            pltpu.VMEM((2, *slots), BF16),
            pltpu.VMEM((2, *slots), BF16),
            pltpu.VMEM((2, LAST_FIRST * NY, LINES, 128), BF16),
            pltpu.VMEM((2, HD, toks), BF16),
            pltpu.VMEM((2, HD, toks), BF16),
            pltpu.VMEM((1, toks), F32),
            pltpu.VMEM((HEADS, 1, toks), F32),
            pltpu.VMEM((3, HD, PAD), F32),
            pltpu.VMEM((FH, HD), BF16),
            pltpu.VMEM((FH, HD), BF16),
            pltpu.VMEM((HD, FH), BF16),
            pltpu.VMEM((2, HD, toks), BF16),
            pltpu.VMEM((HD, toks), F32),
            pltpu.VMEM((3, toks, toks), BF16),
            pltpu.VMEM((LINES, 128), F32),
            dma((10,)),
            dma((2,)), dma((2, NZ)),
            dma((2,)), dma((2, NZ)),
            dma((2,)), dma((2, NZ)),
            dma((2,)), dma((2,)),
            dma((4,)), dma((4,)),
            dma, dma,
            pltpu.SemaphoreType.REGULAR,
        ],
        compiler_params=pltpu.CompilerParams(
            collective_id=0, has_side_effects=True, vmem_limit_bytes=48 * 1024 * 1024
        ),
        name="layer",
    )(
        group_end,
        *(
            pltpu.with_memory_space_constraint(array, pltpu.HBM)
            for array in (
                queries.T, keys.T, values.T, rates.T, back.reshape(1, toks), *shares, gain,
                jnp.asarray(perm, BF16),
            )
        ),
    )
    out, *finals = pl.pallas_call(
        write_out,
        out_shape=shapes,
        in_specs=[vmem] * 4,
        out_specs=(hbm,) * 4,
        scratch_shapes=[dma((4,))],
        compiler_params=pltpu.CompilerParams(vmem_limit_bytes=1024 * 1024),
        name="write_out",
    )(*results)
    return (out.T, *(w.transpose(1, 2, 0) for w in finals))


def solution(mesh):
    placed = (
        P("tok", "head"),
        P("tok", "head"),
        P("tok", "head"),
        P("tok", "head"),
        P("tok"),
        P(),
        P("head", None, "tok"),
        P("head", None, "tok"),
        P("head", None, "tok"),
        P("head"),
    )
    return jax.shard_map(
        on_device,
        mesh=mesh,
        in_specs=placed,
        out_specs=(
            P("tok", "head"),
            P("head", None, "tok"),
            P("head", None, "tok"),
            P("head", None, "tok"),
        ),
        check_vma=False,
    )
```

```python
import functools
import math

import jax
import jax.numpy as jnp
import numpy as np
from jax import lax
from jax.experimental import pallas as pl
from jax.experimental.pallas import tpu as pltpu
from jax.sharding import PartitionSpec as P

HEADS = 8
HD = 320
FH = 320
WINDOW = 512
NZ, NY, NC = 8, 4, 2
CHIPS = NZ * NY
NX = 4
OWN = 5
SLOT = 16
LINES = 40
PAD = 384
ZROWS = NY * NC * OWN
LAST_FIRST = 12288 * NZ // 16384
FIRST_SECOND = 4096 * NZ // 16384
FAR_FIRST = (4, 3, 5, 2, 6, 1, 7, 0)
NEAR_FIRST = (6, 2, 0, 1, 7, 5, 3, 4)
F32, BF16 = jnp.float32, jnp.bfloat16


def nn(a, b):
    return lax.dot_general(a, b, (((1,), (0,)), ((), ())), preferred_element_type=F32)


def nt(a, b):
    return lax.dot_general(a, b, (((1,), (1,)), ((), ())), preferred_element_type=F32)


def tn(a, b):
    return lax.dot_general(a, b, (((0,), (0,)), ((), ())), preferred_element_type=F32)


def order_matrices():
    perm = np.zeros((2, 128, 128), np.float32)
    for m in range(3):
        for y in range(NY):
            for c in range(NC):
                for j in range(OWN):
                    row = m * OWN + j
                    natural = m * ZROWS + (y * NC + c) * OWN + j
                    perm[0, natural, c * 64 + y * SLOT + row] = 1.0
                    perm[1, natural, row // 8 * 64 + c * 32 + y * 8 + row % 8] = 1.0
    return np.concatenate([perm, perm.transpose(0, 2, 1)])


def pack(rows):
    last = rows[:, 256:384]
    return jnp.concatenate([rows[:, 0:128], rows[:, 128:256], last[0:8] + pltpu.roll(last[8:16], 64, 1)], axis=0)


def unpack(packed):
    last = jnp.concatenate([packed[32:40], pltpu.roll(packed[32:40], 64, 1)], axis=0)
    return jnp.concatenate([packed[0:16], packed[16:32], last[:, 0:64]], axis=1)


def row_sums(packed):
    left = lax.broadcasted_iota(jnp.int32, (8, 128), 1) < 64
    last = packed[32:40]
    ends = [jnp.where(left, last, 0.0), jnp.where(left, 0.0, last)]
    whole = packed[0:16] + packed[16:32] + jnp.concatenate(ends, axis=0)
    return jnp.sum(whole, axis=1, keepdims=True)


def spread(factor):
    wide = jnp.broadcast_to(factor, (SLOT, 128))
    left = lax.broadcasted_iota(jnp.int32, (8, 128), 1) < 64
    return jnp.concatenate([wide, wide, jnp.where(left, wide[0:8], wide[8:16])], axis=0)


def kernel(
    ge, q_hbm, k_hbm, v_hbm, rates_hbm, back_hbm, g_hbm, u_hbm, d_hbm, gain_hbm, perm_hbm,
    out, g_out, u_out, d_out,
    q, k, v, rates, back, rows0, gain, perm,
    own, ag, gs, cr, red, rr, kv_far, kv_near, sq, sqr, nat, gt, ut, dt, es, y_buf, probs, state,
    in_sem, ag_send, ag_recv, fw_send, fw_recv, cs_send, cs_recv, rs_send, rs_recv, kv_send, kv_recv, sq_send, sq_recv, go,
):
    toks = q.shape[1]
    t = lax.axis_index("tok")
    h = lax.axis_index("head")
    c = lax.rem(t, 2)
    chip = lax.div(t, 2)
    zme = lax.div(chip, NY)
    yme = lax.rem(chip, NY)
    mate = t + 1 - 2 * c

    loads = [
        pltpu.make_async_copy(src, dst, in_sem.at[n])
        for n, (src, dst) in enumerate(
            (
                (g_hbm, rows0.at[pl.ds(0, OWN)]),
                (u_hbm, rows0.at[pl.ds(OWN, OWN)]),
                (d_hbm, rows0.at[pl.ds(2 * OWN, OWN)]),
                (k_hbm, k.at[pl.ds(0, HD)]),
                (v_hbm, v),
                (q_hbm, q),
                (rates_hbm, rates),
                (back_hbm, back),
                (gain_hbm, gain),
                (perm_hbm, perm),
            )
        )
    ]
    def at_chip(p):
        return {"tok": 2 * p + c}

    barrier = pltpu.get_barrier_semaphore()

    for dz in (2, 6, 1, 7, 0):
        zz = lax.rem(zme + dz, NZ)
        for dy in range(NY):
            if dz or dy:
                pl.semaphore_signal(barrier, inc=1, device_id=at_chip(zz * NY + lax.rem(yme + dy, NY)))
    across, along = lax.div(h, NX), lax.rem(h, NX)
    opposite = {"head": (1 - across) * NX + along}
    pl.semaphore_signal(barrier, inc=1, device_id=opposite)
    beside = [{"head": across * NX + lax.rem(along + n, NX)} for n in range(1, NX)]
    for there in beside:
        pl.semaphore_signal(barrier, inc=1, device_id=there)
    pl.semaphore_signal(barrier, inc=1, device_id={"tok": mate})
    for load in loads:
        load.start()

    rows0[pl.ds(3 * OWN, 1)] = jnp.zeros((1, 1, HD), F32)
    for load in loads:
        load.wait()
    share = rows0[...].reshape(SLOT, HD)
    state[...] = pack(jnp.concatenate([share, jnp.zeros((SLOT, PAD - HD), F32)], axis=1))
    own[0] = state[...].astype(BF16)
    k[pl.ds(HD, PAD - HD)] = jnp.zeros((PAD - HD, toks), BF16)
    start = t * toks
    first = start + lax.broadcasted_iota(jnp.int32, (1, toks), 1) < ge[0]
    rate = rates[...]
    vf = v[...].astype(F32)
    es[0] = (-jnp.where(first, rate, 0.0) * vf).astype(BF16)
    es[1] = (-jnp.where(first, 0.0, rate) * vf).astype(BF16)
    y_buf[...] = jnp.zeros_like(y_buf)

    pl.semaphore_wait(barrier, (5 * NY - 1) + 1 + (NX - 1) + 1)

    def active(g, z):
        return z < LAST_FIRST if g == 0 else z >= FIRST_SECOND

    live = [active(g, zme) for g in range(2)]
    z_from = (0, FIRST_SECOND)

    def peers(dzs, body):
        for dz in dzs:
            zz = lax.rem(zme + dz, NZ)
            for dy in range(NY):
                yy = lax.rem(yme + dy, NY)
                body(zz, yy, dz == 0 and dy == 0)

    def gather_start(g):
        mine = ag.at[g, c, chip]

        def send(zz, yy, is_me):
            if is_me:
                pltpu.make_async_copy(own.at[g], mine, ag_recv.at[g, zme]).start()
            else:
                pltpu.make_async_remote_copy(
                    own.at[g], mine, ag_send.at[g], ag_recv.at[g, zme], at_chip(zz * NY + yy)
                ).start()

        peers((2, 6), send)
        for dz in (1, 7, 0):

            @pl.when(active(g, lax.rem(zme + dz, NZ)))
            def _():
                peers((dz,), send)

    def arrived(g, zz):
        four = ag.at[g, c, pl.ds(zz * NY, NY)]
        pltpu.make_async_copy(four, four, ag_recv.at[g, zz]).wait()

    def relay(g, dz):
        zz = lax.rem(zme + dz, NZ)
        half = 0 if dz == 6 else NY // 2
        for more, begin, size in ((1, 0, NY), (2, half, NY // 2)):
            to = lax.rem(zme + (more if dz == 6 else NZ - more), NZ)

            @pl.when(active(g, to))
            def _():
                some = ag.at[g, c, pl.ds(zz * NY + begin, size)]
                pltpu.make_async_remote_copy(
                    some, some, ag_send.at[g], ag_recv.at[g, zz], at_chip(to * NY + yme)
                ).start()

    def relay_only(g):
        for dz in (2, 6):
            arrived(g, lax.rem(zme + dz, NZ))
            relay(g, dz)

    def block_at(zz):
        return pl.ds(pl.multiple_of(zz * ZROWS, 8), ZROWS)

    def gather_finish(g):
        def forwarded(zz):
            four = ag.at[g, 1 - c, pl.ds(zz * NY, NY)]
            pltpu.make_async_copy(four, four, fw_recv.at[g, zz]).wait()

        def arrange(zz):
            both = [ag[g, core, pl.ds(zz * NY, NY)] for core in range(NC)]
            wide = [
                jnp.concatenate([x[:, r : r + SLOT].reshape(NY * SLOT, 128) for x in both], axis=0) for r in (0, SLOT)
            ]
            ordered = nn(perm[0], jnp.concatenate(wide, axis=1))
            ends = jnp.concatenate([x[:, 2 * SLOT :].reshape(NY * 8, 128) for x in both], axis=0).astype(F32)
            left = lax.broadcasted_iota(jnp.int32, ends.shape, 1) < 64
            halves = [jnp.where(left, x, 0.0) for x in (ends, pltpu.roll(ends, 64, 1))]
            ordered_ends = nn(perm[1], jnp.concatenate(halves, axis=0).astype(BF16))
            for m in range(3):
                rows = slice(m * ZROWS, (m + 1) * ZROWS)
                nat[m, block_at(zz), 0:256] = ordered[rows]
                nat[m, block_at(zz), 256:PAD] = ordered_ends[rows]

        order = [lax.rem(zme + dz, NZ) for dz in NEAR_FIRST]
        for n, zz in enumerate(order):
            four = ag.at[g, c, pl.ds(zz * NY, NY)]
            arrived(g, zz)
            if NEAR_FIRST[n] in (2, 6):
                relay(g, NEAR_FIRST[n])
            pltpu.make_async_remote_copy(four, four, fw_send.at[g], fw_recv.at[g, zz], {"tok": mate}).start()
            if n % 2 and n >= 5:
                for zz in order[n - 5 : n - 3]:
                    forwarded(zz)
                for zz in order[n - 5 : n - 3]:
                    arrange(zz)
        far_copy(g).start()
        tell, away = ((2, 3), 4) if g == 0 else ((4, 5), -4)

        @pl.when((zme == tell[0]) | (zme == tell[1]))
        def _():
            pl.semaphore_signal(go, inc=1, device_id={"tok": t + away * NY * NC})

        for pair in (order[4:6], order[6:8]):
            for zz in pair:
                forwarded(zz)
            for zz in pair:
                arrange(zz)
        for m, ref in enumerate((gt, ut, dt)):
            ref[...] = nat[m, :, 0:HD].astype(BF16)

    def gather_drain(g):
        taking = [z < LAST_FIRST if g == 0 else z >= FIRST_SECOND for z in range(NZ)]
        weights = ((1, 2 * NY), (7, 2 * NY), (0, NY - 1), (2, NY // 2), (6, NY // 2))
        sent = [2 * NY + sum(n for dz, n in weights if taking[(z + dz) % NZ]) for z in range(NZ)]
        for n in sorted(set(sent)):
            same = functools.reduce(jnp.logical_or, [zme == z for z in range(NZ) if sent[z] == n])

            @pl.when(same)
            def _():
                some = ag.at[g, 0, pl.ds(0, n)]
                pltpu.make_async_copy(some, some, ag_send.at[g]).wait()

        @pl.when(live[g])
        def _():
            every = ag.at[g, 0]
            pltpu.make_async_copy(every, every, fw_send.at[g]).wait()

    def grads(g):
        kk, e = k[pl.ds(0, HD)], es[g]
        a = nn(gt[...], kk)
        b = nn(ut[...], kk)
        s = jax.nn.sigmoid(a)
        act = a * s
        r = (act * b).astype(BF16)
        du = tn(dt[...], e)
        da = (du * b * s * (1.0 + a * (1.0 - s))).astype(BF16)
        db = (du * act).astype(BF16)
        nat[0] = nt(da, k[...])
        nat[1] = nt(db, k[...])
        nat[2] = nt(e, jnp.concatenate([r, jnp.zeros((PAD - FH, toks), BF16)], axis=0))

    def reduce_start(g, meanwhile):
        def split(zz):
            part = [nat[m, block_at(zz)] for m in range(3)]
            part.append(jnp.zeros((128 - 3 * ZROWS, PAD), F32))
            block = jnp.concatenate(part, axis=0).astype(BF16)
            slots = nn(perm[2], block[:, 0:256]).astype(BF16)
            ends = nn(perm[3], block[:, 256:PAD])
            ends = (ends[0:64] + pltpu.roll(ends[64:128], 64, 1)).astype(BF16)
            here = pl.ds(zz * NY, NY)
            gs[g, :, here, 0:SLOT] = slots[:, 0:128].reshape(NC, NY, SLOT, 128)
            gs[g, :, here, SLOT : 2 * SLOT] = slots[:, 128:256].reshape(NC, NY, SLOT, 128)
            gs[g, :, here, 2 * SLOT : LINES] = ends.reshape(NC, NY, 8, 128)

        def to_mate(zz):
            here = pl.ds(zz * NY, NY)
            pltpu.make_async_remote_copy(
                gs.at[g, 1 - c, here], cr.at[g, here], cs_send.at[g], cs_recv.at[g, zz], {"tok": mate}
            ).start()

        landing = rr.at[g, chip - z_from[g] * NY]

        def send(zz, yy, is_me):
            p = zz * NY + yy
            if is_me:
                pltpu.make_async_copy(red.at[g, p], landing, rs_recv.at[g]).start()
            else:
                pltpu.make_async_remote_copy(
                    red.at[g, p], landing, rs_send.at[g], rs_recv.at[g], at_chip(p)
                ).start()

        def pass_sum(dz):
            zz = lax.rem(zme + dz, NZ)
            here = pl.ds(zz * NY, NY)
            four = cr.at[g, here]
            pltpu.make_async_copy(four, four, cs_recv.at[g, zz]).wait()
            red[g, here] = (gs[g, c, here].astype(F32) + cr[g, here].astype(F32)).astype(BF16)
            peers((dz,), send)

        for half in (FAR_FIRST[: NZ // 2], FAR_FIRST[NZ // 2 :]):
            for dz in half:
                split(lax.rem(zme + dz, NZ))
            for dz in half:
                to_mate(lax.rem(zme + dz, NZ))
        meanwhile()
        for dz in FAR_FIRST:
            pass_sum(dz)

    def reduce_finish(g):
        every = rr.at[g]
        pltpu.make_async_copy(every, every, rs_recv.at[g]).wait()
        total = jnp.sum(rr[g].astype(F32), axis=0)
        old = state[...]
        fresh = old - total
        old_norm = jnp.sqrt(row_sums(old * old))
        new_norm = jnp.sqrt(row_sums(fresh * fresh) + 1e-06)
        return fresh * spread(old_norm / new_norm)

    def reduce_drain(g):
        @pl.when(live[g])
        def _():
            every = cr.at[g]
            pltpu.make_async_copy(every, every, cs_send.at[g]).wait()
            thirty_one = red.at[g, pl.ds(0, CHIPS - 1)]
            pltpu.make_async_copy(thirty_one, thirty_one, rs_send.at[g]).wait()

    def apply_queries():
        a = nn(gt[...], q[...])
        b = nn(ut[...], q[...])
        hidden = (a * jax.nn.sigmoid(a) * b).astype(BF16)
        return nn(dt[...], hidden)

    def far_copy(n):
        return pltpu.make_async_remote_copy(
            (k.at[pl.ds(0, HD)], v)[n], kv_far.at[n], kv_send.at[n], kv_recv.at[n], at_chip(lax.rem(chip + 1, CHIPS))
        )

    def near_copy(n, src):
        return pltpu.make_async_remote_copy(src, kv_near.at[n], kv_send.at[2 + n], kv_recv.at[2 + n], {"tok": mate})

    def pass_on(n):
        far_copy(n).wait()

        @pl.when(c == 1)
        def _():
            near_copy(n, kv_far.at[n]).start()

    def exchange_squares():
        mixed = y_buf[...]
        sums = jnp.sum(mixed * mixed, axis=0, keepdims=True)
        sq[0] = sums
        sqr[along] = sums
        for there in beside:
            pltpu.make_async_remote_copy(sq.at[0], sqr.at[along], sq_send.at[0], sq_recv.at[0], there).start()

    gather_start(0)

    @pl.when(c == 0)
    def _():
        for n in range(2):
            near_copy(n, (k.at[pl.ds(0, HD)], v)[n]).start()

    @pl.when(live[0])
    def _():
        gather_finish(0)
        grads(0)
        reduce_start(0, lambda: None)
        y_buf[...] = apply_queries()

    @pl.when(jnp.logical_not(live[0]))
    def _():
        relay_only(0)
        pl.semaphore_wait(go, 1)
        far_copy(0).start()

    pass_on(0)
    middle = reduce_finish(0)
    state[...] = middle
    own[1] = middle.astype(BF16)
    gather_start(1)

    near_copy(0, kv_far.at[0]).wait()
    scale = 1.0 / math.sqrt(HD)
    j = lax.broadcasted_iota(jnp.int32, (toks, toks), 0)
    i = lax.broadcasted_iota(jnp.int32, (toks, toks), 1)
    reach = back[...]
    scores = []
    for ahead, keys in ((2 * toks, kv_far.at[0]), (toks, kv_near.at[0]), (0, k.at[pl.ds(0, HD)])):
        away = i - j + ahead
        seen = (away >= 0) & (away <= reach) & (start + j - ahead >= 0)
        scores.append(jnp.where(seen, tn(keys[...], q[...]) * scale, -jnp.inf))
    top = functools.reduce(jnp.maximum, [jnp.max(s, axis=0, keepdims=True) for s in scores])
    weights = [jnp.exp(s - top) for s in scores]
    total = functools.reduce(jnp.add, [jnp.sum(w, axis=0, keepdims=True) for w in weights])
    for n, w in enumerate(weights):
        probs[n] = (w / total).astype(BF16)

    @pl.when(jnp.logical_not(live[1]))
    def _():
        relay_only(1)
        pl.semaphore_wait(go, 1)
        far_copy(1).start()

    @pl.when(live[1])
    def _():
        gather_finish(1)
        grads(1)

        def outputs():
            y_buf[...] = jnp.where(first, y_buf[...], apply_queries())
            exchange_squares()

        reduce_start(1, outputs)

    @pl.when(jnp.logical_not(live[1]))
    def _():
        exchange_squares()

    three = sqr.at[pl.ds(0, NX - 1)]
    pltpu.make_async_copy(three, three, sq_recv.at[0]).wait()
    sq[1] = jnp.sum(sqr[...], axis=0)
    squares = pltpu.make_async_remote_copy(sq.at[1], sq.at[2], sq_send.at[1], sq_recv.at[1], opposite)
    squares.start()
    pass_on(1)
    near_copy(1, v).wait()
    attn = nn(kv_far[1], probs[0]) + nn(kv_near[1], probs[1]) + nn(v[...], probs[2])
    squares.wait()
    mean_square = (sq[1] + sq[2]) / (HEADS * HD)
    gains = jnp.broadcast_to(gain[...].reshape(1, HD), (8, HD)).T[:, 0:1]
    normed = y_buf[...] / jnp.sqrt(mean_square + 1e-06) * gains
    out[...] = (normed + attn).astype(BF16)
    last = unpack(reduce_finish(1))
    for m, ref in enumerate((g_out, u_out, d_out)):
        ref[...] = last[m * OWN : (m + 1) * OWN].reshape(OWN, 1, HD)
    pltpu.make_async_copy(three, three, sq_send.at[0]).wait()
    for g in range(2):
        gather_drain(g)
        reduce_drain(g)


def write_out(*refs):
    half = len(refs) // 2
    srcs, dsts, sem = refs[:half], refs[half:-1], refs[-1]
    copies = [pltpu.make_async_copy(src, dst, sem.at[n]) for n, (src, dst) in enumerate(zip(srcs, dsts))]
    for copy in copies:
        copy.start()
    for copy in copies:
        copy.wait()


def on_device(queries, keys, values, rates, back, group_end, gate_init, up_init, down_init, gain):
    toks = rates.shape[0]
    perm = order_matrices()
    vmem = pl.BlockSpec(memory_space=pltpu.VMEM)
    hbm = pl.BlockSpec(memory_space=pltpu.HBM)
    slots = (CHIPS, LINES, 128)
    dma = pltpu.SemaphoreType.DMA
    shares = [w.transpose(2, 0, 1) for w in (gate_init, up_init, down_init)]
    share = jax.ShapeDtypeStruct((OWN, 1, HD), F32)
    shapes = (jax.ShapeDtypeStruct((HD, toks), BF16), share, share, share)
    results = pl.pallas_call(
        kernel,
        out_shape=shapes,
        in_specs=[pl.BlockSpec(memory_space=pltpu.SMEM)] + [hbm] * 10,
        out_specs=(vmem,) * 4,
        scratch_shapes=[
            pltpu.VMEM((HD, toks), BF16),
            pltpu.VMEM((PAD, toks), BF16),
            pltpu.VMEM((HD, toks), BF16),
            pltpu.VMEM((1, toks), F32),
            pltpu.VMEM((1, toks), jnp.int32),
            pltpu.VMEM((SLOT, 1, HD), F32),
            pltpu.VMEM((HD,), F32),
            pltpu.VMEM((4, 128, 128), BF16),
            pltpu.VMEM((2, LINES, 128), BF16),
            pltpu.VMEM((2, NC, *slots), BF16),
            pltpu.VMEM((2, NC, *slots), BF16),
            pltpu.VMEM((2, *slots), BF16),
            pltpu.VMEM((2, *slots), BF16),
            pltpu.VMEM((2, LAST_FIRST * NY, LINES, 128), BF16),
            pltpu.VMEM((2, HD, toks), BF16),
            pltpu.VMEM((2, HD, toks), BF16),
            pltpu.VMEM((3, 1, toks), F32),
            pltpu.VMEM((NX, 1, toks), F32),
            pltpu.VMEM((3, HD, PAD), F32),
            pltpu.VMEM((FH, HD), BF16),
            pltpu.VMEM((FH, HD), BF16),
            pltpu.VMEM((HD, FH), BF16),
            pltpu.VMEM((2, HD, toks), BF16),
            pltpu.VMEM((HD, toks), F32),
            pltpu.VMEM((3, toks, toks), BF16),
            pltpu.VMEM((LINES, 128), F32),
            dma((10,)),
            dma((2,)), dma((2, NZ)),
            dma((2,)), dma((2, NZ)),
            dma((2,)), dma((2, NZ)),
            dma((2,)), dma((2,)),
            dma((4,)), dma((4,)),
            dma((2,)), dma((2,)),
            pltpu.SemaphoreType.REGULAR,
        ],
        compiler_params=pltpu.CompilerParams(
            collective_id=0, has_side_effects=True, vmem_limit_bytes=48 * 1024 * 1024
        ),
        name="layer",
    )(
        group_end,
        *(
            pltpu.with_memory_space_constraint(array, pltpu.HBM)
            for array in (
                queries.T, keys.T, values.T, rates.T, back.reshape(1, toks), *shares, gain,
                jnp.asarray(perm, BF16),
            )
        ),
    )
    out, *finals = pl.pallas_call(
        write_out,
        out_shape=shapes,
        in_specs=[vmem] * 4,
        out_specs=(hbm,) * 4,
        scratch_shapes=[dma((4,))],
        compiler_params=pltpu.CompilerParams(vmem_limit_bytes=1024 * 1024),
        name="write_out",
    )(*results)
    return (out.T, *(w.transpose(1, 2, 0) for w in finals))


def solution(mesh):
    placed = (
        P("tok", "head"),
        P("tok", "head"),
        P("tok", "head"),
        P("tok", "head"),
        P("tok"),
        P(),
        P("head", None, "tok"),
        P("head", None, "tok"),
        P("head", None, "tok"),
        P("head"),
    )
    return jax.shard_map(
        on_device,
        mesh=mesh,
        in_specs=placed,
        out_specs=(
            P("tok", "head"),
            P("head", None, "tok"),
            P("head", None, "tok"),
            P("head", None, "tok"),
        ),
        check_vma=False,
    )
```

```python
import functools
import math

import jax
import jax.numpy as jnp
import numpy as np
from jax import lax
from jax.experimental import pallas as pl
from jax.experimental.pallas import tpu as pltpu
from jax.sharding import PartitionSpec as P

HEADS = 8
HD = 320
FH = 320
WINDOW = 512
NZ, NY, NC = 8, 4, 2
CHIPS = NZ * NY
NX = 4
OWN = 5
SLOT = 16
LINES = 40
PAD = 384
ZROWS = NY * NC * OWN
LAST_FIRST = 12288 * NZ // 16384
FIRST_SECOND = 4096 * NZ // 16384
FAR_FIRST = (4, 3, 5, 2, 6, 1, 7, 0)
NEAR_FIRST = (6, 2, 0, 1, 7, 5, 3, 4)
F32, BF16 = jnp.float32, jnp.bfloat16


def nn(a, b):
    return lax.dot_general(a, b, (((1,), (0,)), ((), ())), preferred_element_type=F32)


def nt(a, b):
    return lax.dot_general(a, b, (((1,), (1,)), ((), ())), preferred_element_type=F32)


def tn(a, b):
    return lax.dot_general(a, b, (((0,), (0,)), ((), ())), preferred_element_type=F32)


def order_matrices():
    perm = np.zeros((2, 128, 128), np.float32)
    for m in range(3):
        for y in range(NY):
            for c in range(NC):
                for j in range(OWN):
                    row = m * OWN + j
                    natural = m * ZROWS + (y * NC + c) * OWN + j
                    perm[0, natural, c * 64 + y * SLOT + row] = 1.0
                    perm[1, natural, row // 8 * 64 + c * 32 + y * 8 + row % 8] = 1.0
    return np.concatenate([perm, perm.transpose(0, 2, 1)])


def pack(rows):
    last = rows[:, 256:384]
    return jnp.concatenate([rows[:, 0:128], rows[:, 128:256], last[0:8] + pltpu.roll(last[8:16], 64, 1)], axis=0)


def unpack(packed):
    last = jnp.concatenate([packed[32:40], pltpu.roll(packed[32:40], 64, 1)], axis=0)
    return jnp.concatenate([packed[0:16], packed[16:32], last[:, 0:64]], axis=1)


def row_sums(packed):
    left = lax.broadcasted_iota(jnp.int32, (8, 128), 1) < 64
    last = packed[32:40]
    ends = [jnp.where(left, last, 0.0), jnp.where(left, 0.0, last)]
    whole = packed[0:16] + packed[16:32] + jnp.concatenate(ends, axis=0)
    return jnp.sum(whole, axis=1, keepdims=True)


def spread(factor):
    wide = jnp.broadcast_to(factor, (SLOT, 128))
    left = lax.broadcasted_iota(jnp.int32, (8, 128), 1) < 64
    return jnp.concatenate([wide, wide, jnp.where(left, wide[0:8], wide[8:16])], axis=0)


def kernel(
    ge, q_hbm, k_hbm, v_hbm, rates_hbm, back_hbm, g_hbm, u_hbm, d_hbm, gain_hbm, perm_hbm,
    out, g_out, u_out, d_out,
    q, k, v, rates, back, rows0, gain, perm,
    own, ag, gs, cr, red, rr, kv_far, kv_near, sq, sqr, nat, gt, ut, dt, es, y_buf, probs, state,
    in_sem, ag_send, ag_recv, fw_send, fw_recv, cs_send, cs_recv, rs_send, rs_recv, kv_send, kv_recv, sq_send, sq_recv, go,
):
    toks = q.shape[1]
    t = lax.axis_index("tok")
    h = lax.axis_index("head")
    c = lax.rem(t, 2)
    chip = lax.div(t, 2)
    zme = lax.div(chip, NY)
    yme = lax.rem(chip, NY)
    mate = t + 1 - 2 * c

    loads = [
        pltpu.make_async_copy(src, dst, in_sem.at[n])
        for n, (src, dst) in enumerate(
            (
                (g_hbm, rows0.at[pl.ds(0, OWN)]),
                (u_hbm, rows0.at[pl.ds(OWN, OWN)]),
                (d_hbm, rows0.at[pl.ds(2 * OWN, OWN)]),
                (k_hbm, k.at[pl.ds(0, HD)]),
                (v_hbm, v),
                (q_hbm, q),
                (rates_hbm, rates),
                (back_hbm, back),
                (gain_hbm, gain),
                (perm_hbm, perm),
            )
        )
    ]
    def at_chip(p):
        return {"tok": 2 * p + c}

    barrier = pltpu.get_barrier_semaphore()

    for dz in (2, 6, 1, 7, 0):
        zz = lax.rem(zme + dz, NZ)
        for dy in range(NY):
            if dz or dy:
                pl.semaphore_signal(barrier, inc=1, device_id=at_chip(zz * NY + lax.rem(yme + dy, NY)))
    across, along = lax.div(h, NX), lax.rem(h, NX)
    opposite = {"head": (1 - across) * NX + along}
    pl.semaphore_signal(barrier, inc=1, device_id=opposite)
    beside = [{"head": across * NX + lax.rem(along + n, NX)} for n in range(1, NX)]
    for there in beside:
        pl.semaphore_signal(barrier, inc=1, device_id=there)
    pl.semaphore_signal(barrier, inc=1, device_id={"tok": mate})
    for load in loads:
        load.start()

    rows0[pl.ds(3 * OWN, 1)] = jnp.zeros((1, 1, HD), F32)
    for load in loads:
        load.wait()
    share = rows0[...].reshape(SLOT, HD)
    state[...] = pack(jnp.concatenate([share, jnp.zeros((SLOT, PAD - HD), F32)], axis=1))
    own[0] = state[...].astype(BF16)
    k[pl.ds(HD, PAD - HD)] = jnp.zeros((PAD - HD, toks), BF16)
    start = t * toks
    first = start + lax.broadcasted_iota(jnp.int32, (1, toks), 1) < ge[0]
    rate = rates[...]
    vf = v[...].astype(F32)
    es[0] = (-jnp.where(first, rate, 0.0) * vf).astype(BF16)
    es[1] = (-jnp.where(first, 0.0, rate) * vf).astype(BF16)
    y_buf[...] = jnp.zeros_like(y_buf)

    pl.semaphore_wait(barrier, (5 * NY - 1) + 1 + (NX - 1) + 1)

    def active(g, z):
        return z < LAST_FIRST if g == 0 else z >= FIRST_SECOND

    live = [active(g, zme) for g in range(2)]
    z_from = (0, FIRST_SECOND)

    def peers(dzs, body):
        for dz in dzs:
            zz = lax.rem(zme + dz, NZ)
            for dy in range(NY):
                yy = lax.rem(yme + dy, NY)
                body(zz, yy, dz == 0 and dy == 0)

    def gather_start(g):
        mine = ag.at[g, c, chip]

        def send(zz, yy, is_me):
            if is_me:
                pltpu.make_async_copy(own.at[g], mine, ag_recv.at[g, zme]).start()
            else:
                pltpu.make_async_remote_copy(
                    own.at[g], mine, ag_send.at[g], ag_recv.at[g, zme], at_chip(zz * NY + yy)
                ).start()

        peers((2, 6), send)
        for dz in (1, 7, 0):

            @pl.when(active(g, lax.rem(zme + dz, NZ)))
            def _():
                peers((dz,), send)

    def arrived(g, zz):
        four = ag.at[g, c, pl.ds(zz * NY, NY)]
        pltpu.make_async_copy(four, four, ag_recv.at[g, zz]).wait()

    def relay(g, dz):
        zz = lax.rem(zme + dz, NZ)
        half = 0 if dz == 6 else NY // 2
        for more, begin, size in ((1, 0, NY), (2, half, NY // 2)):
            to = lax.rem(zme + (more if dz == 6 else NZ - more), NZ)

            @pl.when(active(g, to))
            def _():
                some = ag.at[g, c, pl.ds(zz * NY + begin, size)]
                pltpu.make_async_remote_copy(
                    some, some, ag_send.at[g], ag_recv.at[g, zz], at_chip(to * NY + yme)
                ).start()

    def relay_only(g):
        for dz in (2, 6):
            arrived(g, lax.rem(zme + dz, NZ))
            relay(g, dz)

    def block_at(zz):
        return pl.ds(pl.multiple_of(zz * ZROWS, 8), ZROWS)

    def gather_finish(g):
        def forwarded(zz):
            four = ag.at[g, 1 - c, pl.ds(zz * NY, NY)]
            pltpu.make_async_copy(four, four, fw_recv.at[g, zz]).wait()

        def arrange(zz):
            both = [ag[g, core, pl.ds(zz * NY, NY)] for core in range(NC)]
            wide = [
                jnp.concatenate([x[:, r : r + SLOT].reshape(NY * SLOT, 128) for x in both], axis=0) for r in (0, SLOT)
            ]
            ordered = nn(perm[0], jnp.concatenate(wide, axis=1))
            ends = jnp.concatenate([x[:, 2 * SLOT :].reshape(NY * 8, 128) for x in both], axis=0).astype(F32)
            left = lax.broadcasted_iota(jnp.int32, ends.shape, 1) < 64
            halves = [jnp.where(left, x, 0.0) for x in (ends, pltpu.roll(ends, 64, 1))]
            ordered_ends = nn(perm[1], jnp.concatenate(halves, axis=0).astype(BF16))
            for m in range(3):
                rows = slice(m * ZROWS, (m + 1) * ZROWS)
                nat[m, block_at(zz), 0:256] = ordered[rows]
                nat[m, block_at(zz), 256:PAD] = ordered_ends[rows]

        order = [lax.rem(zme + dz, NZ) for dz in NEAR_FIRST]
        for n, zz in enumerate(order):
            four = ag.at[g, c, pl.ds(zz * NY, NY)]
            arrived(g, zz)
            if NEAR_FIRST[n] in (2, 6):
                relay(g, NEAR_FIRST[n])
            pltpu.make_async_remote_copy(four, four, fw_send.at[g], fw_recv.at[g, zz], {"tok": mate}).start()
            if n >= 6:
                for zz in order[2 * n - 12 : 2 * n - 10]:
                    forwarded(zz)
                for zz in order[2 * n - 12 : 2 * n - 10]:
                    arrange(zz)
        far_copy(g).start()
        tell, away = ((2, 3), 4) if g == 0 else ((4, 5), -4)

        @pl.when((zme == tell[0]) | (zme == tell[1]))
        def _():
            pl.semaphore_signal(go, inc=1, device_id={"tok": t + away * NY * NC})

        for pair in (order[4:6], order[6:7], order[7:8]):
            for zz in pair:
                forwarded(zz)
            for zz in pair:
                arrange(zz)
        for m, ref in enumerate((gt, ut, dt)):
            ref[...] = nat[m, :, 0:HD].astype(BF16)

    def gather_drain(g):
        taking = [z < LAST_FIRST if g == 0 else z >= FIRST_SECOND for z in range(NZ)]
        weights = ((1, 2 * NY), (7, 2 * NY), (0, NY - 1), (2, NY // 2), (6, NY // 2))
        sent = [2 * NY + sum(n for dz, n in weights if taking[(z + dz) % NZ]) for z in range(NZ)]
        for n in sorted(set(sent)):
            same = functools.reduce(jnp.logical_or, [zme == z for z in range(NZ) if sent[z] == n])

            @pl.when(same)
            def _():
                some = ag.at[g, 0, pl.ds(0, n)]
                pltpu.make_async_copy(some, some, ag_send.at[g]).wait()

        @pl.when(live[g])
        def _():
            every = ag.at[g, 0]
            pltpu.make_async_copy(every, every, fw_send.at[g]).wait()

    def grads(g):
        kk, e = k[pl.ds(0, HD)], es[g]
        a = nn(gt[...], kk)
        b = nn(ut[...], kk)
        s = jax.nn.sigmoid(a)
        act = a * s
        r = (act * b).astype(BF16)
        du = tn(dt[...], e)
        da = (du * b * s * (1.0 + a * (1.0 - s))).astype(BF16)
        db = (du * act).astype(BF16)
        nat[0] = nt(da, k[...])
        nat[1] = nt(db, k[...])
        nat[2] = nt(e, jnp.concatenate([r, jnp.zeros((PAD - FH, toks), BF16)], axis=0))

    def reduce_start(g, meanwhile):
        def split(zz):
            part = [nat[m, block_at(zz)] for m in range(3)]
            part.append(jnp.zeros((128 - 3 * ZROWS, PAD), F32))
            block = jnp.concatenate(part, axis=0).astype(BF16)
            slots = nn(perm[2], block[:, 0:256]).astype(BF16)
            ends = nn(perm[3], block[:, 256:PAD])
            ends = (ends[0:64] + pltpu.roll(ends[64:128], 64, 1)).astype(BF16)
            here = pl.ds(zz * NY, NY)
            gs[g, :, here, 0:SLOT] = slots[:, 0:128].reshape(NC, NY, SLOT, 128)
            gs[g, :, here, SLOT : 2 * SLOT] = slots[:, 128:256].reshape(NC, NY, SLOT, 128)
            gs[g, :, here, 2 * SLOT : LINES] = ends.reshape(NC, NY, 8, 128)

        def to_mate(zz):
            here = pl.ds(zz * NY, NY)
            pltpu.make_async_remote_copy(
                gs.at[g, 1 - c, here], cr.at[g, here], cs_send.at[g], cs_recv.at[g, zz], {"tok": mate}
            ).start()

        landing = rr.at[g, chip - z_from[g] * NY]

        def send(zz, yy, is_me):
            p = zz * NY + yy
            if is_me:
                pltpu.make_async_copy(red.at[g, p], landing, rs_recv.at[g]).start()
            else:
                pltpu.make_async_remote_copy(
                    red.at[g, p], landing, rs_send.at[g], rs_recv.at[g], at_chip(p)
                ).start()

        def pass_sum(dz):
            zz = lax.rem(zme + dz, NZ)
            here = pl.ds(zz * NY, NY)
            four = cr.at[g, here]
            pltpu.make_async_copy(four, four, cs_recv.at[g, zz]).wait()
            red[g, here] = (gs[g, c, here].astype(F32) + cr[g, here].astype(F32)).astype(BF16)
            peers((dz,), send)

        for batch in (FAR_FIRST[:2], FAR_FIRST[2:4], FAR_FIRST[4:]):
            for dz in batch:
                split(lax.rem(zme + dz, NZ))
            for dz in batch:
                to_mate(lax.rem(zme + dz, NZ))
        meanwhile()
        for dz in FAR_FIRST:
            pass_sum(dz)

    def reduce_finish(g):
        every = rr.at[g]
        pltpu.make_async_copy(every, every, rs_recv.at[g]).wait()
        total = jnp.sum(rr[g].astype(F32), axis=0)
        old = state[...]
        fresh = old - total
        old_norm = jnp.sqrt(row_sums(old * old))
        new_norm = jnp.sqrt(row_sums(fresh * fresh) + 1e-06)
        return fresh * spread(old_norm / new_norm)

    def reduce_drain(g):
        @pl.when(live[g])
        def _():
            every = cr.at[g]
            pltpu.make_async_copy(every, every, cs_send.at[g]).wait()
            thirty_one = red.at[g, pl.ds(0, CHIPS - 1)]
            pltpu.make_async_copy(thirty_one, thirty_one, rs_send.at[g]).wait()

    def apply_queries():
        a = nn(gt[...], q[...])
        b = nn(ut[...], q[...])
        hidden = (a * jax.nn.sigmoid(a) * b).astype(BF16)
        return nn(dt[...], hidden)

    def far_copy(n):
        return pltpu.make_async_remote_copy(
            (k.at[pl.ds(0, HD)], v)[n], kv_far.at[n], kv_send.at[n], kv_recv.at[n], at_chip(lax.rem(chip + 1, CHIPS))
        )

    def near_copy(n, src):
        return pltpu.make_async_remote_copy(src, kv_near.at[n], kv_send.at[2 + n], kv_recv.at[2 + n], {"tok": mate})

    def pass_on(n):
        far_copy(n).wait()

        @pl.when(c == 1)
        def _():
            near_copy(n, kv_far.at[n]).start()

    def exchange_squares():
        mixed = y_buf[...]
        sums = jnp.sum(mixed * mixed, axis=0, keepdims=True)
        sq[0] = sums
        sqr[along] = sums
        for there in beside:
            pltpu.make_async_remote_copy(sq.at[0], sqr.at[along], sq_send.at[0], sq_recv.at[0], there).start()

    gather_start(0)

    @pl.when(c == 0)
    def _():
        for n in range(2):
            near_copy(n, (k.at[pl.ds(0, HD)], v)[n]).start()

    @pl.when(live[0])
    def _():
        gather_finish(0)
        grads(0)
        reduce_start(0, lambda: None)
        y_buf[...] = apply_queries()

    @pl.when(jnp.logical_not(live[0]))
    def _():
        relay_only(0)
        pl.semaphore_wait(go, 1)
        far_copy(0).start()

    pass_on(0)
    middle = reduce_finish(0)
    state[...] = middle
    own[1] = middle.astype(BF16)
    gather_start(1)

    near_copy(0, kv_far.at[0]).wait()
    scale = 1.0 / math.sqrt(HD)
    j = lax.broadcasted_iota(jnp.int32, (toks, toks), 0)
    i = lax.broadcasted_iota(jnp.int32, (toks, toks), 1)
    reach = back[...]
    scores = []
    for ahead, keys in ((2 * toks, kv_far.at[0]), (toks, kv_near.at[0]), (0, k.at[pl.ds(0, HD)])):
        away = i - j + ahead
        seen = (away >= 0) & (away <= reach) & (start + j - ahead >= 0)
        scores.append(jnp.where(seen, tn(keys[...], q[...]) * scale, -jnp.inf))
    top = functools.reduce(jnp.maximum, [jnp.max(s, axis=0, keepdims=True) for s in scores])
    weights = [jnp.exp(s - top) for s in scores]
    total = functools.reduce(jnp.add, [jnp.sum(w, axis=0, keepdims=True) for w in weights])
    for n, w in enumerate(weights):
        probs[n] = (w / total).astype(BF16)

    @pl.when(jnp.logical_not(live[1]))
    def _():
        relay_only(1)
        pl.semaphore_wait(go, 1)
        far_copy(1).start()

    @pl.when(live[1])
    def _():
        gather_finish(1)
        grads(1)

        def outputs():
            y_buf[...] = jnp.where(first, y_buf[...], apply_queries())
            exchange_squares()

        reduce_start(1, outputs)

    @pl.when(jnp.logical_not(live[1]))
    def _():
        exchange_squares()

    three = sqr.at[pl.ds(0, NX - 1)]
    pltpu.make_async_copy(three, three, sq_recv.at[0]).wait()
    sq[1] = jnp.sum(sqr[...], axis=0)
    squares = pltpu.make_async_remote_copy(sq.at[1], sq.at[2], sq_send.at[1], sq_recv.at[1], opposite)
    squares.start()
    pass_on(1)
    near_copy(1, v).wait()
    attn = nn(kv_far[1], probs[0]) + nn(kv_near[1], probs[1]) + nn(v[...], probs[2])
    squares.wait()
    mean_square = (sq[1] + sq[2]) / (HEADS * HD)
    gains = jnp.broadcast_to(gain[...].reshape(1, HD), (8, HD)).T[:, 0:1]
    normed = y_buf[...] / jnp.sqrt(mean_square + 1e-06) * gains
    out[...] = (normed + attn).astype(BF16)
    last = unpack(reduce_finish(1))
    for m, ref in enumerate((g_out, u_out, d_out)):
        ref[...] = last[m * OWN : (m + 1) * OWN].reshape(OWN, 1, HD)
    pltpu.make_async_copy(three, three, sq_send.at[0]).wait()
    for g in range(2):
        gather_drain(g)
        reduce_drain(g)


def write_out(*refs):
    half = len(refs) // 2
    srcs, dsts, sem = refs[:half], refs[half:-1], refs[-1]
    copies = [pltpu.make_async_copy(src, dst, sem.at[n]) for n, (src, dst) in enumerate(zip(srcs, dsts))]
    for copy in copies:
        copy.start()
    for copy in copies:
        copy.wait()


def on_device(queries, keys, values, rates, back, group_end, gate_init, up_init, down_init, gain):
    toks = rates.shape[0]
    perm = order_matrices()
    vmem = pl.BlockSpec(memory_space=pltpu.VMEM)
    hbm = pl.BlockSpec(memory_space=pltpu.HBM)
    slots = (CHIPS, LINES, 128)
    dma = pltpu.SemaphoreType.DMA
    shares = [w.transpose(2, 0, 1) for w in (gate_init, up_init, down_init)]
    share = jax.ShapeDtypeStruct((OWN, 1, HD), F32)
    shapes = (jax.ShapeDtypeStruct((HD, toks), BF16), share, share, share)
    results = pl.pallas_call(
        kernel,
        out_shape=shapes,
        in_specs=[pl.BlockSpec(memory_space=pltpu.SMEM)] + [hbm] * 10,
        out_specs=(vmem,) * 4,
        scratch_shapes=[
            pltpu.VMEM((HD, toks), BF16),
            pltpu.VMEM((PAD, toks), BF16),
            pltpu.VMEM((HD, toks), BF16),
            pltpu.VMEM((1, toks), F32),
            pltpu.VMEM((1, toks), jnp.int32),
            pltpu.VMEM((SLOT, 1, HD), F32),
            pltpu.VMEM((HD,), F32),
            pltpu.VMEM((4, 128, 128), BF16),
            pltpu.VMEM((2, LINES, 128), BF16),
            pltpu.VMEM((2, NC, *slots), BF16),
            pltpu.VMEM((2, NC, *slots), BF16),
            pltpu.VMEM((2, *slots), BF16),
            pltpu.VMEM((2, *slots), BF16),
            pltpu.VMEM((2, LAST_FIRST * NY, LINES, 128), BF16),
            pltpu.VMEM((2, HD, toks), BF16),
            pltpu.VMEM((2, HD, toks), BF16),
            pltpu.VMEM((3, 1, toks), F32),
            pltpu.VMEM((NX, 1, toks), F32),
            pltpu.VMEM((3, HD, PAD), F32),
            pltpu.VMEM((FH, HD), BF16),
            pltpu.VMEM((FH, HD), BF16),
            pltpu.VMEM((HD, FH), BF16),
            pltpu.VMEM((2, HD, toks), BF16),
            pltpu.VMEM((HD, toks), F32),
            pltpu.VMEM((3, toks, toks), BF16),
            pltpu.VMEM((LINES, 128), F32),
            dma((10,)),
            dma((2,)), dma((2, NZ)),
            dma((2,)), dma((2, NZ)),
            dma((2,)), dma((2, NZ)),
            dma((2,)), dma((2,)),
            dma((4,)), dma((4,)),
            dma((2,)), dma((2,)),
            pltpu.SemaphoreType.REGULAR,
        ],
        compiler_params=pltpu.CompilerParams(
            collective_id=0, has_side_effects=True, vmem_limit_bytes=48 * 1024 * 1024
        ),
        name="layer",
    )(
        group_end,
        *(
            pltpu.with_memory_space_constraint(array, pltpu.HBM)
            for array in (
                queries.T, keys.T, values.T, rates.T, back.reshape(1, toks), *shares, gain,
                jnp.asarray(perm, BF16),
            )
        ),
    )
    out, *finals = pl.pallas_call(
        write_out,
        out_shape=shapes,
        in_specs=[vmem] * 4,
        out_specs=(hbm,) * 4,
        scratch_shapes=[dma((4,))],
        compiler_params=pltpu.CompilerParams(vmem_limit_bytes=1024 * 1024),
        name="write_out",
    )(*results)
    return (out.T, *(w.transpose(1, 2, 0) for w in finals))


def solution(mesh):
    placed = (
        P("tok", "head"),
        P("tok", "head"),
        P("tok", "head"),
        P("tok", "head"),
        P("tok"),
        P(),
        P("head", None, "tok"),
        P("head", None, "tok"),
        P("head", None, "tok"),
        P("head"),
    )
    return jax.shard_map(
        on_device,
        mesh=mesh,
        in_specs=placed,
        out_specs=(
            P("tok", "head"),
            P("head", None, "tok"),
            P("head", None, "tok"),
            P("head", None, "tok"),
        ),
        check_vma=False,
    )
```

```python
import functools
import math

import jax
import jax.numpy as jnp
import numpy as np
from jax import lax
from jax.experimental import pallas as pl
from jax.experimental.pallas import tpu as pltpu
from jax.sharding import PartitionSpec as P

HEADS = 8
HD = 320
FH = 320
WINDOW = 512
NZ, NY, NC = 8, 4, 2
CHIPS = NZ * NY
NX = 4
OWN = 5
SLOT = 16
LINES = 40
PAD = 384
ZROWS = NY * NC * OWN
LAST_FIRST = 12288 * NZ // 16384
FIRST_SECOND = 4096 * NZ // 16384
FAR_FIRST = (4, 3, 5, 2, 6, 1, 7, 0)
NEAR_FIRST = (6, 2, 0, 1, 7, 5, 3, 4)
F32, BF16 = jnp.float32, jnp.bfloat16


def nn(a, b):
    return lax.dot_general(a, b, (((1,), (0,)), ((), ())), preferred_element_type=F32)


def nt(a, b):
    return lax.dot_general(a, b, (((1,), (1,)), ((), ())), preferred_element_type=F32)


def tn(a, b):
    return lax.dot_general(a, b, (((0,), (0,)), ((), ())), preferred_element_type=F32)


def order_matrices():
    perm = np.zeros((2, 128, 128), np.float32)
    for m in range(3):
        for y in range(NY):
            for c in range(NC):
                for j in range(OWN):
                    row = m * OWN + j
                    natural = m * ZROWS + (y * NC + c) * OWN + j
                    perm[0, natural, c * 64 + y * SLOT + row] = 1.0
                    perm[1, natural, row // 8 * 64 + c * 32 + y * 8 + row % 8] = 1.0
    return np.concatenate([perm, perm.transpose(0, 2, 1)])


def pack(rows):
    last = rows[:, 256:384]
    return jnp.concatenate([rows[:, 0:128], rows[:, 128:256], last[0:8] + pltpu.roll(last[8:16], 64, 1)], axis=0)


def unpack(packed):
    last = jnp.concatenate([packed[32:40], pltpu.roll(packed[32:40], 64, 1)], axis=0)
    return jnp.concatenate([packed[0:16], packed[16:32], last[:, 0:64]], axis=1)


def row_sums(packed):
    left = lax.broadcasted_iota(jnp.int32, (8, 128), 1) < 64
    last = packed[32:40]
    ends = [jnp.where(left, last, 0.0), jnp.where(left, 0.0, last)]
    whole = packed[0:16] + packed[16:32] + jnp.concatenate(ends, axis=0)
    return jnp.sum(whole, axis=1, keepdims=True)


def spread(factor):
    wide = jnp.broadcast_to(factor, (SLOT, 128))
    left = lax.broadcasted_iota(jnp.int32, (8, 128), 1) < 64
    return jnp.concatenate([wide, wide, jnp.where(left, wide[0:8], wide[8:16])], axis=0)


def kernel(
    ge, q_hbm, k_hbm, v_hbm, rates_hbm, back_hbm, g_hbm, u_hbm, d_hbm, gain_hbm, perm_hbm,
    out, g_out, u_out, d_out,
    q, k, v, rates, back, rows0, gain, perm,
    own, ag, gs, cr, red, rr, kv_far, kv_near, sq, sqr, nat, gt, ut, dt, es, y_buf, probs, state,
    in_sem, ag_send, ag_recv, fw_send, fw_recv, cs_send, cs_recv, rs_send, rs_recv, kv_send, kv_recv, sq_send, sq_recv, go,
):
    toks = q.shape[1]
    t = lax.axis_index("tok")
    h = lax.axis_index("head")
    c = lax.rem(t, 2)
    chip = lax.div(t, 2)
    zme = lax.div(chip, NY)
    yme = lax.rem(chip, NY)
    mate = t + 1 - 2 * c

    loads = [
        pltpu.make_async_copy(src, dst, in_sem.at[n])
        for n, (src, dst) in enumerate(
            (
                (g_hbm, rows0.at[pl.ds(0, OWN)]),
                (u_hbm, rows0.at[pl.ds(OWN, OWN)]),
                (d_hbm, rows0.at[pl.ds(2 * OWN, OWN)]),
                (k_hbm, k.at[pl.ds(0, HD)]),
                (v_hbm, v),
                (q_hbm, q),
                (rates_hbm, rates),
                (back_hbm, back),
                (gain_hbm, gain),
                (perm_hbm, perm),
            )
        )
    ]
    def at_chip(p):
        return {"tok": 2 * p + c}

    barrier = pltpu.get_barrier_semaphore()

    for dz in (2, 6, 1, 7, 0):
        zz = lax.rem(zme + dz, NZ)
        for dy in range(NY):
            if dz or dy:
                pl.semaphore_signal(barrier, inc=1, device_id=at_chip(zz * NY + lax.rem(yme + dy, NY)))
    across, along = lax.div(h, NX), lax.rem(h, NX)
    opposite = {"head": (1 - across) * NX + along}
    pl.semaphore_signal(barrier, inc=1, device_id=opposite)
    beside = [{"head": across * NX + lax.rem(along + n, NX)} for n in range(1, NX)]
    for there in beside:
        pl.semaphore_signal(barrier, inc=1, device_id=there)
    pl.semaphore_signal(barrier, inc=1, device_id={"tok": mate})
    for load in loads:
        load.start()

    rows0[pl.ds(3 * OWN, 1)] = jnp.zeros((1, 1, HD), F32)
    for load in loads:
        load.wait()
    share = rows0[...].reshape(SLOT, HD)
    state[...] = pack(jnp.concatenate([share, jnp.zeros((SLOT, PAD - HD), F32)], axis=1))
    own[0] = state[...].astype(BF16)
    k[pl.ds(HD, PAD - HD)] = jnp.zeros((PAD - HD, toks), BF16)
    start = t * toks
    first = start + lax.broadcasted_iota(jnp.int32, (1, toks), 1) < ge[0]
    rate = rates[...]
    vf = v[...].astype(F32)
    es[0] = (-jnp.where(first, rate, 0.0) * vf).astype(BF16)
    es[1] = (-jnp.where(first, 0.0, rate) * vf).astype(BF16)
    y_buf[...] = jnp.zeros_like(y_buf)

    pl.semaphore_wait(barrier, (5 * NY - 1) + 1 + (NX - 1) + 1)

    def active(g, z):
        return z < LAST_FIRST if g == 0 else z >= FIRST_SECOND

    live = [active(g, zme) for g in range(2)]
    z_from = (0, FIRST_SECOND)

    def peers(dzs, body):
        for dz in dzs:
            zz = lax.rem(zme + dz, NZ)
            for dy in range(NY):
                yy = lax.rem(yme + dy, NY)
                body(zz, yy, dz == 0 and dy == 0)

    def gather_start(g):
        mine = ag.at[g, c, chip]

        def send(zz, yy, is_me):
            if is_me:
                pltpu.make_async_copy(own.at[g], mine, ag_recv.at[g, zme]).start()
            else:
                pltpu.make_async_remote_copy(
                    own.at[g], mine, ag_send.at[g], ag_recv.at[g, zme], at_chip(zz * NY + yy)
                ).start()

        peers((2, 6), send)
        for dz in (1, 7, 0):

            @pl.when(active(g, lax.rem(zme + dz, NZ)))
            def _():
                peers((dz,), send)

    def arrived(g, zz):
        four = ag.at[g, c, pl.ds(zz * NY, NY)]
        pltpu.make_async_copy(four, four, ag_recv.at[g, zz]).wait()

    def relay(g, dz):
        zz = lax.rem(zme + dz, NZ)
        half = 0 if dz == 6 else NY // 2
        for more, begin, size in ((1, 0, NY), (2, half, NY // 2)):
            to = lax.rem(zme + (more if dz == 6 else NZ - more), NZ)

            @pl.when(active(g, to))
            def _():
                some = ag.at[g, c, pl.ds(zz * NY + begin, size)]
                pltpu.make_async_remote_copy(
                    some, some, ag_send.at[g], ag_recv.at[g, zz], at_chip(to * NY + yme)
                ).start()

    def relay_only(g):
        for dz in (2, 6):
            arrived(g, lax.rem(zme + dz, NZ))
            relay(g, dz)

    def block_at(zz):
        return pl.ds(pl.multiple_of(zz * ZROWS, 8), ZROWS)

    def start_far(g):
        far_copy(g).start()
        tell, away = ((2, 3), 4) if g == 0 else ((4, 5), -4)

        @pl.when((zme == tell[0]) | (zme == tell[1]))
        def _():
            pl.semaphore_signal(go, inc=1, device_id={"tok": t + away * NY * NC})

    def gather_finish(g):
        def forwarded(zz):
            four = ag.at[g, 1 - c, pl.ds(zz * NY, NY)]
            pltpu.make_async_copy(four, four, fw_recv.at[g, zz]).wait()

        def arrange(zz):
            both = [ag[g, core, pl.ds(zz * NY, NY)] for core in range(NC)]
            wide = [
                jnp.concatenate([x[:, r : r + SLOT].reshape(NY * SLOT, 128) for x in both], axis=0) for r in (0, SLOT)
            ]
            ordered = nn(perm[0], jnp.concatenate(wide, axis=1))
            ends = jnp.concatenate([x[:, 2 * SLOT :].reshape(NY * 8, 128) for x in both], axis=0).astype(F32)
            left = lax.broadcasted_iota(jnp.int32, ends.shape, 1) < 64
            halves = [jnp.where(left, x, 0.0) for x in (ends, pltpu.roll(ends, 64, 1))]
            ordered_ends = nn(perm[1], jnp.concatenate(halves, axis=0).astype(BF16))
            for m in range(3):
                rows = slice(m * ZROWS, (m + 1) * ZROWS)
                nat[m, block_at(zz), 0:256] = ordered[rows]
                nat[m, block_at(zz), 256:PAD] = ordered_ends[rows]

        order = [lax.rem(zme + dz, NZ) for dz in NEAR_FIRST]
        for n, zz in enumerate(order):
            if n == NZ - 1:
                start_far(g)
            four = ag.at[g, c, pl.ds(zz * NY, NY)]
            arrived(g, zz)
            if NEAR_FIRST[n] in (2, 6):
                relay(g, NEAR_FIRST[n])
            pltpu.make_async_remote_copy(four, four, fw_send.at[g], fw_recv.at[g, zz], {"tok": mate}).start()
            if n >= 6:
                for zz in order[2 * n - 12 : 2 * n - 10]:
                    forwarded(zz)
                for zz in order[2 * n - 12 : 2 * n - 10]:
                    arrange(zz)
        for pair in (order[4:6], order[6:7], order[7:8]):
            for zz in pair:
                forwarded(zz)
            for zz in pair:
                arrange(zz)
        for m, ref in enumerate((gt, ut, dt)):
            ref[...] = nat[m, :, 0:HD].astype(BF16)

    def gather_drain(g):
        taking = [z < LAST_FIRST if g == 0 else z >= FIRST_SECOND for z in range(NZ)]
        weights = ((1, 2 * NY), (7, 2 * NY), (0, NY - 1), (2, NY // 2), (6, NY // 2))
        sent = [2 * NY + sum(n for dz, n in weights if taking[(z + dz) % NZ]) for z in range(NZ)]
        for n in sorted(set(sent)):
            same = functools.reduce(jnp.logical_or, [zme == z for z in range(NZ) if sent[z] == n])

            @pl.when(same)
            def _():
                some = ag.at[g, 0, pl.ds(0, n)]
                pltpu.make_async_copy(some, some, ag_send.at[g]).wait()

        @pl.when(live[g])
        def _():
            every = ag.at[g, 0]
            pltpu.make_async_copy(every, every, fw_send.at[g]).wait()

    def grads(g):
        kk, e = k[pl.ds(0, HD)], es[g]
        a = nn(gt[...], kk)
        b = nn(ut[...], kk)
        s = jax.nn.sigmoid(a)
        act = a * s
        r = (act * b).astype(BF16)
        du = tn(dt[...], e)
        da = (du * b * s * (1.0 + a * (1.0 - s))).astype(BF16)
        db = (du * act).astype(BF16)
        nat[0] = nt(da, k[...])
        nat[1] = nt(db, k[...])
        nat[2] = nt(e, jnp.concatenate([r, jnp.zeros((PAD - FH, toks), BF16)], axis=0))

    def reduce_start(g, meanwhile):
        def split(zz):
            part = [nat[m, block_at(zz)] for m in range(3)]
            part.append(jnp.zeros((128 - 3 * ZROWS, PAD), F32))
            block = jnp.concatenate(part, axis=0).astype(BF16)
            slots = nn(perm[2], block[:, 0:256]).astype(BF16)
            ends = nn(perm[3], block[:, 256:PAD])
            ends = (ends[0:64] + pltpu.roll(ends[64:128], 64, 1)).astype(BF16)
            here = pl.ds(zz * NY, NY)
            gs[g, :, here, 0:SLOT] = slots[:, 0:128].reshape(NC, NY, SLOT, 128)
            gs[g, :, here, SLOT : 2 * SLOT] = slots[:, 128:256].reshape(NC, NY, SLOT, 128)
            gs[g, :, here, 2 * SLOT : LINES] = ends.reshape(NC, NY, 8, 128)

        def to_mate(zz):
            here = pl.ds(zz * NY, NY)
            pltpu.make_async_remote_copy(
                gs.at[g, 1 - c, here], cr.at[g, here], cs_send.at[g], cs_recv.at[g, zz], {"tok": mate}
            ).start()

        landing = rr.at[g, chip - z_from[g] * NY]

        def send(zz, yy, is_me):
            p = zz * NY + yy
            if is_me:
                pltpu.make_async_copy(red.at[g, p], landing, rs_recv.at[g]).start()
            else:
                pltpu.make_async_remote_copy(
                    red.at[g, p], landing, rs_send.at[g], rs_recv.at[g], at_chip(p)
                ).start()

        def pass_sum(dz):
            zz = lax.rem(zme + dz, NZ)
            here = pl.ds(zz * NY, NY)
            four = cr.at[g, here]
            pltpu.make_async_copy(four, four, cs_recv.at[g, zz]).wait()
            red[g, here] = (gs[g, c, here].astype(F32) + cr[g, here].astype(F32)).astype(BF16)
            peers((dz,), send)

        for batch in (FAR_FIRST[:2], FAR_FIRST[2:4], FAR_FIRST[4:]):
            for dz in batch:
                split(lax.rem(zme + dz, NZ))
            for dz in batch:
                to_mate(lax.rem(zme + dz, NZ))
        meanwhile()
        for dz in FAR_FIRST:
            pass_sum(dz)

    def reduce_finish(g):
        every = rr.at[g]
        pltpu.make_async_copy(every, every, rs_recv.at[g]).wait()
        total = jnp.sum(rr[g].astype(F32), axis=0)
        old = state[...]
        fresh = old - total
        old_norm = jnp.sqrt(row_sums(old * old))
        new_norm = jnp.sqrt(row_sums(fresh * fresh) + 1e-06)
        return fresh * spread(old_norm / new_norm)

    def reduce_drain(g):
        @pl.when(live[g])
        def _():
            every = cr.at[g]
            pltpu.make_async_copy(every, every, cs_send.at[g]).wait()
            thirty_one = red.at[g, pl.ds(0, CHIPS - 1)]
            pltpu.make_async_copy(thirty_one, thirty_one, rs_send.at[g]).wait()

    def apply_queries():
        a = nn(gt[...], q[...])
        b = nn(ut[...], q[...])
        hidden = (a * jax.nn.sigmoid(a) * b).astype(BF16)
        return nn(dt[...], hidden)

    def far_copy(n):
        return pltpu.make_async_remote_copy(
            (k.at[pl.ds(0, HD)], v)[n], kv_far.at[n], kv_send.at[n], kv_recv.at[n], at_chip(lax.rem(chip + 1, CHIPS))
        )

    def near_copy(n, src):
        return pltpu.make_async_remote_copy(src, kv_near.at[n], kv_send.at[2 + n], kv_recv.at[2 + n], {"tok": mate})

    def pass_on(n):
        far_copy(n).wait()

        @pl.when(c == 1)
        def _():
            near_copy(n, kv_far.at[n]).start()

    def exchange_squares():
        mixed = y_buf[...]
        sums = jnp.sum(mixed * mixed, axis=0, keepdims=True)
        sq[0] = sums
        sqr[along] = sums
        for there in beside:
            pltpu.make_async_remote_copy(sq.at[0], sqr.at[along], sq_send.at[0], sq_recv.at[0], there).start()

    gather_start(0)

    @pl.when(c == 0)
    def _():
        for n in range(2):
            near_copy(n, (k.at[pl.ds(0, HD)], v)[n]).start()

    @pl.when(live[0])
    def _():
        gather_finish(0)
        grads(0)
        reduce_start(0, lambda: None)
        y_buf[...] = apply_queries()

    @pl.when(jnp.logical_not(live[0]))
    def _():
        relay_only(0)
        pl.semaphore_wait(go, 1)
        far_copy(0).start()

    pass_on(0)
    middle = reduce_finish(0)
    state[...] = middle
    own[1] = middle.astype(BF16)
    gather_start(1)

    near_copy(0, kv_far.at[0]).wait()
    scale = 1.0 / math.sqrt(HD)
    j = lax.broadcasted_iota(jnp.int32, (toks, toks), 0)
    i = lax.broadcasted_iota(jnp.int32, (toks, toks), 1)
    reach = back[...]
    scores = []
    for ahead, keys in ((2 * toks, kv_far.at[0]), (toks, kv_near.at[0]), (0, k.at[pl.ds(0, HD)])):
        away = i - j + ahead
        seen = (away >= 0) & (away <= reach) & (start + j - ahead >= 0)
        scores.append(jnp.where(seen, tn(keys[...], q[...]) * scale, -jnp.inf))
    top = functools.reduce(jnp.maximum, [jnp.max(s, axis=0, keepdims=True) for s in scores])
    weights = [jnp.exp(s - top) for s in scores]
    total = functools.reduce(jnp.add, [jnp.sum(w, axis=0, keepdims=True) for w in weights])
    for n, w in enumerate(weights):
        probs[n] = (w / total).astype(BF16)

    @pl.when(jnp.logical_not(live[1]))
    def _():
        relay_only(1)
        pl.semaphore_wait(go, 1)
        far_copy(1).start()

    @pl.when(live[1])
    def _():
        gather_finish(1)
        grads(1)

        def outputs():
            y_buf[...] = jnp.where(first, y_buf[...], apply_queries())
            exchange_squares()

        reduce_start(1, outputs)

    @pl.when(jnp.logical_not(live[1]))
    def _():
        exchange_squares()

    three = sqr.at[pl.ds(0, NX - 1)]
    pltpu.make_async_copy(three, three, sq_recv.at[0]).wait()
    sq[1] = jnp.sum(sqr[...], axis=0)
    squares = pltpu.make_async_remote_copy(sq.at[1], sq.at[2], sq_send.at[1], sq_recv.at[1], opposite)
    squares.start()
    pass_on(1)
    near_copy(1, v).wait()
    attn = nn(kv_far[1], probs[0]) + nn(kv_near[1], probs[1]) + nn(v[...], probs[2])
    squares.wait()
    mean_square = (sq[1] + sq[2]) / (HEADS * HD)
    gains = jnp.broadcast_to(gain[...].reshape(1, HD), (8, HD)).T[:, 0:1]
    normed = y_buf[...] / jnp.sqrt(mean_square + 1e-06) * gains
    out[...] = (normed + attn).astype(BF16)
    last = unpack(reduce_finish(1))
    for m, ref in enumerate((g_out, u_out, d_out)):
        ref[...] = last[m * OWN : (m + 1) * OWN].reshape(OWN, 1, HD)
    pltpu.make_async_copy(three, three, sq_send.at[0]).wait()
    for g in range(2):
        gather_drain(g)
        reduce_drain(g)


def write_out(*refs):
    half = len(refs) // 2
    srcs, dsts, sem = refs[:half], refs[half:-1], refs[-1]
    copies = [pltpu.make_async_copy(src, dst, sem.at[n]) for n, (src, dst) in enumerate(zip(srcs, dsts))]
    for copy in copies:
        copy.start()
    for copy in copies:
        copy.wait()


def on_device(queries, keys, values, rates, back, group_end, gate_init, up_init, down_init, gain):
    toks = rates.shape[0]
    perm = order_matrices()
    vmem = pl.BlockSpec(memory_space=pltpu.VMEM)
    hbm = pl.BlockSpec(memory_space=pltpu.HBM)
    slots = (CHIPS, LINES, 128)
    dma = pltpu.SemaphoreType.DMA
    shares = [w.transpose(2, 0, 1) for w in (gate_init, up_init, down_init)]
    share = jax.ShapeDtypeStruct((OWN, 1, HD), F32)
    shapes = (jax.ShapeDtypeStruct((HD, toks), BF16), share, share, share)
    results = pl.pallas_call(
        kernel,
        out_shape=shapes,
        in_specs=[pl.BlockSpec(memory_space=pltpu.SMEM)] + [hbm] * 10,
        out_specs=(vmem,) * 4,
        scratch_shapes=[
            pltpu.VMEM((HD, toks), BF16),
            pltpu.VMEM((PAD, toks), BF16),
            pltpu.VMEM((HD, toks), BF16),
            pltpu.VMEM((1, toks), F32),
            pltpu.VMEM((1, toks), jnp.int32),
            pltpu.VMEM((SLOT, 1, HD), F32),
            pltpu.VMEM((HD,), F32),
            pltpu.VMEM((4, 128, 128), BF16),
            pltpu.VMEM((2, LINES, 128), BF16),
            pltpu.VMEM((2, NC, *slots), BF16),
            pltpu.VMEM((2, NC, *slots), BF16),
            pltpu.VMEM((2, *slots), BF16),
            pltpu.VMEM((2, *slots), BF16),
            pltpu.VMEM((2, LAST_FIRST * NY, LINES, 128), BF16),
            pltpu.VMEM((2, HD, toks), BF16),
            pltpu.VMEM((2, HD, toks), BF16),
            pltpu.VMEM((3, 1, toks), F32),
            pltpu.VMEM((NX, 1, toks), F32),
            pltpu.VMEM((3, HD, PAD), F32),
            pltpu.VMEM((FH, HD), BF16),
            pltpu.VMEM((FH, HD), BF16),
            pltpu.VMEM((HD, FH), BF16),
            pltpu.VMEM((2, HD, toks), BF16),
            pltpu.VMEM((HD, toks), F32),
            pltpu.VMEM((3, toks, toks), BF16),
            pltpu.VMEM((LINES, 128), F32),
            dma((10,)),
            dma((2,)), dma((2, NZ)),
            dma((2,)), dma((2, NZ)),
            dma((2,)), dma((2, NZ)),
            dma((2,)), dma((2,)),
            dma((4,)), dma((4,)),
            dma((2,)), dma((2,)),
            pltpu.SemaphoreType.REGULAR,
        ],
        compiler_params=pltpu.CompilerParams(
            collective_id=0, has_side_effects=True, vmem_limit_bytes=48 * 1024 * 1024
        ),
        name="layer",
    )(
        group_end,
        *(
            pltpu.with_memory_space_constraint(array, pltpu.HBM)
            for array in (
                queries.T, keys.T, values.T, rates.T, back.reshape(1, toks), *shares, gain,
                jnp.asarray(perm, BF16),
            )
        ),
    )
    out, *finals = pl.pallas_call(
        write_out,
        out_shape=shapes,
        in_specs=[vmem] * 4,
        out_specs=(hbm,) * 4,
        scratch_shapes=[dma((4,))],
        compiler_params=pltpu.CompilerParams(vmem_limit_bytes=1024 * 1024),
        name="write_out",
    )(*results)
    return (out.T, *(w.transpose(1, 2, 0) for w in finals))


def solution(mesh):
    placed = (
        P("tok", "head"),
        P("tok", "head"),
        P("tok", "head"),
        P("tok", "head"),
        P("tok"),
        P(),
        P("head", None, "tok"),
        P("head", None, "tok"),
        P("head", None, "tok"),
        P("head"),
    )
    return jax.shard_map(
        on_device,
        mesh=mesh,
        in_specs=placed,
        out_specs=(
            P("tok", "head"),
            P("head", None, "tok"),
            P("head", None, "tok"),
            P("head", None, "tok"),
        ),
        check_vma=False,
    )
```
